256 devices in a mesh: grp: 32 (over x_lo, z, core), tp: 8 (over y, x_hi).
Axes of the slice: x: 4 (x_hi: 2, x_lo: 2; x = x_hi * 2 + x_lo), y: 4, z: 8, core: 2. Of those that a mesh axis runs over, the one named last changes fastest.
Arguments:
- tokens: bfloat16 [32, 1024, 2048], P(None, 'grp'), may hold values from -6 to 6
- w_query: bfloat16 [2048, 2048], P(None, 'tp'), may hold values from -0.375 to 0.375
- w_key: bfloat16 [2048, 2048], P(None, 'tp'), may hold values from -0.125 to 0.125
- w_value: bfloat16 [2048, 2048], P(None, 'tp'), may hold values from -0.125 to 0.125
- w_out: bfloat16 [2048, 2048], P('tp'), may hold values from -0.125 to 0.125
- own_cache: bfloat16 [32, 2, 2048, 2048], P('grp', None, None, 'tp'), may hold values from -330 to 330
- guest_cache: bfloat16 [32, 2, 2048, 2048], P('grp', None, None, 'tp'), may hold values from -6 to 6
- rec_hidden: bfloat16 [32, 256, 2048], P('grp'), may hold values from -6 to 6
- deal_order: int32 [32], replicated, may hold values from 0 to 31, each once
- own_len: int32 [32], replicated, may hold values from 256 to 2048, as said below
- guest_len: int32 [32], replicated, may hold values from 0 to 2048, as said below
- rec_index: int32 [32, 256], P('grp'), may hold values from 0 to 2047, as said below
Outputs:
- attn_out: bfloat16 [32, 1024, 2048], P(None, 'grp', 'tp')
The draws below stay inside these ranges and needn't reach their ends.
Inputs may be any that keep to these rules, and one draw needn't show every extreme that they name: Rows 0 to own_len[g] - 1 of group g's own slot hold cached positions 0 to own_len[g] - 1 of the request served at group g; a request whose cache continues in a guest region fills its own slot. The guest_len[g] used rows of group g's guest region continue the cache of the request served at group (g + 16) mod 32. rec_index[g] holds 256 distinct rows of group g's own slot, each below own_len[g].
All inputs are finite; a program needn't handle non-finite values.
Results may differ from the reference program's by a relative error of at most 0.02.
The reference program's roundings to bfloat16 on the way count: a program that leaves them out, or rounds other values in their place, can miss the bound.
Values may be sent and summed in bfloat16 or wider, within the bound.
A program may use at most 128 MiB of HBM per device.

```python
import jax
import jax.numpy as jnp
from jax import lax

D = 2048
HEADS = 16
HEAD_DIM = 128
SPAN = 1024
CAP = 2048
GCAP = 2048
RECOMP = 256
N_GRP = 32
N_TP = 8


def cache_layout(key):
    base_key = jax.random.fold_in(key, 7)
    key_short, key_flag, key_pair, key_side, key_extra, key_other = jax.random.split(base_key, 6)
    half_count = N_GRP // 2
    pair_ids = jnp.arange(half_count, dtype=jnp.int32)
    short_rows = jax.random.randint(key_short, (N_GRP,), CAP // 8, CAP + 1)
    forced_pair = jax.random.randint(key_pair, (), 0, half_count)
    long_flag = jnp.where(pair_ids == forced_pair, 1, jax.random.randint(key_flag, (half_count,), 0, 2))
    side_flag = jax.random.randint(key_side, (half_count,), 0, 2)
    both_long = jnp.where(pair_ids == 0, 1, 0)
    extra_rows = jnp.where((pair_ids == forced_pair) | (pair_ids == 0), GCAP, jax.random.randint(key_extra, (half_count,), 1, GCAP + 1))
    other_rows = jnp.where(pair_ids == 0, GCAP, jax.random.randint(key_other, (half_count,), 1, GCAP + 1))
    lower_long = jnp.maximum(long_flag * (1 - side_flag), both_long)
    upper_long = jnp.maximum(long_flag * side_flag, both_long)
    is_long = jnp.concatenate([lower_long, upper_long])
    own_rows = jnp.where(is_long == 1, CAP, short_rows).astype(jnp.int32)
    guest_rows = jnp.concatenate([upper_long * extra_rows, lower_long * other_rows]).astype(jnp.int32)
    return (own_rows, guest_rows)


def draw_own_len(key, part):
    return cache_layout(key)[0]


def draw_guest_len(key, part):
    return cache_layout(key)[1]


def draw_rec_index(key, part):
    own_rows = cache_layout(key)[0]
    ranking = jax.random.randint(jax.random.fold_in(key, 11), (N_GRP, CAP), 0, 4096)
    position = jnp.arange(CAP, dtype=jnp.int32)[None, :]
    keyed = jnp.where(position < own_rows[:, None], ranking * CAP + position, 4096 * CAP + position)
    ordering = jnp.argsort(keyed, axis=1)
    return ordering[:, :CAP // 8].astype(jnp.int32)


def draw_own_cache(key, part):
    key_base = jax.random.fold_in(jax.random.fold_in(key, 3), 0)
    full_width = HEADS * HEAD_DIM
    shape = (N_GRP, 2, CAP, full_width)
    drawn = jnp.clip(jax.random.normal(key_base, shape, jnp.float32), -6.0, 6.0)
    return drawn.astype(jnp.bfloat16)


def shard_levels(key, dims, shards, low, high):
    loudness = 1.0
    for axis_at, parts in shards:
        heights = jax.random.uniform(jax.random.fold_in(jax.random.fold_in(key, 6), axis_at), (parts,), jnp.float32, low / len(shards), high / len(shards))
        loudness = loudness * jnp.repeat(jnp.exp(heights), dims[axis_at] // parts).reshape((-1,) + (1,) * (len(dims) - 1 - axis_at))
    return loudness


def noise(stream_key, extent, spread, bound, cuts=(), kind=jnp.bfloat16):
    result = spread * jax.random.normal(stream_key, extent, jnp.float32)
    if cuts:
        result = result * shard_levels(stream_key, extent, cuts, -0.22, 0.18)
    return jnp.clip(result, -bound, bound).astype(kind)


def setup_inputs(seed: int = 0) -> dict:
    keys = jax.random.split(jax.random.key(seed), 13)
    return {
        "tokens": noise(keys[0], (N_GRP, SPAN, D), 1.0, 6.0, ((1, 32),)),
        "w_query": noise(keys[1], (D, HEADS * HEAD_DIM), (D // 9) ** -0.5, 0.375, ((1, 8),)),
        "w_key": noise(keys[2], (D, HEADS * HEAD_DIM), D ** -0.5, 0.125, ((1, 8),)),
        "w_value": noise(keys[3], (D, HEADS * HEAD_DIM), D ** -0.5, 0.125, ((1, 8),)),
        "w_out": noise(keys[4], (HEADS * HEAD_DIM, D), (HEADS * HEAD_DIM) ** -0.5, 0.125, ((0, 8),)),
        "own_cache": draw_own_cache(jax.random.fold_in(keys[12], 71), 0),
        "guest_cache": noise(keys[6], (N_GRP, 2, GCAP, HEADS * HEAD_DIM), 1.0, 6.0, ((0, 32), (3, 8))),
        "rec_hidden": noise(keys[7], (N_GRP, RECOMP, D), 1.0, 6.0, ((0, 32),)),
        "deal_order": jax.random.permutation(keys[8], N_GRP).astype(jnp.int32),
        "own_len": draw_own_len(jax.random.fold_in(keys[12], 71), 0),
        "guest_len": draw_guest_len(jax.random.fold_in(keys[12], 71), 0),
        "rec_index": draw_rec_index(jax.random.fold_in(keys[12], 71), 0),
    }


rope_base = 10000.0
norm_eps = 1e-05

def layer_norm(token_rows):
    widened = token_rows.astype(jnp.float32)
    centred = widened - lax.optimization_barrier(jnp.mean(widened, axis=-1, keepdims=True))
    variance = lax.optimization_barrier(jnp.mean(centred * centred, axis=-1, keepdims=True))
    return centred * lax.rsqrt(variance + norm_eps)

def rotate(projected, positions, head_dim):
    half_dim = head_dim // 2
    frequency = jnp.exp(-jnp.log(rope_base) * jnp.arange(half_dim, dtype=jnp.float32) / half_dim)
    angles = positions.astype(jnp.float32)[:, None] * frequency[None, :]
    cosine = jnp.cos(angles)[:, None, :]
    sine_part = jnp.sin(angles)[:, None, :]
    shaped = projected.reshape(projected.shape[0], -1, head_dim)
    first_half = shaped[..., :half_dim]
    second = shaped[..., half_dim:]
    turned = jnp.concatenate([first_half * cosine - second * sine_part, second * cosine + first_half * sine_part], axis=-1)
    return turned.reshape(projected.shape)

def reference(tokens, w_query, w_key, w_value, w_out, own_cache, guest_cache, rec_hidden, deal_order, own_len, guest_len, rec_index):
    full_width = HEADS * HEAD_DIM
    block_width = full_width // N_TP
    score_scale = HEAD_DIM ** (-0.5)

    def one_group(group_id):
        partner_id = (group_id + N_GRP // 2) % N_GRP
        own_count = own_len[group_id]
        guest_count = guest_len[partner_id]
        token_rows = tokens[deal_order[group_id]]
        positions = own_count + guest_count + jnp.arange(SPAN, dtype=jnp.int32)
        normed = layer_norm(token_rows).astype(jnp.bfloat16)
        queries = rotate(jnp.dot(normed, w_query, preferred_element_type=jnp.float32), positions, HEAD_DIM).astype(jnp.bfloat16)
        new_keys = rotate(jnp.dot(normed, w_key, preferred_element_type=jnp.float32), positions, HEAD_DIM).astype(jnp.bfloat16)
        new_values = jnp.dot(normed, w_value, preferred_element_type=jnp.float32).astype(jnp.bfloat16)
        rec_rows = layer_norm(rec_hidden[group_id]).astype(jnp.bfloat16)
        rec_positions = rec_index[group_id].astype(jnp.int32)
        rec_keys = rotate(jnp.dot(rec_rows, w_key, preferred_element_type=jnp.float32), rec_positions, HEAD_DIM).astype(jnp.bfloat16)
        rec_values = jnp.dot(rec_rows, w_value, preferred_element_type=jnp.float32).astype(jnp.bfloat16)
        cached_keys = own_cache[group_id, 0].at[rec_positions].set(rec_keys)
        cached_values = own_cache[group_id, 1].at[rec_positions].set(rec_values)
        all_keys = jnp.concatenate([cached_keys, guest_cache[partner_id, 0], new_keys], axis=0)
        all_values = jnp.concatenate([cached_values, guest_cache[partner_id, 1], new_values], axis=0)
        query_place = jnp.arange(SPAN, dtype=jnp.int32)[:, None]
        is_valid = jnp.concatenate([jnp.broadcast_to(jnp.arange(CAP, dtype=jnp.int32)[None, :] < own_count, (SPAN, CAP)), jnp.broadcast_to(jnp.arange(GCAP, dtype=jnp.int32)[None, :] < guest_count, (SPAN, GCAP)), jnp.arange(SPAN, dtype=jnp.int32)[None, :] <= query_place], axis=1)
        query_heads = queries.astype(jnp.float32).reshape(SPAN, HEADS, HEAD_DIM)
        key_heads = all_keys.astype(jnp.float32).reshape(-1, HEADS, HEAD_DIM)
        value_heads = all_values.astype(jnp.float32).reshape(-1, HEADS, HEAD_DIM)
        scores = jnp.einsum('qhd,khd->hqk', query_heads, key_heads) * score_scale
        scores = jnp.where(is_valid[None], scores, -jnp.inf)
        top_score = lax.optimization_barrier(jnp.max(scores, axis=-1, keepdims=True))
        expanded = jnp.exp(scores - top_score)
        weight_sum = lax.optimization_barrier(jnp.sum(expanded, axis=-1))
        weights = lax.optimization_barrier(expanded.astype(jnp.bfloat16))
        numerator = jnp.einsum('hqk,khd->qhd', weights.astype(jnp.float32), value_heads)
        attended = (numerator / jnp.transpose(weight_sum)[:, :, None]).astype(jnp.bfloat16).reshape(SPAN, full_width)
        mixed_sum = jnp.zeros((SPAN, D), jnp.float32)
        for tp_block in range(N_TP):
            lower_edge = tp_block * block_width
            term_part = jnp.dot(attended[:, lower_edge:lower_edge + block_width], w_out[lower_edge:lower_edge + block_width], preferred_element_type=jnp.float32)
            rounded = lax.optimization_barrier(term_part.astype(jnp.bfloat16))
            mixed_sum = mixed_sum + rounded.astype(jnp.float32)
        return mixed_sum.astype(jnp.bfloat16)
    outputs = lax.map(one_group, jnp.arange(N_GRP, dtype=jnp.int32))
    return jnp.zeros_like(outputs).at[deal_order].set(outputs)
```

```python
import jax
import jax.numpy as jnp
from jax import lax
from jax.sharding import PartitionSpec as P

HEAD_DIM = 128


rope_base = 10000.0
norm_eps = 1e-05


def swapped(value, axis, apart):
    mask = 2**apart
    pairs = [(source, source ^ mask) for source in range(lax.axis_size(axis))]
    return lax.ppermute(value, axis, pairs)


def layer_norm(token_rows):
    widened = token_rows.astype(jnp.float32)
    centred = widened - jnp.mean(widened, axis=-1, keepdims=True)
    variance = jnp.mean(centred * centred, axis=-1, keepdims=True)
    return centred * lax.rsqrt(variance + norm_eps)


def rotate(projected, positions, head_dim):
    half_dim = head_dim // 2
    frequency = jnp.exp(-jnp.log(rope_base) * jnp.arange(half_dim, dtype=jnp.float32) / half_dim)
    angles = positions.astype(jnp.float32)[:, None] * frequency[None, :]
    cosine = jnp.cos(angles)[:, None, :]
    sine_part = jnp.sin(angles)[:, None, :]
    shaped = projected.reshape(projected.shape[0], -1, head_dim)
    first_half = shaped[..., :half_dim]
    second = shaped[..., half_dim:]
    turned = jnp.concatenate(
        [first_half * cosine - second * sine_part, second * cosine + first_half * sine_part],
        axis=-1,
    )
    return turned.reshape(projected.shape)


def absorb(softmax_state, queries, key_rows, value_rows, is_valid):
    running_max, weight_sum, numerator = softmax_state
    score_scale = queries.shape[-1] ** (-0.5)
    scores = (
        jnp.einsum("qhd,khd->hqk", queries, key_rows, preferred_element_type=jnp.float32)
        * score_scale
    )
    scores = jnp.where(is_valid[None], scores, -jnp.inf)
    new_max = jnp.maximum(running_max, jnp.max(scores, axis=-1))
    factor = jnp.exp(running_max - new_max)
    expanded = jnp.exp(scores - new_max[..., None])
    weight_sum = weight_sum * factor + jnp.sum(expanded, axis=-1)
    product = jnp.einsum(
        "hqk,khd->qhd",
        expanded.astype(jnp.bfloat16),
        value_rows,
        preferred_element_type=jnp.float32,
    )
    numerator = numerator * jnp.transpose(factor)[:, :, None] + product
    return (new_max, weight_sum, numerator)


def sweep_keys(softmax_state, queries, key_rows, value_rows, live_count, skip=None):
    block_len = min(512, key_rows.shape[0])
    block_count = (live_count + block_len - 1) // block_len

    def visit_block(block_index, carried):
        block_start = block_index * block_len
        key_block = lax.dynamic_slice_in_dim(key_rows, block_start, block_len, 0)
        value_block = lax.dynamic_slice_in_dim(value_rows, block_start, block_len, 0)
        is_valid = block_start + jnp.arange(block_len, dtype=jnp.int32) < live_count
        if skip is not None:
            is_valid = is_valid & ~lax.dynamic_slice_in_dim(skip, block_start, block_len, 0)
        return absorb(carried, queries, key_block, value_block, is_valid[None, :])

    return lax.fori_loop(jnp.int32(0), block_count, visit_block, softmax_state)


def shards(
    tokens,
    w_query,
    w_key,
    w_value,
    w_out,
    own_cache,
    guest_cache,
    rec_hidden,
    deal_order,
    own_len,
    guest_len,
    rec_index,
):
    groups = lax.axis_size("grp")
    group_id = lax.axis_index("grp")
    partner_id = (group_id + groups // 2) % groups
    swap_bit = groups.bit_length() - 2
    local_width = w_query.shape[1]
    local_heads = local_width // HEAD_DIM
    requests, local_rows, model_width = tokens.shape

    fetched = swapped(guest_cache[0], "grp", swap_bit)

    server = jnp.zeros_like(deal_order).at[deal_order].set(jnp.arange(groups, dtype=jnp.int32))
    start_of = own_len[server] + guest_len[(server + groups // 2) % groups]
    local_positions = (
        start_of[:, None] + group_id * local_rows + jnp.arange(local_rows, dtype=jnp.int32)[None, :]
    ).reshape(-1)

    normed = layer_norm(tokens.reshape(-1, model_width)).astype(jnp.bfloat16)
    queries = rotate(
        jnp.dot(normed, w_query, preferred_element_type=jnp.float32), local_positions, HEAD_DIM
    ).astype(jnp.bfloat16)
    new_keys = rotate(
        jnp.dot(normed, w_key, preferred_element_type=jnp.float32), local_positions, HEAD_DIM
    ).astype(jnp.bfloat16)
    new_values = jnp.dot(normed, w_value, preferred_element_type=jnp.float32).astype(jnp.bfloat16)
    projected = jnp.concatenate([queries, new_keys, new_values], axis=-1).reshape(
        requests, local_rows, 3 * local_width
    )
    arranged = jnp.take(projected, deal_order, axis=0)
    dealt = lax.all_to_all(arranged, "grp", split_axis=0, concat_axis=1, tiled=True)[0]
    span_len = dealt.shape[0]
    queries = dealt[:, :local_width]
    new_keys = dealt[:, local_width : 2 * local_width]
    new_values = dealt[:, 2 * local_width :]

    own_count = own_len[group_id]
    guest_count = guest_len[partner_id]
    rec_rows = layer_norm(rec_hidden[0]).astype(jnp.bfloat16)
    rec_positions = rec_index[0]
    rec_keys = rotate(
        jnp.dot(rec_rows, w_key, preferred_element_type=jnp.float32), rec_positions, HEAD_DIM
    ).astype(jnp.bfloat16)
    rec_values = jnp.dot(rec_rows, w_value, preferred_element_type=jnp.float32).astype(jnp.bfloat16)
    replaced = jnp.zeros((own_cache.shape[2],), jnp.bool_).at[rec_positions].set(True)

    def by_head(matrix):
        return matrix.reshape(matrix.shape[0], local_heads, HEAD_DIM)

    empty_state = (
        jnp.full((local_heads, span_len), -jnp.inf, jnp.float32),
        jnp.zeros((local_heads, span_len), jnp.float32),
        jnp.zeros((span_len, local_heads, HEAD_DIM), jnp.float32),
    )
    causal = jnp.arange(span_len)[None, :] <= jnp.arange(span_len)[:, None]
    query_heads = by_head(queries)
    softmax_state = absorb(empty_state, query_heads, by_head(new_keys), by_head(new_values), causal)
    softmax_state = absorb(
        softmax_state,
        query_heads,
        by_head(rec_keys),
        by_head(rec_values),
        jnp.ones((1, rec_keys.shape[0]), jnp.bool_),
    )
    softmax_state = sweep_keys(
        softmax_state,
        query_heads,
        by_head(own_cache[0, 0]),
        by_head(own_cache[0, 1]),
        own_count,
        replaced,
    )
    softmax_state = sweep_keys(
        softmax_state, query_heads, by_head(fetched[0]), by_head(fetched[1]), guest_count
    )
    weight_sum = softmax_state[1]
    numerator = softmax_state[2]
    attended = (
        (numerator / jnp.transpose(weight_sum)[:, :, None])
        .astype(jnp.bfloat16)
        .reshape(span_len, local_width)
    )
    partial_value = jnp.dot(attended, w_out, preferred_element_type=jnp.float32).astype(
        jnp.bfloat16
    )
    blocks = lax.axis_size("tp")
    exchanged = lax.all_to_all(
        partial_value.reshape(span_len, blocks, -1), "tp", split_axis=1, concat_axis=1, tiled=True
    )
    mixed_rows = exchanged.astype(jnp.float32).sum(axis=1).astype(jnp.bfloat16)
    returned_rows = lax.all_to_all(
        mixed_rows.reshape(groups, local_rows, -1), "grp", split_axis=0, concat_axis=0, tiled=True
    )
    return jnp.take(returned_rows, server, axis=0)


def solution(mesh):
    return jax.shard_map(
        shards,
        mesh=mesh,
        in_specs=(
            P(None, "grp", None),
            P(None, "tp"),
            P(None, "tp"),
            P(None, "tp"),
            P("tp", None),
            P("grp", None, None, "tp"),
            P("grp", None, None, "tp"),
            P("grp", None, None),
            P(),
            P(),
            P(),
            P("grp", None),
        ),
        out_specs=P(None, "grp", "tp"),
        check_vma=False,
    )
```

```python
import jax
import jax.numpy as jnp
from jax import lax
from jax.experimental import pallas as pl
from jax.experimental.pallas import tpu as pltpu
from jax.sharding import PartitionSpec as P

HEAD_DIM = 128


FLOOR = -1e30


def flash_step(flags_ref, qrow_ref, rank_ref, q_ref, k_ref, v_ref, m_in, l_in, acc_in, m_out, l_out, acc_out):
    kb = pl.program_id(1)

    @pl.when(kb == 0)
    def _():
        m_out[...] = m_in[...]
        l_out[...] = l_in[...]
        acc_out[...] = acc_in[...]

    @pl.when(flags_ref[kb] > 0)
    def _():
        scores = lax.dot_general(
            q_ref[...], k_ref[...], (((1,), (1,)), ((), ())), preferred_element_type=jnp.float32
        ) * (HEAD_DIM ** -0.5)
        scores = jnp.where(rank_ref[...] <= qrow_ref[...], scores, FLOOR)
        m_prev = m_out[...]
        m_new = jnp.maximum(m_prev, jnp.max(scores, axis=1, keepdims=True))
        factor = jnp.exp(m_prev - m_new)
        expanded = jnp.exp(scores - m_new[:, :1])
        l_out[...] = factor * l_out[...] + jnp.sum(expanded, axis=1, keepdims=True)
        acc_out[...] = factor * acc_out[...] + jnp.dot(
            expanded.astype(jnp.bfloat16), v_ref[...], preferred_element_type=jnp.float32
        )
        m_out[...] = m_new


def attend(state, flags, qrow, rank, q_src, k_src, k_map, v_src, v_map, key_count, heads, block_len):
    query_count = qrow.shape[0]
    state_spec = pl.BlockSpec((query_count, HEAD_DIM), lambda h, kb, f: (0, h))
    k_block = (block_len, HEAD_DIM) if k_src.ndim == 2 else (None, block_len, HEAD_DIM)
    v_block = (block_len, HEAD_DIM) if v_src.ndim == 2 else (None, block_len, HEAD_DIM)
    grid_spec = pltpu.PrefetchScalarGridSpec(
        num_scalar_prefetch=1,
        grid=(heads, key_count // block_len),
        in_specs=[
            pl.BlockSpec((query_count, 1), lambda h, kb, f: (0, 0)),
            pl.BlockSpec((1, block_len), lambda h, kb, f: (0, kb)),
            pl.BlockSpec((query_count, HEAD_DIM), lambda h, kb, f: (0, h)),
            pl.BlockSpec(k_block, lambda h, kb, f: k_map(h, kb)),
            pl.BlockSpec(v_block, lambda h, kb, f: v_map(h, kb)),
            state_spec,
            state_spec,
            state_spec,
        ],
        out_specs=[state_spec, state_spec, state_spec],
    )
    shape = jax.ShapeDtypeStruct(state[0].shape, jnp.float32)
    return pl.pallas_call(
        flash_step,
        grid_spec=grid_spec,
        out_shape=[shape, shape, shape],
        input_output_aliases={6: 0, 7: 1, 8: 2},
        compiler_params=pltpu.CompilerParams(dimension_semantics=("arbitrary", "arbitrary")),
    )(flags, qrow, rank, q_src, k_src, v_src, *state)


rope_base = 10000.0
norm_eps = 1e-05


def swapped(value, axis, apart):
    mask = 2**apart
    pairs = [(source, source ^ mask) for source in range(lax.axis_size(axis))]
    return lax.ppermute(value, axis, pairs)


def layer_norm(token_rows):
    widened = token_rows.astype(jnp.float32)
    centred = widened - jnp.mean(widened, axis=-1, keepdims=True)
    variance = jnp.mean(centred * centred, axis=-1, keepdims=True)
    return centred * lax.rsqrt(variance + norm_eps)


def rotate(projected, positions, head_dim):
    half_dim = head_dim // 2
    frequency = jnp.exp(-jnp.log(rope_base) * jnp.arange(half_dim, dtype=jnp.float32) / half_dim)
    angles = positions.astype(jnp.float32)[:, None] * frequency[None, :]
    cosine = jnp.cos(angles)[:, None, :]
    sine_part = jnp.sin(angles)[:, None, :]
    shaped = projected.reshape(projected.shape[0], -1, head_dim)
    first_half = shaped[..., :half_dim]
    second = shaped[..., half_dim:]
    turned = jnp.concatenate(
        [first_half * cosine - second * sine_part, second * cosine + first_half * sine_part],
        axis=-1,
    )
    return turned.reshape(projected.shape)


def shards(
    tokens,
    w_query,
    w_key,
    w_value,
    w_out,
    own_cache,
    guest_cache,
    rec_hidden,
    deal_order,
    own_len,
    guest_len,
    rec_index,
):
    groups = lax.axis_size("grp")
    group_id = lax.axis_index("grp")
    partner_id = (group_id + groups // 2) % groups
    swap_bit = groups.bit_length() - 2
    local_width = w_query.shape[1]
    local_heads = local_width // HEAD_DIM
    requests, local_rows, model_width = tokens.shape

    fetched = swapped(guest_cache[0], "grp", swap_bit)

    server = jnp.zeros_like(deal_order).at[deal_order].set(jnp.arange(groups, dtype=jnp.int32))
    start_of = own_len[server] + guest_len[(server + groups // 2) % groups]
    local_positions = (
        start_of[:, None] + group_id * local_rows + jnp.arange(local_rows, dtype=jnp.int32)[None, :]
    ).reshape(-1)

    normed = layer_norm(tokens.reshape(-1, model_width)).astype(jnp.bfloat16)
    queries = rotate(
        jnp.dot(normed, w_query, preferred_element_type=jnp.float32), local_positions, HEAD_DIM
    ).astype(jnp.bfloat16)
    new_keys = rotate(
        jnp.dot(normed, w_key, preferred_element_type=jnp.float32), local_positions, HEAD_DIM
    ).astype(jnp.bfloat16)
    new_values = jnp.dot(normed, w_value, preferred_element_type=jnp.float32).astype(jnp.bfloat16)
    projected = jnp.concatenate([queries, new_keys, new_values], axis=-1).reshape(
        requests, local_rows, 3 * local_width
    )
    arranged = jnp.take(projected, deal_order, axis=0)
    dealt = lax.all_to_all(arranged, "grp", split_axis=0, concat_axis=1, tiled=True)[0]
    span_len = dealt.shape[0]

    own_count = own_len[group_id]
    guest_count = guest_len[partner_id]
    rec_rows = layer_norm(rec_hidden[0]).astype(jnp.bfloat16)
    rec_positions = rec_index[0]
    rec_keys = rotate(
        jnp.dot(rec_rows, w_key, preferred_element_type=jnp.float32), rec_positions, HEAD_DIM
    ).astype(jnp.bfloat16)
    rec_values = jnp.dot(rec_rows, w_value, preferred_element_type=jnp.float32).astype(jnp.bfloat16)
    replaced = jnp.zeros((own_cache.shape[2],), jnp.bool_).at[rec_positions].set(True)

    heads = local_heads
    query_rows = jnp.arange(span_len, dtype=jnp.int32)[:, None]
    never = jnp.int32(1 << 30)
    state = (
        jnp.full((span_len, local_width), FLOOR, jnp.float32),
        jnp.zeros((span_len, local_width), jnp.float32),
        jnp.zeros((span_len, local_width), jnp.float32),
    )
    state = attend(
        state, jnp.ones((2,), jnp.int32), query_rows,
        jnp.arange(span_len, dtype=jnp.int32)[None, :],
        dealt, dealt, lambda h, kb: (kb, heads + h), dealt, lambda h, kb: (kb, 2 * heads + h),
        span_len, heads, span_len // 2,
    )
    rec_count = rec_keys.shape[0]
    state = attend(
        state, jnp.ones((1,), jnp.int32), query_rows, jnp.full((1, rec_count), -1, jnp.int32),
        dealt, rec_keys, lambda h, kb: (kb, h), rec_values, lambda h, kb: (kb, h),
        rec_count, heads, rec_count,
    )
    cap = own_cache.shape[2]
    block_len = 512
    key_rows = jnp.arange(cap, dtype=jnp.int32)
    own_rank = jnp.where((key_rows < own_count) & ~replaced, -1, never)[None, :]
    own_flags = (jnp.arange(cap // block_len, dtype=jnp.int32) * block_len < own_count).astype(jnp.int32)
    state = attend(
        state, own_flags, query_rows, own_rank,
        dealt, own_cache[0], lambda h, kb: (0, kb, h), own_cache[0], lambda h, kb: (1, kb, h),
        cap, heads, block_len,
    )
    gcap = fetched.shape[1]
    guest_rows = jnp.arange(gcap, dtype=jnp.int32)
    guest_rank = jnp.where(guest_rows < guest_count, -1, never)[None, :]
    guest_flags = (jnp.arange(gcap // block_len, dtype=jnp.int32) * block_len < guest_count).astype(jnp.int32)
    state = attend(
        state, guest_flags, query_rows, guest_rank,
        dealt, fetched, lambda h, kb: (0, kb, h), fetched, lambda h, kb: (1, kb, h),
        gcap, heads, block_len,
    )
    attended = (state[2] / state[1]).astype(jnp.bfloat16)
    partial_value = jnp.dot(attended, w_out, preferred_element_type=jnp.float32).astype(
        jnp.bfloat16
    )
    blocks = lax.axis_size("tp")
    exchanged = lax.all_to_all(
        partial_value.reshape(span_len, blocks, -1), "tp", split_axis=1, concat_axis=1, tiled=True
    )
    mixed_rows = exchanged.astype(jnp.float32).sum(axis=1).astype(jnp.bfloat16)
    returned_rows = lax.all_to_all(
        mixed_rows.reshape(groups, local_rows, -1), "grp", split_axis=0, concat_axis=0, tiled=True
    )
    return jnp.take(returned_rows, server, axis=0)


def solution(mesh):
    return jax.shard_map(
        shards,
        mesh=mesh,
        in_specs=(
            P(None, "grp", None),
            P(None, "tp"),
            P(None, "tp"),
            P(None, "tp"),
            P("tp", None),
            P("grp", None, None, "tp"),
            P("grp", None, None, "tp"),
            P("grp", None, None),
            P(),
            P(),
            P(),
            P("grp", None),
        ),
        out_specs=P(None, "grp", "tp"),
        check_vma=False,
    )
```

```python
import jax
import jax.numpy as jnp
from jax import lax
from jax.experimental import pallas as pl
from jax.experimental.pallas import tpu as pltpu
from jax.sharding import PartitionSpec as P

HEAD_DIM = 128


FLOOR = -1e30


def flash_step(flags_ref, qrow_ref, rank_ref, q_ref, k_ref, v_ref, m_in, l_in, acc_in, m_out, l_out, acc_out):
    kb = pl.program_id(1)

    @pl.when(kb == 0)
    def _():
        m_out[...] = m_in[...]
        l_out[...] = l_in[...]
        acc_out[...] = acc_in[...]

    @pl.when(flags_ref[kb] > 0)
    def _():
        scores = lax.dot_general(
            q_ref[...], k_ref[...], (((1,), (1,)), ((), ())), preferred_element_type=jnp.float32
        ) * (HEAD_DIM ** -0.5)
        scores = jnp.where(rank_ref[...] <= qrow_ref[...], scores, FLOOR)
        m_prev = m_out[...]
        m_new = jnp.maximum(m_prev, jnp.max(scores, axis=1, keepdims=True))
        factor = jnp.exp(m_prev - m_new)
        expanded = jnp.exp(scores - m_new[:, :1])
        l_out[...] = factor * l_out[...] + jnp.sum(expanded, axis=1, keepdims=True)
        acc_out[...] = factor * acc_out[...] + jnp.dot(
            expanded.astype(jnp.bfloat16), v_ref[...], preferred_element_type=jnp.float32
        )
        m_out[...] = m_new


def attend(state, flags, qrow, rank, q_src, q_block, k_src, k_map, v_src, v_map, key_count, heads, block_len):
    query_count = qrow.shape[0]
    state_spec = pl.BlockSpec((query_count, HEAD_DIM), lambda h, kb, f: (0, h))
    k_block = (block_len, HEAD_DIM) if k_src.ndim == 2 else (None, block_len, HEAD_DIM)
    v_block = (block_len, HEAD_DIM) if v_src.ndim == 2 else (None, block_len, HEAD_DIM)
    grid_spec = pltpu.PrefetchScalarGridSpec(
        num_scalar_prefetch=1,
        grid=(heads, key_count // block_len),
        in_specs=[
            pl.BlockSpec((query_count, 1), lambda h, kb, f: (0, 0)),
            pl.BlockSpec((1, block_len), lambda h, kb, f: (0, kb)),
            pl.BlockSpec((query_count, HEAD_DIM), lambda h, kb, f: (q_block, h)),
            pl.BlockSpec(k_block, lambda h, kb, f: k_map(h, kb)),
            pl.BlockSpec(v_block, lambda h, kb, f: v_map(h, kb)),
            state_spec,
            state_spec,
            state_spec,
        ],
        out_specs=[state_spec, state_spec, state_spec],
    )
    shape = jax.ShapeDtypeStruct(state[0].shape, jnp.float32)
    return pl.pallas_call(
        flash_step,
        grid_spec=grid_spec,
        out_shape=[shape, shape, shape],
        input_output_aliases={6: 0, 7: 1, 8: 2},
        compiler_params=pltpu.CompilerParams(dimension_semantics=("arbitrary", "arbitrary")),
    )(flags, qrow, rank, q_src, k_src, v_src, *state)


rope_base = 10000.0
norm_eps = 1e-05


def swapped(value, axis, apart):
    mask = 2**apart
    pairs = [(source, source ^ mask) for source in range(lax.axis_size(axis))]
    return lax.ppermute(value, axis, pairs)


def layer_norm(token_rows):
    widened = token_rows.astype(jnp.float32)
    centred = widened - jnp.mean(widened, axis=-1, keepdims=True)
    variance = jnp.mean(centred * centred, axis=-1, keepdims=True)
    return centred * lax.rsqrt(variance + norm_eps)


def rotate(projected, positions, head_dim):
    half_dim = head_dim // 2
    frequency = jnp.exp(-jnp.log(rope_base) * jnp.arange(half_dim, dtype=jnp.float32) / half_dim)
    angles = positions.astype(jnp.float32)[:, None] * frequency[None, :]
    cosine = jnp.cos(angles)[:, None, :]
    sine_part = jnp.sin(angles)[:, None, :]
    shaped = projected.reshape(projected.shape[0], -1, head_dim)
    first_half = shaped[..., :half_dim]
    second = shaped[..., half_dim:]
    turned = jnp.concatenate(
        [first_half * cosine - second * sine_part, second * cosine + first_half * sine_part],
        axis=-1,
    )
    return turned.reshape(projected.shape)


def shards(
    tokens,
    w_query,
    w_key,
    w_value,
    w_out,
    own_cache,
    guest_cache,
    rec_hidden,
    deal_order,
    own_len,
    guest_len,
    rec_index,
):
    groups = lax.axis_size("grp")
    group_id = lax.axis_index("grp")
    partner_id = (group_id + groups // 2) % groups
    swap_bit = groups.bit_length() - 2
    local_width = w_query.shape[1]
    local_heads = local_width // HEAD_DIM
    requests, local_rows, model_width = tokens.shape

    fetched = swapped(guest_cache[0], "grp", swap_bit)

    server = jnp.zeros_like(deal_order).at[deal_order].set(jnp.arange(groups, dtype=jnp.int32))
    start_of = own_len[server] + guest_len[(server + groups // 2) % groups]
    local_positions = (
        start_of[:, None] + group_id * local_rows + jnp.arange(local_rows, dtype=jnp.int32)[None, :]
    ).reshape(-1)

    normed = layer_norm(tokens.reshape(-1, model_width)).astype(jnp.bfloat16)
    queries = rotate(
        jnp.dot(normed, w_query, preferred_element_type=jnp.float32), local_positions, HEAD_DIM
    ).astype(jnp.bfloat16)
    new_keys = rotate(
        jnp.dot(normed, w_key, preferred_element_type=jnp.float32), local_positions, HEAD_DIM
    ).astype(jnp.bfloat16)
    new_values = jnp.dot(normed, w_value, preferred_element_type=jnp.float32).astype(jnp.bfloat16)
    projected = jnp.concatenate([queries, new_keys, new_values], axis=-1).reshape(
        requests, local_rows, 3 * local_width
    )
    arranged = jnp.take(projected, deal_order, axis=0)
    dealt = lax.all_to_all(arranged, "grp", split_axis=0, concat_axis=1, tiled=True)[0]
    span_len = dealt.shape[0]

    own_count = own_len[group_id]
    guest_count = guest_len[partner_id]
    rec_rows = layer_norm(rec_hidden[0]).astype(jnp.bfloat16)
    rec_positions = rec_index[0]
    rec_keys = rotate(
        jnp.dot(rec_rows, w_key, preferred_element_type=jnp.float32), rec_positions, HEAD_DIM
    ).astype(jnp.bfloat16)
    rec_values = jnp.dot(rec_rows, w_value, preferred_element_type=jnp.float32).astype(jnp.bfloat16)
    replaced = jnp.zeros((own_cache.shape[2],), jnp.bool_).at[rec_positions].set(True)

    heads = local_heads
    chunks = 2
    piece = local_rows // chunks
    chunk_len = span_len // chunks
    order = dealt.reshape(groups, chunks, piece, -1).transpose(1, 0, 2, 3).reshape(span_len, -1)
    row_of = (
        jnp.arange(span_len, dtype=jnp.int32).reshape(groups, chunks, piece).transpose(1, 0, 2).reshape(-1)
    )
    rec_count = rec_keys.shape[0]
    fresh = jnp.concatenate(
        [order[:, local_width:], jnp.concatenate([rec_keys, rec_values], axis=1)], axis=0
    )
    fresh_rank = jnp.concatenate([row_of, jnp.full((rec_count,), -1, jnp.int32)])[None, :]
    fresh_count = span_len + rec_count
    never = jnp.int32(1 << 30)
    cap = own_cache.shape[2]
    block_len = 512
    key_rows = jnp.arange(cap, dtype=jnp.int32)
    own_rank = jnp.where((key_rows < own_count) & ~replaced, -1, never)[None, :]
    own_flags = (jnp.arange(cap // block_len, dtype=jnp.int32) * block_len < own_count).astype(jnp.int32)
    gcap = fetched.shape[1]
    guest_rows = jnp.arange(gcap, dtype=jnp.int32)
    guest_rank = jnp.where(guest_rows < guest_count, -1, never)[None, :]
    guest_flags = (jnp.arange(gcap // block_len, dtype=jnp.int32) * block_len < guest_count).astype(jnp.int32)
    blocks = lax.axis_size("tp")
    out_by_block = w_out.reshape(local_width, blocks, -1)

    returned = []
    for chunk in range(chunks):
        query_rows = row_of[chunk * chunk_len : (chunk + 1) * chunk_len][:, None]
        state = (
            jnp.full((chunk_len, local_width), FLOOR, jnp.float32),
            jnp.zeros((chunk_len, local_width), jnp.float32),
            jnp.zeros((chunk_len, local_width), jnp.float32),
        )
        state = attend(
            state, jnp.ones((2,), jnp.int32), query_rows, fresh_rank, order, chunk,
            fresh, lambda h, kb: (kb, h), fresh, lambda h, kb: (kb, heads + h),
            fresh_count, heads, fresh_count // 2,
        )
        state = attend(
            state, own_flags, query_rows, own_rank, order, chunk,
            own_cache[0], lambda h, kb: (0, kb, h), own_cache[0], lambda h, kb: (1, kb, h),
            cap, heads, block_len,
        )
        state = attend(
            state, guest_flags, query_rows, guest_rank, order, chunk,
            fetched, lambda h, kb: (0, kb, h), fetched, lambda h, kb: (1, kb, h),
            gcap, heads, block_len,
        )
        attended = (state[2] / state[1]).astype(jnp.bfloat16)
        partial_value = jnp.einsum(
            "qc,ctd->tqd", attended, out_by_block, preferred_element_type=jnp.float32
        ).astype(jnp.bfloat16)
        exchanged = lax.all_to_all(partial_value, "tp", split_axis=0, concat_axis=0, tiled=True)
        mixed_rows = exchanged.astype(jnp.float32).sum(axis=0).astype(jnp.bfloat16)
        returned.append(
            lax.all_to_all(
                mixed_rows.reshape(groups, piece, -1), "grp", split_axis=0, concat_axis=0, tiled=True
            )
        )
    returned_rows = jnp.stack(returned, axis=1).reshape(groups, local_rows, -1)
    return jnp.take(returned_rows, server, axis=0)


def solution(mesh):
    return jax.shard_map(
        shards,
        mesh=mesh,
        in_specs=(
            P(None, "grp", None),
            P(None, "tp"),
            P(None, "tp"),
            P(None, "tp"),
            P("tp", None),
            P("grp", None, None, "tp"),
            P("grp", None, None, "tp"),
            P("grp", None, None),
            P(),
            P(),
            P(),
            P("grp", None),
        ),
        out_specs=P(None, "grp", "tp"),
        check_vma=False,
    )
```

```python
import jax
import jax.numpy as jnp
from jax import lax
from jax.experimental import pallas as pl
from jax.experimental.pallas import tpu as pltpu
from jax.sharding import PartitionSpec as P

HEAD_DIM = 128


FLOOR = -1e30


def flash_step(flags_ref, qrow_ref, rank_ref, q_ref, k_ref, v_ref, m_in, l_in, acc_in, m_out, l_out, acc_out):
    kb = pl.program_id(1)

    @pl.when(kb == 0)
    def _():
        m_out[...] = m_in[...]
        l_out[...] = l_in[...]
        acc_out[...] = acc_in[...]

    @pl.when(flags_ref[kb] > 0)
    def _():
        scores = lax.dot_general(
            q_ref[...], k_ref[...], (((1,), (1,)), ((), ())), preferred_element_type=jnp.float32
        ) * (HEAD_DIM ** -0.5)
        scores = jnp.where(rank_ref[...] <= qrow_ref[...], scores, FLOOR)
        m_prev = m_out[...]
        m_new = jnp.maximum(m_prev, jnp.max(scores, axis=1, keepdims=True))
        factor = jnp.exp(m_prev - m_new)
        expanded = jnp.exp(scores - m_new[:, :1])
        l_out[...] = factor * l_out[...] + jnp.sum(expanded, axis=1, keepdims=True)
        acc_out[...] = factor * acc_out[...] + jnp.dot(
            expanded.astype(jnp.bfloat16), v_ref[...], preferred_element_type=jnp.float32
        )
        m_out[...] = m_new


def attend(state, flags, qrow, rank, q_src, q_block, k_src, k_map, v_src, v_map, key_count, heads, block_len):
    query_count = qrow.shape[0]
    state_spec = pl.BlockSpec((query_count, HEAD_DIM), lambda h, kb, f: (0, h))
    k_block = (block_len, HEAD_DIM) if k_src.ndim == 2 else (None, block_len, HEAD_DIM)
    v_block = (block_len, HEAD_DIM) if v_src.ndim == 2 else (None, block_len, HEAD_DIM)
    grid_spec = pltpu.PrefetchScalarGridSpec(
        num_scalar_prefetch=1,
        grid=(heads, key_count // block_len),
        in_specs=[
            pl.BlockSpec((query_count, 1), lambda h, kb, f: (0, 0)),
            pl.BlockSpec((1, block_len), lambda h, kb, f: (0, kb)),
            pl.BlockSpec((query_count, HEAD_DIM), lambda h, kb, f: (q_block, h)),
            pl.BlockSpec(k_block, lambda h, kb, f: k_map(h, kb)),
            pl.BlockSpec(v_block, lambda h, kb, f: v_map(h, kb)),
            state_spec,
            state_spec,
            state_spec,
        ],
        out_specs=[state_spec, state_spec, state_spec],
    )
    shape = jax.ShapeDtypeStruct(state[0].shape, jnp.float32)
    return pl.pallas_call(
        flash_step,
        grid_spec=grid_spec,
        out_shape=[shape, shape, shape],
        input_output_aliases={6: 0, 7: 1, 8: 2},
        compiler_params=pltpu.CompilerParams(dimension_semantics=("arbitrary", "arbitrary")),
    )(flags, qrow, rank, q_src, k_src, v_src, *state)


rope_base = 10000.0
norm_eps = 1e-05


def swapped(value, axis, apart):
    mask = 2**apart
    pairs = [(source, source ^ mask) for source in range(lax.axis_size(axis))]
    return lax.ppermute(value, axis, pairs)


def layer_norm(token_rows):
    widened = token_rows.astype(jnp.float32)
    centred = widened - jnp.mean(widened, axis=-1, keepdims=True)
    variance = jnp.mean(centred * centred, axis=-1, keepdims=True)
    return centred * lax.rsqrt(variance + norm_eps)


def rotate(projected, positions, head_dim):
    half_dim = head_dim // 2
    frequency = jnp.exp(-jnp.log(rope_base) * jnp.arange(half_dim, dtype=jnp.float32) / half_dim)
    angles = positions.astype(jnp.float32)[:, None] * frequency[None, :]
    cosine = jnp.cos(angles)[:, None, :]
    sine_part = jnp.sin(angles)[:, None, :]
    shaped = projected.reshape(projected.shape[0], -1, head_dim)
    first_half = shaped[..., :half_dim]
    second = shaped[..., half_dim:]
    turned = jnp.concatenate(
        [first_half * cosine - second * sine_part, second * cosine + first_half * sine_part],
        axis=-1,
    )
    return turned.reshape(projected.shape)


def shards(
    tokens,
    w_query,
    w_key,
    w_value,
    w_out,
    own_cache,
    guest_cache,
    rec_hidden,
    deal_order,
    own_len,
    guest_len,
    rec_index,
):
    groups = lax.axis_size("grp")
    group_id = lax.axis_index("grp")
    partner_id = (group_id + groups // 2) % groups
    swap_bit = groups.bit_length() - 2
    local_width = w_query.shape[1]
    local_heads = local_width // HEAD_DIM
    requests, local_rows, model_width = tokens.shape

    fetched = swapped(guest_cache[0], "grp", swap_bit)

    server = jnp.zeros_like(deal_order).at[deal_order].set(jnp.arange(groups, dtype=jnp.int32))
    start_of = own_len[server] + guest_len[(server + groups // 2) % groups]
    local_positions = (
        start_of[:, None] + group_id * local_rows + jnp.arange(local_rows, dtype=jnp.int32)[None, :]
    ).reshape(-1)

    normed = layer_norm(tokens.reshape(-1, model_width)).astype(jnp.bfloat16)
    queries = rotate(
        jnp.dot(normed, w_query, preferred_element_type=jnp.float32), local_positions, HEAD_DIM
    ).astype(jnp.bfloat16)
    new_keys = rotate(
        jnp.dot(normed, w_key, preferred_element_type=jnp.float32), local_positions, HEAD_DIM
    ).astype(jnp.bfloat16)
    new_values = jnp.dot(normed, w_value, preferred_element_type=jnp.float32).astype(jnp.bfloat16)
    fresh_kv = jnp.concatenate([new_keys, new_values], axis=-1).reshape(requests, local_rows, -1)
    dealt_q = lax.all_to_all(
        jnp.take(queries.reshape(requests, local_rows, -1), deal_order, axis=0),
        "grp", split_axis=0, concat_axis=1, tiled=True,
    )[0]
    dealt_kv = lax.all_to_all(
        jnp.take(fresh_kv, deal_order, axis=0), "grp", split_axis=0, concat_axis=1, tiled=True
    )[0]
    span_len = dealt_q.shape[0]

    own_count = own_len[group_id]
    guest_count = guest_len[partner_id]
    rec_rows = layer_norm(rec_hidden[0]).astype(jnp.bfloat16)
    rec_positions = rec_index[0]
    rec_keys = rotate(
        jnp.dot(rec_rows, w_key, preferred_element_type=jnp.float32), rec_positions, HEAD_DIM
    ).astype(jnp.bfloat16)
    rec_values = jnp.dot(rec_rows, w_value, preferred_element_type=jnp.float32).astype(jnp.bfloat16)
    replaced = jnp.zeros((own_cache.shape[2],), jnp.bool_).at[rec_positions].set(True)

    heads = local_heads
    chunks = 2
    piece = local_rows // chunks
    chunk_len = span_len // chunks
    def chunk_major(rows):
        return rows.reshape(groups, chunks, piece, -1).transpose(1, 0, 2, 3).reshape(span_len, -1)

    order = chunk_major(dealt_q)
    row_of = (
        jnp.arange(span_len, dtype=jnp.int32).reshape(groups, chunks, piece).transpose(1, 0, 2).reshape(-1)
    )
    rec_count = rec_keys.shape[0]
    fresh = jnp.concatenate(
        [chunk_major(dealt_kv), jnp.concatenate([rec_keys, rec_values], axis=1)], axis=0
    )
    fresh_rank = jnp.concatenate([row_of, jnp.full((rec_count,), -1, jnp.int32)])[None, :]
    fresh_count = span_len + rec_count
    never = jnp.int32(1 << 30)
    cap = own_cache.shape[2]
    block_len = 512
    key_rows = jnp.arange(cap, dtype=jnp.int32)
    own_rank = jnp.where((key_rows < own_count) & ~replaced, -1, never)[None, :]
    own_flags = (jnp.arange(cap // block_len, dtype=jnp.int32) * block_len < own_count).astype(jnp.int32)
    gcap = fetched.shape[1]
    guest_rows = jnp.arange(gcap, dtype=jnp.int32)
    guest_rank = jnp.where(guest_rows < guest_count, -1, never)[None, :]
    guest_flags = (jnp.arange(gcap // block_len, dtype=jnp.int32) * block_len < guest_count).astype(jnp.int32)
    blocks = lax.axis_size("tp")
    out_by_block = w_out.reshape(local_width, blocks, -1)

    returned = []
    for chunk in range(chunks):
        query_rows = row_of[chunk * chunk_len : (chunk + 1) * chunk_len][:, None]
        state = (
            jnp.full((chunk_len, local_width), FLOOR, jnp.float32),
            jnp.zeros((chunk_len, local_width), jnp.float32),
            jnp.zeros((chunk_len, local_width), jnp.float32),
        )
        state = attend(
            state, own_flags, query_rows, own_rank, order, chunk,
            own_cache[0], lambda h, kb: (0, kb, h), own_cache[0], lambda h, kb: (1, kb, h),
            cap, heads, block_len,
        )
        state = attend(
            state, guest_flags, query_rows, guest_rank, order, chunk,
            fetched, lambda h, kb: (0, kb, h), fetched, lambda h, kb: (1, kb, h),
            gcap, heads, block_len,
        )
        state = attend(
            state, jnp.ones((2,), jnp.int32), query_rows, fresh_rank, order, chunk,
            fresh, lambda h, kb: (kb, h), fresh, lambda h, kb: (kb, heads + h),
            fresh_count, heads, fresh_count // 2,
        )
        attended = (state[2] / state[1]).astype(jnp.bfloat16)
        partial_value = jnp.einsum(
            "qc,ctd->tqd", attended, out_by_block, preferred_element_type=jnp.float32
        ).astype(jnp.bfloat16)
        exchanged = lax.all_to_all(partial_value, "tp", split_axis=0, concat_axis=0, tiled=True)
        mixed_rows = exchanged.astype(jnp.float32).sum(axis=0).astype(jnp.bfloat16)
        returned.append(
            lax.all_to_all(
                mixed_rows.reshape(groups, piece, -1), "grp", split_axis=0, concat_axis=0, tiled=True
            )
        )
    returned_rows = jnp.stack(returned, axis=1).reshape(groups, local_rows, -1)
    return jnp.take(returned_rows, server, axis=0)


def solution(mesh):
    return jax.shard_map(
        shards,
        mesh=mesh,
        in_specs=(
            P(None, "grp", None),
            P(None, "tp"),
            P(None, "tp"),
            P(None, "tp"),
            P("tp", None),
            P("grp", None, None, "tp"),
            P("grp", None, None, "tp"),
            P("grp", None, None),
            P(),
            P(),
            P(),
            P("grp", None),
        ),
        out_specs=P(None, "grp", "tp"),
        check_vma=False,
    )
```

```python
import functools

import jax
import jax.numpy as jnp
from jax import lax
from jax.experimental import pallas as pl
from jax.experimental.pallas import tpu as pltpu
from jax.sharding import PartitionSpec as P

HEAD_DIM = 128


FLOOR = -1e30


def flash_step(flags_ref, qrow_ref, rank_ref, q_ref, k_ref, v_ref, m_in, l_in, acc_in, m_out, l_out, acc_out):
    kb = pl.program_id(1)

    @pl.when(kb == 0)
    def _():
        m_out[...] = m_in[...]
        l_out[...] = l_in[...]
        acc_out[...] = acc_in[...]

    @pl.when(flags_ref[kb] > 0)
    def _():
        scores = lax.dot_general(
            q_ref[...], k_ref[...], (((1,), (1,)), ((), ())), preferred_element_type=jnp.float32
        ) * (HEAD_DIM ** -0.5)
        scores = jnp.where(rank_ref[...] <= qrow_ref[...], scores, FLOOR)
        m_prev = m_out[...]
        m_new = jnp.maximum(m_prev, jnp.max(scores, axis=1, keepdims=True))
        factor = jnp.exp(m_prev - m_new)
        expanded = jnp.exp(scores - m_new[:, :1])
        l_out[...] = factor * l_out[...] + jnp.sum(expanded, axis=1, keepdims=True)
        acc_out[...] = factor * acc_out[...] + jnp.dot(
            expanded.astype(jnp.bfloat16), v_ref[...], preferred_element_type=jnp.float32
        )
        m_out[...] = m_new


def attend(state, flags, qrow, rank, q_src, k_src, k_map, v_src, v_map, key_count, heads, block_len):
    query_count = qrow.shape[0]
    state_spec = pl.BlockSpec((query_count, HEAD_DIM), lambda h, kb, f: (0, h))
    k_block = (block_len, HEAD_DIM) if k_src.ndim == 2 else (None, block_len, HEAD_DIM)
    v_block = (block_len, HEAD_DIM) if v_src.ndim == 2 else (None, block_len, HEAD_DIM)
    grid_spec = pltpu.PrefetchScalarGridSpec(
        num_scalar_prefetch=1,
        grid=(heads, key_count // block_len),
        in_specs=[
            pl.BlockSpec((query_count, 1), lambda h, kb, f: (0, 0)),
            pl.BlockSpec((1, block_len), lambda h, kb, f: (0, kb)),
            pl.BlockSpec((query_count, HEAD_DIM), lambda h, kb, f: (0, h)),
            pl.BlockSpec(k_block, lambda h, kb, f: k_map(h, kb)),
            pl.BlockSpec(v_block, lambda h, kb, f: v_map(h, kb)),
            state_spec,
            state_spec,
            state_spec,
        ],
        out_specs=[state_spec, state_spec, state_spec],
    )
    shape = jax.ShapeDtypeStruct(state[0].shape, jnp.float32)
    return pl.pallas_call(
        flash_step,
        grid_spec=grid_spec,
        out_shape=[shape, shape, shape],
        input_output_aliases={6: 0, 7: 1, 8: 2},
        compiler_params=pltpu.CompilerParams(dimension_semantics=("arbitrary", "arbitrary")),
    )(flags, qrow, rank, q_src, k_src, v_src, *state)


def exchange_step(axis, count, x_ref, y_ref, local_sem, send_sem, recv_sem):
    me = lax.axis_index(axis)
    barrier = pltpu.get_barrier_semaphore()
    for step in range(1, count):
        pl.semaphore_signal(
            barrier, inc=1, device_id={axis: lax.rem(me + step, count)},
            device_id_type=pl.DeviceIdType.MESH,
        )
    pl.semaphore_wait(barrier, count - 1)
    own = pltpu.make_async_copy(x_ref.at[me], y_ref.at[me], local_sem)
    own.start()
    sends = []
    for step in range(1, count):
        target = lax.rem(me + step, count)
        copy = pltpu.make_async_remote_copy(
            src_ref=x_ref.at[target],
            dst_ref=y_ref.at[me],
            send_sem=send_sem.at[step],
            recv_sem=recv_sem.at[me],
            device_id={axis: target},
            device_id_type=pl.DeviceIdType.MESH,
        )
        copy.start()
        sends.append(copy)
    for copy in sends:
        copy.wait_send()
    for step in range(1, count):
        source = lax.rem(me + count - step, count)
        pltpu.make_async_remote_copy(
            src_ref=x_ref.at[source],
            dst_ref=y_ref.at[source],
            send_sem=send_sem.at[step],
            recv_sem=recv_sem.at[source],
            device_id={axis: source},
            device_id_type=pl.DeviceIdType.MESH,
        ).wait_recv()
    own.wait()


def exchange(blocks, axis, collective):
    count = blocks.shape[0]
    return pl.pallas_call(
        functools.partial(exchange_step, axis, count),
        out_shape=jax.ShapeDtypeStruct(blocks.shape, blocks.dtype),
        in_specs=[pl.BlockSpec(memory_space=pl.ANY)],
        out_specs=pl.BlockSpec(memory_space=pl.ANY),
        scratch_shapes=[
            pltpu.SemaphoreType.DMA(()),
            pltpu.SemaphoreType.DMA((count,)),
            pltpu.SemaphoreType.DMA((count,)),
        ],
        compiler_params=pltpu.CompilerParams(collective_id=collective, has_side_effects=True),
    )(blocks)


rope_base = 10000.0
norm_eps = 1e-05


def swapped(value, axis, apart):
    mask = 2**apart
    pairs = [(source, source ^ mask) for source in range(lax.axis_size(axis))]
    return lax.ppermute(value, axis, pairs)


def layer_norm(token_rows):
    widened = token_rows.astype(jnp.float32)
    centred = widened - jnp.mean(widened, axis=-1, keepdims=True)
    variance = jnp.mean(centred * centred, axis=-1, keepdims=True)
    return centred * lax.rsqrt(variance + norm_eps)


def rotate(projected, positions, head_dim):
    half_dim = head_dim // 2
    frequency = jnp.exp(-jnp.log(rope_base) * jnp.arange(half_dim, dtype=jnp.float32) / half_dim)
    angles = positions.astype(jnp.float32)[:, None] * frequency[None, :]
    cosine = jnp.cos(angles)[:, None, :]
    sine_part = jnp.sin(angles)[:, None, :]
    shaped = projected.reshape(projected.shape[0], -1, head_dim)
    first_half = shaped[..., :half_dim]
    second = shaped[..., half_dim:]
    turned = jnp.concatenate(
        [first_half * cosine - second * sine_part, second * cosine + first_half * sine_part],
        axis=-1,
    )
    return turned.reshape(projected.shape)


def shards(
    tokens,
    w_query,
    w_key,
    w_value,
    w_out,
    own_cache,
    guest_cache,
    rec_hidden,
    deal_order,
    own_len,
    guest_len,
    rec_index,
):
    groups = lax.axis_size("grp")
    group_id = lax.axis_index("grp")
    partner_id = (group_id + groups // 2) % groups
    swap_bit = groups.bit_length() - 2
    local_width = w_query.shape[1]
    local_heads = local_width // HEAD_DIM
    requests, local_rows, model_width = tokens.shape

    fetched = swapped(guest_cache[0], "grp", swap_bit)

    server = jnp.zeros_like(deal_order).at[deal_order].set(jnp.arange(groups, dtype=jnp.int32))
    start_of = own_len[server] + guest_len[(server + groups // 2) % groups]
    local_positions = (
        start_of[:, None] + group_id * local_rows + jnp.arange(local_rows, dtype=jnp.int32)[None, :]
    ).reshape(-1)

    normed = layer_norm(tokens.reshape(-1, model_width)).astype(jnp.bfloat16)
    queries = rotate(
        jnp.dot(normed, w_query, preferred_element_type=jnp.float32), local_positions, HEAD_DIM
    ).astype(jnp.bfloat16)
    new_keys = rotate(
        jnp.dot(normed, w_key, preferred_element_type=jnp.float32), local_positions, HEAD_DIM
    ).astype(jnp.bfloat16)
    new_values = jnp.dot(normed, w_value, preferred_element_type=jnp.float32).astype(jnp.bfloat16)
    projected = jnp.concatenate([queries, new_keys, new_values], axis=-1).reshape(
        requests, local_rows, 3 * local_width
    )
    arranged = jnp.take(projected, deal_order, axis=0)
    dealt = lax.all_to_all(arranged, "grp", split_axis=0, concat_axis=1, tiled=True)[0]
    span_len = dealt.shape[0]

    own_count = own_len[group_id]
    guest_count = guest_len[partner_id]
    rec_rows = layer_norm(rec_hidden[0]).astype(jnp.bfloat16)
    rec_positions = rec_index[0]
    rec_keys = rotate(
        jnp.dot(rec_rows, w_key, preferred_element_type=jnp.float32), rec_positions, HEAD_DIM
    ).astype(jnp.bfloat16)
    rec_values = jnp.dot(rec_rows, w_value, preferred_element_type=jnp.float32).astype(jnp.bfloat16)
    replaced = jnp.zeros((own_cache.shape[2],), jnp.bool_).at[rec_positions].set(True)

    heads = local_heads
    query_rows = jnp.arange(span_len, dtype=jnp.int32)[:, None]
    never = jnp.int32(1 << 30)
    state = (
        jnp.full((span_len, local_width), FLOOR, jnp.float32),
        jnp.zeros((span_len, local_width), jnp.float32),
        jnp.zeros((span_len, local_width), jnp.float32),
    )
    state = attend(
        state, jnp.ones((2,), jnp.int32), query_rows,
        jnp.arange(span_len, dtype=jnp.int32)[None, :],
        dealt, dealt, lambda h, kb: (kb, heads + h), dealt, lambda h, kb: (kb, 2 * heads + h),
        span_len, heads, span_len // 2,
    )
    rec_count = rec_keys.shape[0]
    state = attend(
        state, jnp.ones((1,), jnp.int32), query_rows, jnp.full((1, rec_count), -1, jnp.int32),
        dealt, rec_keys, lambda h, kb: (kb, h), rec_values, lambda h, kb: (kb, h),
        rec_count, heads, rec_count,
    )
    cap = own_cache.shape[2]
    block_len = 512
    key_rows = jnp.arange(cap, dtype=jnp.int32)
    own_rank = jnp.where((key_rows < own_count) & ~replaced, -1, never)[None, :]
    own_flags = (jnp.arange(cap // block_len, dtype=jnp.int32) * block_len < own_count).astype(jnp.int32)
    state = attend(
        state, own_flags, query_rows, own_rank,
        dealt, own_cache[0], lambda h, kb: (0, kb, h), own_cache[0], lambda h, kb: (1, kb, h),
        cap, heads, block_len,
    )
    gcap = fetched.shape[1]
    guest_rows = jnp.arange(gcap, dtype=jnp.int32)
    guest_rank = jnp.where(guest_rows < guest_count, -1, never)[None, :]
    guest_flags = (jnp.arange(gcap // block_len, dtype=jnp.int32) * block_len < guest_count).astype(jnp.int32)
    state = attend(
        state, guest_flags, query_rows, guest_rank,
        dealt, fetched, lambda h, kb: (0, kb, h), fetched, lambda h, kb: (1, kb, h),
        gcap, heads, block_len,
    )
    attended = (state[2] / state[1]).astype(jnp.bfloat16)
    blocks = lax.axis_size("tp")
    partial_value = jnp.einsum(
        "qc,ctd->tqd", attended, w_out.reshape(local_width, blocks, -1), preferred_element_type=jnp.float32
    ).astype(jnp.bfloat16)
    exchanged = exchange(partial_value, "tp", 0)
    mixed_rows = exchanged.astype(jnp.float32).sum(axis=0).astype(jnp.bfloat16)
    returned_rows = exchange(mixed_rows.reshape(groups, local_rows, -1), "grp", 1)
    return jnp.take(returned_rows, server, axis=0)


def solution(mesh):
    return jax.shard_map(
        shards,
        mesh=mesh,
        in_specs=(
            P(None, "grp", None),
            P(None, "tp"),
            P(None, "tp"),
            P(None, "tp"),
            P("tp", None),
            P("grp", None, None, "tp"),
            P("grp", None, None, "tp"),
            P("grp", None, None),
            P(),
            P(),
            P(),
            P("grp", None),
        ),
        out_specs=P(None, "grp", "tp"),
        check_vma=False,
    )
```

```python
import functools

import jax
import jax.numpy as jnp
from jax import lax
from jax.experimental import pallas as pl
from jax.experimental.pallas import tpu as pltpu
from jax.sharding import PartitionSpec as P

HEAD_DIM = 128


FLOOR = -1e30


def flash_step(flags_ref, qrow_ref, rank_ref, q_ref, k_ref, v_ref, m_in, l_in, acc_in, m_out, l_out, acc_out):
    kb = pl.program_id(1)

    @pl.when(kb == 0)
    def _():
        m_out[...] = m_in[...]
        l_out[...] = l_in[...]
        acc_out[...] = acc_in[...]

    @pl.when(flags_ref[kb] > 0)
    def _():
        scores = lax.dot_general(
            q_ref[...], k_ref[...], (((1,), (1,)), ((), ())), preferred_element_type=jnp.float32
        ) * (HEAD_DIM ** -0.5)
        scores = jnp.where(rank_ref[...] <= qrow_ref[...], scores, FLOOR)
        m_prev = m_out[...]
        m_new = jnp.maximum(m_prev, jnp.max(scores, axis=1, keepdims=True))
        factor = jnp.exp(m_prev - m_new)
        expanded = jnp.exp(scores - m_new[:, :1])
        l_out[...] = factor * l_out[...] + jnp.sum(expanded, axis=1, keepdims=True)
        acc_out[...] = factor * acc_out[...] + jnp.dot(
            expanded.astype(jnp.bfloat16), v_ref[...], preferred_element_type=jnp.float32
        )
        m_out[...] = m_new


def attend(state, flags, qrow, rank, q_src, q_block, k_src, k_map, v_src, v_map, key_count, heads, block_len):
    query_count = qrow.shape[0]
    state_spec = pl.BlockSpec((query_count, HEAD_DIM), lambda h, kb, f: (0, h))
    k_block = (block_len, HEAD_DIM) if k_src.ndim == 2 else (None, block_len, HEAD_DIM)
    v_block = (block_len, HEAD_DIM) if v_src.ndim == 2 else (None, block_len, HEAD_DIM)
    grid_spec = pltpu.PrefetchScalarGridSpec(
        num_scalar_prefetch=1,
        grid=(heads, key_count // block_len),
        in_specs=[
            pl.BlockSpec((query_count, 1), lambda h, kb, f: (0, 0)),
            pl.BlockSpec((1, block_len), lambda h, kb, f: (0, kb)),
            pl.BlockSpec((query_count, HEAD_DIM), lambda h, kb, f: (q_block, h)),
            pl.BlockSpec(k_block, lambda h, kb, f: k_map(h, kb)),
            pl.BlockSpec(v_block, lambda h, kb, f: v_map(h, kb)),
            state_spec,
            state_spec,
            state_spec,
        ],
        out_specs=[state_spec, state_spec, state_spec],
    )
    shape = jax.ShapeDtypeStruct(state[0].shape, jnp.float32)
    return pl.pallas_call(
        flash_step,
        grid_spec=grid_spec,
        out_shape=[shape, shape, shape],
        input_output_aliases={6: 0, 7: 1, 8: 2},
        compiler_params=pltpu.CompilerParams(dimension_semantics=("arbitrary", "arbitrary")),
    )(flags, qrow, rank, q_src, k_src, v_src, *state)


def exchange_step(axis, count, x_ref, y_ref, local_sem, send_sem, recv_sem):
    me = lax.axis_index(axis)
    barrier = pltpu.get_barrier_semaphore()
    for step in range(1, count):
        pl.semaphore_signal(
            barrier, inc=1, device_id={axis: lax.rem(me + step, count)},
            device_id_type=pl.DeviceIdType.MESH,
        )
    pl.semaphore_wait(barrier, count - 1)
    own = pltpu.make_async_copy(x_ref.at[me], y_ref.at[me], local_sem)
    own.start()
    sends = []
    for step in range(1, count):
        target = lax.rem(me + step, count)
        copy = pltpu.make_async_remote_copy(
            src_ref=x_ref.at[target],
            dst_ref=y_ref.at[me],
            send_sem=send_sem.at[step],
            recv_sem=recv_sem.at[me],
            device_id={axis: target},
            device_id_type=pl.DeviceIdType.MESH,
        )
        copy.start()
        sends.append(copy)
    for copy in sends:
        copy.wait_send()
    for step in range(1, count):
        source = lax.rem(me + count - step, count)
        pltpu.make_async_remote_copy(
            src_ref=x_ref.at[source],
            dst_ref=y_ref.at[source],
            send_sem=send_sem.at[step],
            recv_sem=recv_sem.at[source],
            device_id={axis: source},
            device_id_type=pl.DeviceIdType.MESH,
        ).wait_recv()
    own.wait()


def exchange(blocks, axis, collective):
    count = blocks.shape[0]
    return pl.pallas_call(
        functools.partial(exchange_step, axis, count),
        out_shape=jax.ShapeDtypeStruct(blocks.shape, blocks.dtype),
        in_specs=[pl.BlockSpec(memory_space=pl.ANY)],
        out_specs=pl.BlockSpec(memory_space=pl.ANY),
        scratch_shapes=[
            pltpu.SemaphoreType.DMA(()),
            pltpu.SemaphoreType.DMA((count,)),
            pltpu.SemaphoreType.DMA((count,)),
        ],
        compiler_params=pltpu.CompilerParams(collective_id=collective, has_side_effects=True),
    )(blocks)


rope_base = 10000.0
norm_eps = 1e-05


def swapped(value, axis, apart):
    mask = 2**apart
    pairs = [(source, source ^ mask) for source in range(lax.axis_size(axis))]
    return lax.ppermute(value, axis, pairs)


def layer_norm(token_rows):
    widened = token_rows.astype(jnp.float32)
    centred = widened - jnp.mean(widened, axis=-1, keepdims=True)
    variance = jnp.mean(centred * centred, axis=-1, keepdims=True)
    return centred * lax.rsqrt(variance + norm_eps)


def rotate(projected, positions, head_dim):
    half_dim = head_dim // 2
    frequency = jnp.exp(-jnp.log(rope_base) * jnp.arange(half_dim, dtype=jnp.float32) / half_dim)
    angles = positions.astype(jnp.float32)[:, None] * frequency[None, :]
    cosine = jnp.cos(angles)[:, None, :]
    sine_part = jnp.sin(angles)[:, None, :]
    shaped = projected.reshape(projected.shape[0], -1, head_dim)
    first_half = shaped[..., :half_dim]
    second = shaped[..., half_dim:]
    turned = jnp.concatenate(
        [first_half * cosine - second * sine_part, second * cosine + first_half * sine_part],
        axis=-1,
    )
    return turned.reshape(projected.shape)


def shards(
    tokens,
    w_query,
    w_key,
    w_value,
    w_out,
    own_cache,
    guest_cache,
    rec_hidden,
    deal_order,
    own_len,
    guest_len,
    rec_index,
):
    groups = lax.axis_size("grp")
    group_id = lax.axis_index("grp")
    partner_id = (group_id + groups // 2) % groups
    swap_bit = groups.bit_length() - 2
    local_width = w_query.shape[1]
    local_heads = local_width // HEAD_DIM
    requests, local_rows, model_width = tokens.shape

    fetched = swapped(guest_cache[0], "grp", swap_bit)

    server = jnp.zeros_like(deal_order).at[deal_order].set(jnp.arange(groups, dtype=jnp.int32))
    start_of = own_len[server] + guest_len[(server + groups // 2) % groups]
    local_positions = (
        start_of[:, None] + group_id * local_rows + jnp.arange(local_rows, dtype=jnp.int32)[None, :]
    ).reshape(-1)

    normed = layer_norm(tokens.reshape(-1, model_width)).astype(jnp.bfloat16)
    queries = rotate(
        jnp.dot(normed, w_query, preferred_element_type=jnp.float32), local_positions, HEAD_DIM
    ).astype(jnp.bfloat16)
    new_keys = rotate(
        jnp.dot(normed, w_key, preferred_element_type=jnp.float32), local_positions, HEAD_DIM
    ).astype(jnp.bfloat16)
    new_values = jnp.dot(normed, w_value, preferred_element_type=jnp.float32).astype(jnp.bfloat16)
    projected = jnp.concatenate([queries, new_keys, new_values], axis=-1).reshape(
        requests, local_rows, 3 * local_width
    )
    arranged = jnp.take(projected, deal_order, axis=0)
    dealt = lax.all_to_all(arranged, "grp", split_axis=0, concat_axis=1, tiled=True)[0]
    span_len = dealt.shape[0]

    own_count = own_len[group_id]
    guest_count = guest_len[partner_id]
    rec_rows = layer_norm(rec_hidden[0]).astype(jnp.bfloat16)
    rec_positions = rec_index[0]
    rec_keys = rotate(
        jnp.dot(rec_rows, w_key, preferred_element_type=jnp.float32), rec_positions, HEAD_DIM
    ).astype(jnp.bfloat16)
    rec_values = jnp.dot(rec_rows, w_value, preferred_element_type=jnp.float32).astype(jnp.bfloat16)
    replaced = jnp.zeros((own_cache.shape[2],), jnp.bool_).at[rec_positions].set(True)

    heads = local_heads
    chunks = 2
    piece = local_rows // chunks
    chunk_len = span_len // chunks
    order = dealt.reshape(groups, chunks, piece, -1).transpose(1, 0, 2, 3).reshape(span_len, -1)
    row_of = (
        jnp.arange(span_len, dtype=jnp.int32).reshape(groups, chunks, piece).transpose(1, 0, 2).reshape(-1)
    )
    rec_count = rec_keys.shape[0]
    fresh = jnp.concatenate(
        [order[:, local_width:], jnp.concatenate([rec_keys, rec_values], axis=1)], axis=0
    )
    fresh_rank = jnp.concatenate([row_of, jnp.full((rec_count,), -1, jnp.int32)])[None, :]
    fresh_count = span_len + rec_count
    never = jnp.int32(1 << 30)
    cap = own_cache.shape[2]
    block_len = 512
    key_rows = jnp.arange(cap, dtype=jnp.int32)
    own_rank = jnp.where((key_rows < own_count) & ~replaced, -1, never)[None, :]
    own_flags = (jnp.arange(cap // block_len, dtype=jnp.int32) * block_len < own_count).astype(jnp.int32)
    gcap = fetched.shape[1]
    guest_rows = jnp.arange(gcap, dtype=jnp.int32)
    guest_rank = jnp.where(guest_rows < guest_count, -1, never)[None, :]
    guest_flags = (jnp.arange(gcap // block_len, dtype=jnp.int32) * block_len < guest_count).astype(jnp.int32)
    blocks = lax.axis_size("tp")
    out_by_block = w_out.reshape(local_width, blocks, -1)

    returned = []
    for chunk in range(chunks):
        query_rows = row_of[chunk * chunk_len : (chunk + 1) * chunk_len][:, None]
        state = (
            jnp.full((chunk_len, local_width), FLOOR, jnp.float32),
            jnp.zeros((chunk_len, local_width), jnp.float32),
            jnp.zeros((chunk_len, local_width), jnp.float32),
        )
        state = attend(
            state, jnp.ones((2,), jnp.int32), query_rows, fresh_rank, order, chunk,
            fresh, lambda h, kb: (kb, h), fresh, lambda h, kb: (kb, heads + h),
            fresh_count, heads, fresh_count // 2,
        )
        state = attend(
            state, own_flags, query_rows, own_rank, order, chunk,
            own_cache[0], lambda h, kb: (0, kb, h), own_cache[0], lambda h, kb: (1, kb, h),
            cap, heads, block_len,
        )
        state = attend(
            state, guest_flags, query_rows, guest_rank, order, chunk,
            fetched, lambda h, kb: (0, kb, h), fetched, lambda h, kb: (1, kb, h),
            gcap, heads, block_len,
        )
        attended = (state[2] / state[1]).astype(jnp.bfloat16)
        partial_value = jnp.einsum(
            "qc,ctd->tqd", attended, out_by_block, preferred_element_type=jnp.float32
        ).astype(jnp.bfloat16)
        exchanged = lax.all_to_all(partial_value, "tp", split_axis=0, concat_axis=0, tiled=True)
        mixed_rows = exchanged.astype(jnp.float32).sum(axis=0).astype(jnp.bfloat16)
        returned.append(mixed_rows.reshape(groups, piece, -1))
    returned_rows = exchange(jnp.stack(returned, axis=1).reshape(groups, local_rows, -1), "grp", 1)
    return jnp.take(returned_rows, server, axis=0)


def solution(mesh):
    return jax.shard_map(
        shards,
        mesh=mesh,
        in_specs=(
            P(None, "grp", None),
            P(None, "tp"),
            P(None, "tp"),
            P(None, "tp"),
            P("tp", None),
            P("grp", None, None, "tp"),
            P("grp", None, None, "tp"),
            P("grp", None, None),
            P(),
            P(),
            P(),
            P("grp", None),
        ),
        out_specs=P(None, "grp", "tp"),
        check_vma=False,
    )
```

```python
import functools

import jax
import jax.numpy as jnp
from jax import lax
from jax.experimental import pallas as pl
from jax.experimental.pallas import tpu as pltpu
from jax.sharding import PartitionSpec as P

HEAD_DIM = 128


FLOOR = -1e30


def flash_step(flags_ref, qrow_ref, rank_ref, q_ref, k_ref, v_ref, m_in, l_in, acc_in, m_out, l_out, acc_out):
    kb = pl.program_id(1)

    @pl.when(kb == 0)
    def _():
        m_out[...] = m_in[...]
        l_out[...] = l_in[...]
        acc_out[...] = acc_in[...]

    @pl.when(flags_ref[kb] > 0)
    def _():
        scores = lax.dot_general(
            q_ref[...], k_ref[...], (((1,), (1,)), ((), ())), preferred_element_type=jnp.float32
        ) * (HEAD_DIM ** -0.5)
        scores = jnp.where(rank_ref[...] <= qrow_ref[...], scores, FLOOR)
        m_prev = m_out[...]
        m_new = jnp.maximum(m_prev, jnp.max(scores, axis=1, keepdims=True))
        factor = jnp.exp(m_prev - m_new)
        expanded = jnp.exp(scores - m_new[:, :1])
        l_out[...] = factor * l_out[...] + jnp.sum(expanded, axis=1, keepdims=True)
        acc_out[...] = factor * acc_out[...] + jnp.dot(
            expanded.astype(jnp.bfloat16), v_ref[...], preferred_element_type=jnp.float32
        )
        m_out[...] = m_new


def attend(state, flags, qrow, rank, q_src, q_block, k_src, k_map, v_src, v_map, key_count, heads, block_len):
    query_count = qrow.shape[0]
    state_spec = pl.BlockSpec((query_count, HEAD_DIM), lambda h, kb, f: (0, h))
    k_block = (block_len, HEAD_DIM) if k_src.ndim == 2 else (None, block_len, HEAD_DIM)
    v_block = (block_len, HEAD_DIM) if v_src.ndim == 2 else (None, block_len, HEAD_DIM)
    grid_spec = pltpu.PrefetchScalarGridSpec(
        num_scalar_prefetch=1,
        grid=(heads, key_count // block_len),
        in_specs=[
            pl.BlockSpec((query_count, 1), lambda h, kb, f: (0, 0)),
            pl.BlockSpec((1, block_len), lambda h, kb, f: (0, kb)),
            pl.BlockSpec((query_count, HEAD_DIM), lambda h, kb, f: (q_block, h)),
            pl.BlockSpec(k_block, lambda h, kb, f: k_map(h, kb)),
            pl.BlockSpec(v_block, lambda h, kb, f: v_map(h, kb)),
            state_spec,
            state_spec,
            state_spec,
        ],
        out_specs=[state_spec, state_spec, state_spec],
    )
    shape = jax.ShapeDtypeStruct(state[0].shape, jnp.float32)
    return pl.pallas_call(
        flash_step,
        grid_spec=grid_spec,
        out_shape=[shape, shape, shape],
        input_output_aliases={6: 0, 7: 1, 8: 2},
        compiler_params=pltpu.CompilerParams(dimension_semantics=("arbitrary", "arbitrary")),
    )(flags, qrow, rank, q_src, k_src, v_src, *state)


def exchange_step(axis, count, x_ref, y_ref, local_sem, send_sem, recv_sem):
    me = lax.axis_index(axis)
    barrier = pltpu.get_barrier_semaphore()
    for step in range(1, count):
        pl.semaphore_signal(
            barrier, inc=1, device_id={axis: lax.rem(me + step, count)},
            device_id_type=pl.DeviceIdType.MESH,
        )
    pl.semaphore_wait(barrier, count - 1)
    own = pltpu.make_async_copy(x_ref.at[me], y_ref.at[me], local_sem)
    own.start()
    sends = []
    for step in range(1, count):
        target = lax.rem(me + step, count)
        copy = pltpu.make_async_remote_copy(
            src_ref=x_ref.at[target],
            dst_ref=y_ref.at[me],
            send_sem=send_sem.at[step],
            recv_sem=recv_sem.at[me],
            device_id={axis: target},
            device_id_type=pl.DeviceIdType.MESH,
        )
        copy.start()
        sends.append(copy)
    for copy in sends:
        copy.wait_send()
    for step in range(1, count):
        source = lax.rem(me + count - step, count)
        pltpu.make_async_remote_copy(
            src_ref=x_ref.at[source],
            dst_ref=y_ref.at[source],
            send_sem=send_sem.at[step],
            recv_sem=recv_sem.at[source],
            device_id={axis: source},
            device_id_type=pl.DeviceIdType.MESH,
        ).wait_recv()
    own.wait()


def exchange(blocks, axis, collective):
    count = blocks.shape[0]
    return pl.pallas_call(
        functools.partial(exchange_step, axis, count),
        out_shape=jax.ShapeDtypeStruct(blocks.shape, blocks.dtype),
        in_specs=[pl.BlockSpec(memory_space=pl.ANY)],
        out_specs=pl.BlockSpec(memory_space=pl.ANY),
        scratch_shapes=[
            pltpu.SemaphoreType.DMA(()),
            pltpu.SemaphoreType.DMA((count,)),
            pltpu.SemaphoreType.DMA((count,)),
        ],
        compiler_params=pltpu.CompilerParams(collective_id=collective, has_side_effects=True),
    )(blocks)


def project_step(turned, x_ref, cos_ref, sin_ref, *refs):
    weights, out_ref = refs[:-1], refs[-1]
    widened = x_ref[...].astype(jnp.float32)
    centred = widened - jnp.mean(widened, axis=-1, keepdims=True)
    variance = jnp.mean(centred * centred, axis=-1, keepdims=True)
    normed = (centred * lax.rsqrt(variance + norm_eps)).astype(jnp.bfloat16)
    cosine = cos_ref[...]
    sine = sin_ref[...]
    for index, weight in enumerate(weights):
        width = weight.shape[1]
        product = jnp.dot(normed, weight[...], preferred_element_type=jnp.float32)
        if turned[index]:
            pieces = []
            for head in range(width // HEAD_DIM):
                part = product[:, head * HEAD_DIM : (head + 1) * HEAD_DIM]
                pieces.append(part * cosine + pltpu.roll(part, HEAD_DIM // 2, 1) * sine)
            product = jnp.concatenate(pieces, axis=1)
        out_ref[:, index * width : (index + 1) * width] = product.astype(out_ref.dtype)


def rope_tables(positions):
    half_dim = HEAD_DIM // 2
    frequency = jnp.exp(-jnp.log(rope_base) * jnp.arange(half_dim, dtype=jnp.float32) / half_dim)
    angles = positions.astype(jnp.float32)[:, None] * frequency[None, :]
    cosine = jnp.cos(angles)
    sine = jnp.sin(angles)
    return jnp.concatenate([cosine, cosine], axis=1), jnp.concatenate([-sine, sine], axis=1)


def project(rows, positions, weights, turned, block_rows):
    count, width = rows.shape
    cosine, sine = rope_tables(positions)
    out_width = sum(w.shape[1] for w in weights)
    return pl.pallas_call(
        functools.partial(project_step, tuple(turned)),
        grid=(count // block_rows,),
        in_specs=[
            pl.BlockSpec((block_rows, width), lambda i: (i, 0)),
            pl.BlockSpec((block_rows, HEAD_DIM), lambda i: (i, 0)),
            pl.BlockSpec((block_rows, HEAD_DIM), lambda i: (i, 0)),
        ]
        + [pl.BlockSpec(w.shape, lambda i: (0, 0)) for w in weights],
        out_specs=pl.BlockSpec((block_rows, out_width), lambda i: (i, 0)),
        out_shape=jax.ShapeDtypeStruct((count, out_width), jnp.bfloat16),
    )(rows, cosine, sine, *weights)


rope_base = 10000.0
norm_eps = 1e-05


def swapped(value, axis, apart):
    mask = 2**apart
    pairs = [(source, source ^ mask) for source in range(lax.axis_size(axis))]
    return lax.ppermute(value, axis, pairs)


def shards(
    tokens,
    w_query,
    w_key,
    w_value,
    w_out,
    own_cache,
    guest_cache,
    rec_hidden,
    deal_order,
    own_len,
    guest_len,
    rec_index,
):
    groups = lax.axis_size("grp")
    group_id = lax.axis_index("grp")
    partner_id = (group_id + groups // 2) % groups
    swap_bit = groups.bit_length() - 2
    local_width = w_query.shape[1]
    local_heads = local_width // HEAD_DIM
    requests, local_rows, model_width = tokens.shape

    fetched = swapped(guest_cache[0], "grp", swap_bit)

    server = jnp.zeros_like(deal_order).at[deal_order].set(jnp.arange(groups, dtype=jnp.int32))
    start_of = own_len[server] + guest_len[(server + groups // 2) % groups]
    local_positions = (
        start_of[:, None] + group_id * local_rows + jnp.arange(local_rows, dtype=jnp.int32)[None, :]
    ).reshape(-1)

    projected = project(
        tokens.reshape(-1, model_width), local_positions, [w_query, w_key, w_value],
        [True, True, False], 256,
    ).reshape(requests, local_rows, -1)
    arranged = jnp.take(projected, deal_order, axis=0)
    dealt = lax.all_to_all(arranged, "grp", split_axis=0, concat_axis=1, tiled=True)[0]
    span_len = dealt.shape[0]

    own_count = own_len[group_id]
    guest_count = guest_len[partner_id]
    rec_positions = rec_index[0]
    recomputed = project(rec_hidden[0], rec_positions, [w_key, w_value], [True, False], 256)
    replaced = jnp.zeros((own_cache.shape[2],), jnp.bool_).at[rec_positions].set(True)

    heads = local_heads
    chunks = 2
    piece = local_rows // chunks
    chunk_len = span_len // chunks
    order = dealt.reshape(groups, chunks, piece, -1).transpose(1, 0, 2, 3).reshape(span_len, -1)
    row_of = (
        jnp.arange(span_len, dtype=jnp.int32).reshape(groups, chunks, piece).transpose(1, 0, 2).reshape(-1)
    )
    rec_count = recomputed.shape[0]
    fresh = jnp.concatenate(
        [order[:, local_width:], recomputed], axis=0
    )
    fresh_rank = jnp.concatenate([row_of, jnp.full((rec_count,), -1, jnp.int32)])[None, :]
    fresh_count = span_len + rec_count
    never = jnp.int32(1 << 30)
    cap = own_cache.shape[2]
    block_len = 512
    key_rows = jnp.arange(cap, dtype=jnp.int32)
    own_rank = jnp.where((key_rows < own_count) & ~replaced, -1, never)[None, :]
    own_flags = (jnp.arange(cap // block_len, dtype=jnp.int32) * block_len < own_count).astype(jnp.int32)
    gcap = fetched.shape[1]
    guest_rows = jnp.arange(gcap, dtype=jnp.int32)
    guest_rank = jnp.where(guest_rows < guest_count, -1, never)[None, :]
    guest_flags = (jnp.arange(gcap // block_len, dtype=jnp.int32) * block_len < guest_count).astype(jnp.int32)
    blocks = lax.axis_size("tp")
    out_by_block = w_out.reshape(local_width, blocks, -1)

    returned = []
    for chunk in range(chunks):
        query_rows = row_of[chunk * chunk_len : (chunk + 1) * chunk_len][:, None]
        state = (
            jnp.full((chunk_len, local_width), FLOOR, jnp.float32),
            jnp.zeros((chunk_len, local_width), jnp.float32),
            jnp.zeros((chunk_len, local_width), jnp.float32),
        )
        state = attend(
            state, jnp.ones((2,), jnp.int32), query_rows, fresh_rank, order, chunk,
            fresh, lambda h, kb: (kb, h), fresh, lambda h, kb: (kb, heads + h),
            fresh_count, heads, fresh_count // 2,
        )
        state = attend(
            state, own_flags, query_rows, own_rank, order, chunk,
            own_cache[0], lambda h, kb: (0, kb, h), own_cache[0], lambda h, kb: (1, kb, h),
            cap, heads, block_len,
        )
        state = attend(
            state, guest_flags, query_rows, guest_rank, order, chunk,
            fetched, lambda h, kb: (0, kb, h), fetched, lambda h, kb: (1, kb, h),
            gcap, heads, block_len,
        )
        attended = (state[2] / state[1]).astype(jnp.bfloat16)
        partial_value = jnp.einsum(
            "qc,ctd->tqd", attended, out_by_block, preferred_element_type=jnp.float32
        ).astype(jnp.bfloat16)
        exchanged = lax.all_to_all(partial_value, "tp", split_axis=0, concat_axis=0, tiled=True)
        mixed_rows = exchanged.astype(jnp.float32).sum(axis=0).astype(jnp.bfloat16)
        returned.append(mixed_rows.reshape(groups, piece, -1))
    returned_rows = exchange(jnp.stack(returned, axis=1).reshape(groups, local_rows, -1), "grp", 1)
    return jnp.take(returned_rows, server, axis=0)


def solution(mesh):
    return jax.shard_map(
        shards,
        mesh=mesh,
        in_specs=(
            P(None, "grp", None),
            P(None, "tp"),
            P(None, "tp"),
            P(None, "tp"),
            P("tp", None),
            P("grp", None, None, "tp"),
            P("grp", None, None, "tp"),
            P("grp", None, None),
            P(),
            P(),
            P(),
            P("grp", None),
        ),
        out_specs=P(None, "grp", "tp"),
        check_vma=False,
    )
```

```python
import functools

import jax
import jax.numpy as jnp
from jax import lax
from jax.experimental import pallas as pl
from jax.experimental.pallas import tpu as pltpu
from jax.sharding import PartitionSpec as P

HEAD_DIM = 128


FLOOR = -1e30


def flash_step(flags_ref, qrow_ref, rank_ref, q_ref, k_ref, v_ref, m_in, l_in, acc_in, m_out, l_out, acc_out):
    kb = pl.program_id(1)

    @pl.when(kb == 0)
    def _():
        m_out[...] = m_in[...]
        l_out[...] = l_in[...]
        acc_out[...] = acc_in[...]

    @pl.when(flags_ref[kb] > 0)
    def _():
        scores = lax.dot_general(
            q_ref[...], k_ref[...], (((1,), (1,)), ((), ())), preferred_element_type=jnp.float32
        ) * (HEAD_DIM ** -0.5)
        scores = jnp.where(rank_ref[...] <= qrow_ref[...], scores, FLOOR)
        m_prev = m_out[...]
        m_new = jnp.maximum(m_prev, jnp.max(scores, axis=1, keepdims=True))
        factor = jnp.exp(m_prev - m_new)
        expanded = jnp.exp(scores - m_new[:, :1])
        l_out[...] = factor * l_out[...] + jnp.sum(expanded, axis=1, keepdims=True)
        acc_out[...] = factor * acc_out[...] + jnp.dot(
            expanded.astype(jnp.bfloat16), v_ref[...], preferred_element_type=jnp.float32
        )
        m_out[...] = m_new


def attend(state, flags, qrow, rank, q_src, q_block, k_src, k_map, v_src, v_map, key_count, heads, block_len):
    query_count = qrow.shape[0]
    state_spec = pl.BlockSpec((query_count, HEAD_DIM), lambda h, kb, f: (0, h))
    k_block = (block_len, HEAD_DIM) if k_src.ndim == 2 else (None, block_len, HEAD_DIM)
    v_block = (block_len, HEAD_DIM) if v_src.ndim == 2 else (None, block_len, HEAD_DIM)
    grid_spec = pltpu.PrefetchScalarGridSpec(
        num_scalar_prefetch=1,
        grid=(heads, key_count // block_len),
        in_specs=[
            pl.BlockSpec((query_count, 1), lambda h, kb, f: (0, 0)),
            pl.BlockSpec((1, block_len), lambda h, kb, f: (0, kb)),
            pl.BlockSpec((query_count, HEAD_DIM), lambda h, kb, f: (q_block, h)),
            pl.BlockSpec(k_block, lambda h, kb, f: k_map(h, kb)),
            pl.BlockSpec(v_block, lambda h, kb, f: v_map(h, kb)),
            state_spec,
            state_spec,
            state_spec,
        ],
        out_specs=[state_spec, state_spec, state_spec],
    )
    shape = jax.ShapeDtypeStruct(state[0].shape, jnp.float32)
    return pl.pallas_call(
        flash_step,
        grid_spec=grid_spec,
        out_shape=[shape, shape, shape],
        input_output_aliases={6: 0, 7: 1, 8: 2},
        compiler_params=pltpu.CompilerParams(dimension_semantics=("arbitrary", "arbitrary")),
    )(flags, qrow, rank, q_src, k_src, v_src, *state)


def exchange_step(axis, count, x_ref, y_ref, local_sem, send_sem, recv_sem):
    me = lax.axis_index(axis)
    barrier = pltpu.get_barrier_semaphore()
    for step in range(1, count):
        pl.semaphore_signal(
            barrier, inc=1, device_id={axis: lax.rem(me + step, count)},
            device_id_type=pl.DeviceIdType.MESH,
        )
    pl.semaphore_wait(barrier, count - 1)
    own = pltpu.make_async_copy(x_ref.at[me], y_ref.at[me], local_sem)
    own.start()
    sends = []
    for step in range(1, count):
        target = lax.rem(me + step, count)
        copy = pltpu.make_async_remote_copy(
            src_ref=x_ref.at[target],
            dst_ref=y_ref.at[me],
            send_sem=send_sem.at[step],
            recv_sem=recv_sem.at[me],
            device_id={axis: target},
            device_id_type=pl.DeviceIdType.MESH,
        )
        copy.start()
        sends.append(copy)
    for copy in sends:
        copy.wait_send()
    for step in range(1, count):
        source = lax.rem(me + count - step, count)
        pltpu.make_async_remote_copy(
            src_ref=x_ref.at[source],
            dst_ref=y_ref.at[source],
            send_sem=send_sem.at[step],
            recv_sem=recv_sem.at[source],
            device_id={axis: source},
            device_id_type=pl.DeviceIdType.MESH,
        ).wait_recv()
    own.wait()


def exchange(blocks, axis, collective):
    count = blocks.shape[0]
    return pl.pallas_call(
        functools.partial(exchange_step, axis, count),
        out_shape=jax.ShapeDtypeStruct(blocks.shape, blocks.dtype),
        in_specs=[pl.BlockSpec(memory_space=pl.ANY)],
        out_specs=pl.BlockSpec(memory_space=pl.ANY),
        scratch_shapes=[
            pltpu.SemaphoreType.DMA(()),
            pltpu.SemaphoreType.DMA((count,)),
            pltpu.SemaphoreType.DMA((count,)),
        ],
        compiler_params=pltpu.CompilerParams(collective_id=collective, has_side_effects=True),
    )(blocks)


def project_step(turned, x_ref, cos_ref, sin_ref, *refs):
    weights, out_ref = refs[:-1], refs[-1]
    widened = x_ref[...].astype(jnp.float32)
    centred = widened - jnp.mean(widened, axis=-1, keepdims=True)
    variance = jnp.mean(centred * centred, axis=-1, keepdims=True)
    normed = (centred * lax.rsqrt(variance + norm_eps)).astype(jnp.bfloat16)
    cosine = cos_ref[...]
    sine = sin_ref[...]
    for index, weight in enumerate(weights):
        width = weight.shape[1]
        product = jnp.dot(normed, weight[...], preferred_element_type=jnp.float32)
        if turned[index]:
            pieces = []
            for head in range(width // HEAD_DIM):
                part = product[:, head * HEAD_DIM : (head + 1) * HEAD_DIM]
                pieces.append(part * cosine + pltpu.roll(part, HEAD_DIM // 2, 1) * sine)
            product = jnp.concatenate(pieces, axis=1)
        out_ref[:, index * width : (index + 1) * width] = product.astype(out_ref.dtype)


def rope_tables(positions):
    half_dim = HEAD_DIM // 2
    frequency = jnp.exp(-jnp.log(rope_base) * jnp.arange(half_dim, dtype=jnp.float32) / half_dim)
    angles = positions.astype(jnp.float32)[:, None] * frequency[None, :]
    cosine = jnp.cos(angles)
    sine = jnp.sin(angles)
    return jnp.concatenate([cosine, cosine], axis=1), jnp.concatenate([-sine, sine], axis=1)


def project(rows, positions, weights, turned, block_rows):
    count, width = rows.shape
    cosine, sine = rope_tables(positions)
    out_width = sum(w.shape[1] for w in weights)
    return pl.pallas_call(
        functools.partial(project_step, tuple(turned)),
        grid=(count // block_rows,),
        in_specs=[
            pl.BlockSpec((block_rows, width), lambda i: (i, 0)),
            pl.BlockSpec((block_rows, HEAD_DIM), lambda i: (i, 0)),
            pl.BlockSpec((block_rows, HEAD_DIM), lambda i: (i, 0)),
        ]
        + [pl.BlockSpec(w.shape, lambda i: (0, 0)) for w in weights],
        out_specs=pl.BlockSpec((block_rows, out_width), lambda i: (i, 0)),
        out_shape=jax.ShapeDtypeStruct((count, out_width), jnp.bfloat16),
    )(rows, cosine, sine, *weights)


rope_base = 10000.0
norm_eps = 1e-05


def swapped(value, axis, apart):
    mask = 2**apart
    pairs = [(source, source ^ mask) for source in range(lax.axis_size(axis))]
    return lax.ppermute(value, axis, pairs)


def shards(
    tokens,
    w_query,
    w_key,
    w_value,
    w_out,
    own_cache,
    guest_cache,
    rec_hidden,
    deal_order,
    own_len,
    guest_len,
    rec_index,
):
    groups = lax.axis_size("grp")
    group_id = lax.axis_index("grp")
    partner_id = (group_id + groups // 2) % groups
    swap_bit = groups.bit_length() - 2
    local_width = w_query.shape[1]
    local_heads = local_width // HEAD_DIM
    requests, local_rows, model_width = tokens.shape

    fetched = swapped(guest_cache[0], "grp", swap_bit)

    server = jnp.zeros_like(deal_order).at[deal_order].set(jnp.arange(groups, dtype=jnp.int32))
    start_of = own_len[server] + guest_len[(server + groups // 2) % groups]
    local_positions = (
        start_of[:, None] + group_id * local_rows + jnp.arange(local_rows, dtype=jnp.int32)[None, :]
    ).reshape(-1)

    projected = project(
        tokens.reshape(-1, model_width), local_positions, [w_query, w_key, w_value],
        [True, True, False], 256,
    ).reshape(requests, local_rows, -1)
    arranged = jnp.take(projected, deal_order, axis=0)
    dealt = lax.all_to_all(arranged, "grp", split_axis=0, concat_axis=1, tiled=True)[0]
    span_len = dealt.shape[0]

    own_count = own_len[group_id]
    guest_count = guest_len[partner_id]
    rec_positions = rec_index[0]
    recomputed = project(rec_hidden[0], rec_positions, [w_key, w_value], [True, False], 256)
    replaced = jnp.zeros((own_cache.shape[2],), jnp.bool_).at[rec_positions].set(True)

    heads = local_heads
    chunks = 2
    piece = local_rows // chunks
    chunk_len = span_len // chunks
    order = dealt.reshape(groups, chunks, piece, -1).transpose(1, 0, 2, 3).reshape(span_len, -1)
    row_of = (
        jnp.arange(span_len, dtype=jnp.int32).reshape(groups, chunks, piece).transpose(1, 0, 2).reshape(-1)
    )
    rec_count = recomputed.shape[0]
    fresh = jnp.concatenate(
        [order[:, local_width:], recomputed], axis=0
    )
    fresh_rank = jnp.concatenate([row_of, jnp.full((rec_count,), -1, jnp.int32)])[None, :]
    fresh_count = span_len + rec_count
    never = jnp.int32(1 << 30)
    cap = own_cache.shape[2]
    block_len = 512
    key_rows = jnp.arange(cap, dtype=jnp.int32)
    own_rank = jnp.where((key_rows < own_count) & ~replaced, -1, never)[None, :]
    own_flags = (jnp.arange(cap // block_len, dtype=jnp.int32) * block_len < own_count).astype(jnp.int32)
    gcap = fetched.shape[1]
    guest_rows = jnp.arange(gcap, dtype=jnp.int32)
    guest_rank = jnp.where(guest_rows < guest_count, -1, never)[None, :]
    guest_flags = (jnp.arange(gcap // block_len, dtype=jnp.int32) * block_len < guest_count).astype(jnp.int32)
    blocks = lax.axis_size("tp")
    out_by_block = w_out.reshape(local_width, blocks, -1)

    returned = []
    exchanged = []
    for chunk in range(chunks):
        query_rows = row_of[chunk * chunk_len : (chunk + 1) * chunk_len][:, None]
        state = (
            jnp.full((chunk_len, local_width), FLOOR, jnp.float32),
            jnp.zeros((chunk_len, local_width), jnp.float32),
            jnp.zeros((chunk_len, local_width), jnp.float32),
        )
        state = attend(
            state, jnp.ones((2,), jnp.int32), query_rows, fresh_rank, order, chunk,
            fresh, lambda h, kb: (kb, h), fresh, lambda h, kb: (kb, heads + h),
            fresh_count, heads, fresh_count // 2,
        )
        state = attend(
            state, own_flags, query_rows, own_rank, order, chunk,
            own_cache[0], lambda h, kb: (0, kb, h), own_cache[0], lambda h, kb: (1, kb, h),
            cap, heads, block_len,
        )
        state = attend(
            state, guest_flags, query_rows, guest_rank, order, chunk,
            fetched, lambda h, kb: (0, kb, h), fetched, lambda h, kb: (1, kb, h),
            gcap, heads, block_len,
        )
        attended = (state[2] / state[1]).astype(jnp.bfloat16)
        partial_value = jnp.einsum(
            "qc,ctd->tqd", attended, out_by_block, preferred_element_type=jnp.float32
        ).astype(jnp.bfloat16)
        exchanged.append(
            lax.all_to_all(partial_value, "tp", split_axis=0, concat_axis=0, tiled=True)
        )
    for chunk in range(chunks):
        mixed_rows = exchanged[chunk].astype(jnp.float32).sum(axis=0).astype(jnp.bfloat16)
        returned.append(exchange(mixed_rows.reshape(groups, piece, -1), "grp", 1 + chunk))
    returned_rows = jnp.stack(returned, axis=1).reshape(groups, local_rows, -1)
    return jnp.take(returned_rows, server, axis=0)


def solution(mesh):
    return jax.shard_map(
        shards,
        mesh=mesh,
        in_specs=(
            P(None, "grp", None),
            P(None, "tp"),
            P(None, "tp"),
            P(None, "tp"),
            P("tp", None),
            P("grp", None, None, "tp"),
            P("grp", None, None, "tp"),
            P("grp", None, None),
            P(),
            P(),
            P(),
            P("grp", None),
        ),
        out_specs=P(None, "grp", "tp"),
        check_vma=False,
    )
```

```python
import functools

import jax
import jax.numpy as jnp
from jax import lax
from jax.experimental import pallas as pl
from jax.experimental.pallas import tpu as pltpu
from jax.sharding import PartitionSpec as P

HEAD_DIM = 128


FLOOR = -1e30


def flash_step(flags_ref, qrow_ref, rank_ref, q_ref, k_ref, v_ref, m_in, l_in, acc_in, m_out, l_out, acc_out):
    kb = pl.program_id(1)

    @pl.when(kb == 0)
    def _():
        m_out[...] = m_in[...]
        l_out[...] = l_in[...]
        acc_out[...] = acc_in[...]

    @pl.when(flags_ref[kb] > 0)
    def _():
        scores = lax.dot_general(
            q_ref[...], k_ref[...], (((1,), (1,)), ((), ())), preferred_element_type=jnp.float32
        ) * (HEAD_DIM ** -0.5)
        scores = jnp.where(rank_ref[...] <= qrow_ref[...], scores, FLOOR)
        m_prev = m_out[...]
        m_new = jnp.maximum(m_prev, jnp.max(scores, axis=1, keepdims=True))
        factor = jnp.exp(m_prev - m_new)
        expanded = jnp.exp(scores - m_new[:, :1])
        l_out[...] = factor * l_out[...] + jnp.sum(expanded, axis=1, keepdims=True)
        acc_out[...] = factor * acc_out[...] + jnp.dot(
            expanded.astype(jnp.bfloat16), v_ref[...], preferred_element_type=jnp.float32
        )
        m_out[...] = m_new


def attend(state, flags, qrow, rank, q_src, q_block, k_src, k_map, v_src, v_map, key_count, heads, block_len):
    query_count = qrow.shape[0]
    state_spec = pl.BlockSpec((query_count, HEAD_DIM), lambda h, kb, f: (0, h))
    k_block = (block_len, HEAD_DIM) if k_src.ndim == 2 else (None, block_len, HEAD_DIM)
    v_block = (block_len, HEAD_DIM) if v_src.ndim == 2 else (None, block_len, HEAD_DIM)
    grid_spec = pltpu.PrefetchScalarGridSpec(
        num_scalar_prefetch=1,
        grid=(heads, key_count // block_len),
        in_specs=[
            pl.BlockSpec((query_count, 1), lambda h, kb, f: (0, 0)),
            pl.BlockSpec((1, block_len), lambda h, kb, f: (0, kb)),
            pl.BlockSpec((query_count, HEAD_DIM), lambda h, kb, f: (q_block, h)),
            pl.BlockSpec(k_block, lambda h, kb, f: k_map(h, kb)),
            pl.BlockSpec(v_block, lambda h, kb, f: v_map(h, kb)),
            state_spec,
            state_spec,
            state_spec,
        ],
        out_specs=[state_spec, state_spec, state_spec],
    )
    shape = jax.ShapeDtypeStruct(state[0].shape, jnp.float32)
    return pl.pallas_call(
        flash_step,
        grid_spec=grid_spec,
        out_shape=[shape, shape, shape],
        input_output_aliases={6: 0, 7: 1, 8: 2},
        compiler_params=pltpu.CompilerParams(dimension_semantics=("arbitrary", "arbitrary")),
    )(flags, qrow, rank, q_src, k_src, v_src, *state)


def exchange_step(axis, count, x_ref, y_ref, local_sem, send_sem, recv_sem):
    me = lax.axis_index(axis)
    barrier = pltpu.get_barrier_semaphore()
    for step in range(1, count):
        pl.semaphore_signal(
            barrier, inc=1, device_id={axis: lax.rem(me + step, count)},
            device_id_type=pl.DeviceIdType.MESH,
        )
    pl.semaphore_wait(barrier, count - 1)
    own = pltpu.make_async_copy(x_ref.at[me], y_ref.at[me], local_sem)
    own.start()
    sends = []
    for step in range(1, count):
        target = lax.rem(me + step, count)
        copy = pltpu.make_async_remote_copy(
            src_ref=x_ref.at[target],
            dst_ref=y_ref.at[me],
            send_sem=send_sem.at[step],
            recv_sem=recv_sem.at[me],
            device_id={axis: target},
            device_id_type=pl.DeviceIdType.MESH,
        )
        copy.start()
        sends.append(copy)
    for copy in sends:
        copy.wait_send()
    for step in range(1, count):
        source = lax.rem(me + count - step, count)
        pltpu.make_async_remote_copy(
            src_ref=x_ref.at[source],
            dst_ref=y_ref.at[source],
            send_sem=send_sem.at[step],
            recv_sem=recv_sem.at[source],
            device_id={axis: source},
            device_id_type=pl.DeviceIdType.MESH,
        ).wait_recv()
    own.wait()


def exchange(blocks, axis, collective):
    count = blocks.shape[0]
    return pl.pallas_call(
        functools.partial(exchange_step, axis, count),
        out_shape=jax.ShapeDtypeStruct(blocks.shape, blocks.dtype),
        in_specs=[pl.BlockSpec(memory_space=pl.ANY)],
        out_specs=pl.BlockSpec(memory_space=pl.ANY),
        scratch_shapes=[
            pltpu.SemaphoreType.DMA(()),
            pltpu.SemaphoreType.DMA((count,)),
            pltpu.SemaphoreType.DMA((count,)),
        ],
        compiler_params=pltpu.CompilerParams(collective_id=collective, has_side_effects=True),
    )(blocks)


def project_step(turned, x_ref, cos_ref, sin_ref, *refs):
    weights, out_ref = refs[:-1], refs[-1]
    widened = x_ref[...].astype(jnp.float32)
    centred = widened - jnp.mean(widened, axis=-1, keepdims=True)
    variance = jnp.mean(centred * centred, axis=-1, keepdims=True)
    normed = (centred * lax.rsqrt(variance + norm_eps)).astype(jnp.bfloat16)
    cosine = cos_ref[...]
    sine = sin_ref[...]
    for index, weight in enumerate(weights):
        width = weight.shape[1]
        product = jnp.dot(normed, weight[...], preferred_element_type=jnp.float32)
        if turned[index]:
            pieces = []
            for head in range(width // HEAD_DIM):
                part = product[:, head * HEAD_DIM : (head + 1) * HEAD_DIM]
                pieces.append(part * cosine + pltpu.roll(part, HEAD_DIM // 2, 1) * sine)
            product = jnp.concatenate(pieces, axis=1)
        out_ref[:, index * width : (index + 1) * width] = product.astype(out_ref.dtype)


def rope_tables(positions):
    half_dim = HEAD_DIM // 2
    frequency = jnp.exp(-jnp.log(rope_base) * jnp.arange(half_dim, dtype=jnp.float32) / half_dim)
    angles = positions.astype(jnp.float32)[:, None] * frequency[None, :]
    cosine = jnp.cos(angles)
    sine = jnp.sin(angles)
    return jnp.concatenate([cosine, cosine], axis=1), jnp.concatenate([-sine, sine], axis=1)


def project(rows, positions, weights, turned, block_rows):
    count, width = rows.shape
    cosine, sine = rope_tables(positions)
    out_width = sum(w.shape[1] for w in weights)
    return pl.pallas_call(
        functools.partial(project_step, tuple(turned)),
        grid=(count // block_rows,),
        in_specs=[
            pl.BlockSpec((block_rows, width), lambda i: (i, 0)),
            pl.BlockSpec((block_rows, HEAD_DIM), lambda i: (i, 0)),
            pl.BlockSpec((block_rows, HEAD_DIM), lambda i: (i, 0)),
        ]
        + [pl.BlockSpec(w.shape, lambda i: (0, 0)) for w in weights],
        out_specs=pl.BlockSpec((block_rows, out_width), lambda i: (i, 0)),
        out_shape=jax.ShapeDtypeStruct((count, out_width), jnp.bfloat16),
    )(rows, cosine, sine, *weights)


rope_base = 10000.0
norm_eps = 1e-05


def swapped(value, axis, apart):
    mask = 2**apart
    pairs = [(source, source ^ mask) for source in range(lax.axis_size(axis))]
    return lax.ppermute(value, axis, pairs)


def shards(
    tokens,
    w_query,
    w_key,
    w_value,
    w_out,
    own_cache,
    guest_cache,
    rec_hidden,
    deal_order,
    own_len,
    guest_len,
    rec_index,
):
    groups = lax.axis_size("grp")
    group_id = lax.axis_index("grp")
    partner_id = (group_id + groups // 2) % groups
    swap_bit = groups.bit_length() - 2
    local_width = w_query.shape[1]
    local_heads = local_width // HEAD_DIM
    requests, local_rows, model_width = tokens.shape

    fetched = swapped(guest_cache[0], "grp", swap_bit)

    server = jnp.zeros_like(deal_order).at[deal_order].set(jnp.arange(groups, dtype=jnp.int32))
    start_of = own_len[server] + guest_len[(server + groups // 2) % groups]
    local_positions = (
        start_of[:, None] + group_id * local_rows + jnp.arange(local_rows, dtype=jnp.int32)[None, :]
    ).reshape(-1)

    projected = project(
        tokens.reshape(-1, model_width), local_positions, [w_query, w_key, w_value],
        [True, True, False], 256,
    ).reshape(requests, local_rows, -1)
    arranged = jnp.take(projected, deal_order, axis=0)
    dealt = lax.all_to_all(arranged, "grp", split_axis=0, concat_axis=1, tiled=True)[0]
    span_len = dealt.shape[0]

    own_count = own_len[group_id]
    guest_count = guest_len[partner_id]
    rec_positions = rec_index[0]
    recomputed = project(rec_hidden[0], rec_positions, [w_key, w_value], [True, False], 256)
    replaced = jnp.zeros((own_cache.shape[2],), jnp.bool_).at[rec_positions].set(True)

    heads = local_heads
    chunks = 2
    piece = local_rows // chunks
    chunk_len = span_len // chunks
    order = dealt.reshape(groups, chunks, piece, -1).transpose(1, 0, 2, 3).reshape(span_len, -1)
    row_of = (
        jnp.arange(span_len, dtype=jnp.int32).reshape(groups, chunks, piece).transpose(1, 0, 2).reshape(-1)
    )
    rec_count = recomputed.shape[0]
    fresh = jnp.concatenate(
        [order[:, local_width:], recomputed], axis=0
    )
    fresh_rank = jnp.concatenate([row_of, jnp.full((rec_count,), -1, jnp.int32)])[None, :]
    fresh_count = span_len + rec_count
    never = jnp.int32(1 << 30)
    cap = own_cache.shape[2]
    block_len = 1024
    key_rows = jnp.arange(cap, dtype=jnp.int32)
    own_rank = jnp.where((key_rows < own_count) & ~replaced, -1, never)[None, :]
    own_flags = (jnp.arange(cap // block_len, dtype=jnp.int32) * block_len < own_count).astype(jnp.int32)
    gcap = fetched.shape[1]
    guest_rows = jnp.arange(gcap, dtype=jnp.int32)
    guest_rank = jnp.where(guest_rows < guest_count, -1, never)[None, :]
    guest_flags = (jnp.arange(gcap // block_len, dtype=jnp.int32) * block_len < guest_count).astype(jnp.int32)
    blocks = lax.axis_size("tp")
    out_by_block = w_out.reshape(local_width, blocks, -1)

    returned = []
    exchanged = []
    for chunk in range(chunks):
        query_rows = row_of[chunk * chunk_len : (chunk + 1) * chunk_len][:, None]
        state = (
            jnp.full((chunk_len, local_width), FLOOR, jnp.float32),
            jnp.zeros((chunk_len, local_width), jnp.float32),
            jnp.zeros((chunk_len, local_width), jnp.float32),
        )
        state = attend(
            state, jnp.ones((1,), jnp.int32), query_rows, fresh_rank, order, chunk,
            fresh, lambda h, kb: (kb, h), fresh, lambda h, kb: (kb, heads + h),
            fresh_count, heads, fresh_count,
        )
        state = attend(
            state, own_flags, query_rows, own_rank, order, chunk,
            own_cache[0], lambda h, kb: (0, kb, h), own_cache[0], lambda h, kb: (1, kb, h),
            cap, heads, block_len,
        )
        state = attend(
            state, guest_flags, query_rows, guest_rank, order, chunk,
            fetched, lambda h, kb: (0, kb, h), fetched, lambda h, kb: (1, kb, h),
            gcap, heads, block_len,
        )
        attended = (state[2] / state[1]).astype(jnp.bfloat16)
        partial_value = jnp.einsum(
            "qc,ctd->tqd", attended, out_by_block, preferred_element_type=jnp.float32
        ).astype(jnp.bfloat16)
        exchanged.append(
            lax.all_to_all(partial_value, "tp", split_axis=0, concat_axis=0, tiled=True)
        )
    for chunk in range(chunks):
        mixed_rows = exchanged[chunk].astype(jnp.float32).sum(axis=0).astype(jnp.bfloat16)
        returned.append(exchange(mixed_rows.reshape(groups, piece, -1), "grp", 1 + chunk))
    returned_rows = jnp.stack(returned, axis=1).reshape(groups, local_rows, -1)
    return jnp.take(returned_rows, server, axis=0)


def solution(mesh):
    return jax.shard_map(
        shards,
        mesh=mesh,
        in_specs=(
            P(None, "grp", None),
            P(None, "tp"),
            P(None, "tp"),
            P(None, "tp"),
            P("tp", None),
            P("grp", None, None, "tp"),
            P("grp", None, None, "tp"),
            P("grp", None, None),
            P(),
            P(),
            P(),
            P("grp", None),
        ),
        out_specs=P(None, "grp", "tp"),
        check_vma=False,
    )
```

```python
import functools

import jax
import jax.numpy as jnp
from jax import lax
from jax.experimental import pallas as pl
from jax.experimental.pallas import tpu as pltpu
from jax.sharding import PartitionSpec as P

HEAD_DIM = 128


FLOOR = -1e30


def flash_head(masked, head, qrow_ref, rank_ref, q_ref, k_ref, v_ref, m_out, l_out, acc_out):
    lanes = pl.ds(head * HEAD_DIM, HEAD_DIM)
    scores = lax.dot_general(
        q_ref[:, lanes], k_ref[:, lanes], (((1,), (1,)), ((), ())), preferred_element_type=jnp.float32
    ) * (HEAD_DIM ** -0.5)
    if masked:
        scores = jnp.where(rank_ref[...] <= qrow_ref[...], scores, FLOOR)
    m_prev = m_out[:, lanes]
    m_new = jnp.maximum(m_prev, jnp.max(scores, axis=1, keepdims=True))
    factor = jnp.exp(m_prev - m_new)
    expanded = jnp.exp(scores - m_new[:, :1])
    l_out[:, lanes] = factor * l_out[:, lanes] + jnp.sum(expanded, axis=1, keepdims=True)
    acc_out[:, lanes] = factor * acc_out[:, lanes] + jnp.dot(
        expanded.astype(jnp.bfloat16), v_ref[:, lanes], preferred_element_type=jnp.float32
    )
    m_out[:, lanes] = m_new


def flash_step(heads, flags_ref, qrow_ref, rank_ref, q_ref, k_ref, v_ref, m_in, l_in, acc_in, m_out, l_out, acc_out):
    kb = pl.program_id(0)

    @pl.when(kb == 0)
    def _():
        m_out[...] = m_in[...]
        l_out[...] = l_in[...]
        acc_out[...] = acc_in[...]

    refs = (qrow_ref, rank_ref, q_ref, k_ref, v_ref, m_out, l_out, acc_out)
    for masked, flag in ((True, 1), (False, 2)):
        @pl.when(flags_ref[kb] == flag)
        def _():
            for head in range(heads):
                flash_head(masked, head, *refs)


def attend(state, flags, qrow, rank, q_src, q_block, k_src, k_map, v_src, v_map, key_count, heads, block_len):
    query_count = qrow.shape[0]
    width = heads * HEAD_DIM
    state_spec = pl.BlockSpec((query_count, width), lambda kb, f: (0, 0))
    k_block = (block_len, width) if k_src.ndim == 2 else (None, block_len, width)
    v_block = (block_len, width) if v_src.ndim == 2 else (None, block_len, width)
    grid_spec = pltpu.PrefetchScalarGridSpec(
        num_scalar_prefetch=1,
        grid=(key_count // block_len,),
        in_specs=[
            pl.BlockSpec((query_count, 1), lambda kb, f: (0, 0)),
            pl.BlockSpec((1, block_len), lambda kb, f: (0, kb)),
            pl.BlockSpec((query_count, width), lambda kb, f: (q_block, 0)),
            pl.BlockSpec(k_block, lambda kb, f: k_map(kb)),
            pl.BlockSpec(v_block, lambda kb, f: v_map(kb)),
            state_spec,
            state_spec,
            state_spec,
        ],
        out_specs=[state_spec, state_spec, state_spec],
    )
    shape = jax.ShapeDtypeStruct(state[0].shape, jnp.float32)
    return pl.pallas_call(
        functools.partial(flash_step, heads),
        grid_spec=grid_spec,
        out_shape=[shape, shape, shape],
        input_output_aliases={6: 0, 7: 1, 8: 2},
        cost_estimate=pl.CostEstimate(
            flops=4 * query_count * key_count * HEAD_DIM * heads,
            transcendentals=query_count * key_count * heads,
            bytes_accessed=4 * key_count * HEAD_DIM * heads + 24 * query_count * HEAD_DIM * heads,
        ),
        compiler_params=pltpu.CompilerParams(dimension_semantics=("arbitrary",)),
    )(flags, qrow, rank, q_src, k_src, v_src, *state)


def exchange_step(axis, count, x_ref, y_ref, local_sem, send_sem, recv_sem):
    me = lax.axis_index(axis)
    barrier = pltpu.get_barrier_semaphore()
    for step in range(1, count):
        pl.semaphore_signal(
            barrier, inc=1, device_id={axis: lax.rem(me + step, count)},
            device_id_type=pl.DeviceIdType.MESH,
        )
    pl.semaphore_wait(barrier, count - 1)
    own = pltpu.make_async_copy(x_ref.at[me], y_ref.at[me], local_sem)
    own.start()
    sends = []
    for step in range(1, count):
        target = lax.rem(me + step, count)
        copy = pltpu.make_async_remote_copy(
            src_ref=x_ref.at[target],
            dst_ref=y_ref.at[me],
            send_sem=send_sem.at[step],
            recv_sem=recv_sem.at[me],
            device_id={axis: target},
            device_id_type=pl.DeviceIdType.MESH,
        )
        copy.start()
        sends.append(copy)
    for copy in sends:
        copy.wait_send()
    for step in range(1, count):
        source = lax.rem(me + count - step, count)
        pltpu.make_async_remote_copy(
            src_ref=x_ref.at[source],
            dst_ref=y_ref.at[source],
            send_sem=send_sem.at[step],
            recv_sem=recv_sem.at[source],
            device_id={axis: source},
            device_id_type=pl.DeviceIdType.MESH,
        ).wait_recv()
    own.wait()


def exchange(blocks, axis, collective):
    count = blocks.shape[0]
    return pl.pallas_call(
        functools.partial(exchange_step, axis, count),
        out_shape=jax.ShapeDtypeStruct(blocks.shape, blocks.dtype),
        in_specs=[pl.BlockSpec(memory_space=pl.ANY)],
        out_specs=pl.BlockSpec(memory_space=pl.ANY),
        scratch_shapes=[
            pltpu.SemaphoreType.DMA(()),
            pltpu.SemaphoreType.DMA((count,)),
            pltpu.SemaphoreType.DMA((count,)),
        ],
        compiler_params=pltpu.CompilerParams(collective_id=collective, has_side_effects=True),
    )(blocks)


def project_step(turned, x_ref, cos_ref, sin_ref, *refs):
    weights, out_ref = refs[:-1], refs[-1]
    widened = x_ref[...].astype(jnp.float32)
    centred = widened - jnp.mean(widened, axis=-1, keepdims=True)
    variance = jnp.mean(centred * centred, axis=-1, keepdims=True)
    normed = (centred * lax.rsqrt(variance + norm_eps)).astype(jnp.bfloat16)
    cosine = cos_ref[...]
    sine = sin_ref[...]
    for index, weight in enumerate(weights):
        width = weight.shape[1]
        product = jnp.dot(normed, weight[...], preferred_element_type=jnp.float32)
        if turned[index]:
            pieces = []
            for head in range(width // HEAD_DIM):
                part = product[:, head * HEAD_DIM : (head + 1) * HEAD_DIM]
                pieces.append(part * cosine + pltpu.roll(part, HEAD_DIM // 2, 1) * sine)
            product = jnp.concatenate(pieces, axis=1)
        out_ref[:, index * width : (index + 1) * width] = product.astype(out_ref.dtype)


def rope_tables(positions):
    half_dim = HEAD_DIM // 2
    frequency = jnp.exp(-jnp.log(rope_base) * jnp.arange(half_dim, dtype=jnp.float32) / half_dim)
    angles = positions.astype(jnp.float32)[:, None] * frequency[None, :]
    cosine = jnp.cos(angles)
    sine = jnp.sin(angles)
    return jnp.concatenate([cosine, cosine], axis=1), jnp.concatenate([-sine, sine], axis=1)


def project(rows, positions, weights, turned, block_rows):
    count, width = rows.shape
    cosine, sine = rope_tables(positions)
    out_width = sum(w.shape[1] for w in weights)
    return pl.pallas_call(
        functools.partial(project_step, tuple(turned)),
        grid=(count // block_rows,),
        in_specs=[
            pl.BlockSpec((block_rows, width), lambda i: (i, 0)),
            pl.BlockSpec((block_rows, HEAD_DIM), lambda i: (i, 0)),
            pl.BlockSpec((block_rows, HEAD_DIM), lambda i: (i, 0)),
        ]
        + [pl.BlockSpec(w.shape, lambda i: (0, 0)) for w in weights],
        out_specs=pl.BlockSpec((block_rows, out_width), lambda i: (i, 0)),
        out_shape=jax.ShapeDtypeStruct((count, out_width), jnp.bfloat16),
        cost_estimate=pl.CostEstimate(
            flops=2 * count * width * out_width,
            transcendentals=count,
            bytes_accessed=2 * count * (width + out_width) + 2 * width * out_width,
        ),
    )(rows, cosine, sine, *weights)


rope_base = 10000.0
norm_eps = 1e-05


def swapped(value, axis, apart):
    mask = 2**apart
    pairs = [(source, source ^ mask) for source in range(lax.axis_size(axis))]
    return lax.ppermute(value, axis, pairs)


def shards(
    tokens,
    w_query,
    w_key,
    w_value,
    w_out,
    own_cache,
    guest_cache,
    rec_hidden,
    deal_order,
    own_len,
    guest_len,
    rec_index,
):
    groups = lax.axis_size("grp")
    group_id = lax.axis_index("grp")
    partner_id = (group_id + groups // 2) % groups
    swap_bit = groups.bit_length() - 2
    local_width = w_query.shape[1]
    local_heads = local_width // HEAD_DIM
    requests, local_rows, model_width = tokens.shape

    fetched = swapped(guest_cache[0], "grp", swap_bit)

    server = jnp.zeros_like(deal_order).at[deal_order].set(jnp.arange(groups, dtype=jnp.int32))
    start_of = own_len[server] + guest_len[(server + groups // 2) % groups]
    local_positions = (
        start_of[:, None] + group_id * local_rows + jnp.arange(local_rows, dtype=jnp.int32)[None, :]
    ).reshape(-1)

    projected = project(
        tokens.reshape(-1, model_width), local_positions, [w_query, w_key, w_value],
        [True, True, False], 256,
    ).reshape(requests, local_rows, -1)
    arranged = jnp.take(projected, deal_order, axis=0)
    dealt = lax.all_to_all(arranged, "grp", split_axis=0, concat_axis=1, tiled=True)[0]
    span_len = dealt.shape[0]

    own_count = own_len[group_id]
    guest_count = guest_len[partner_id]
    rec_positions = rec_index[0]
    recomputed = project(rec_hidden[0], rec_positions, [w_key, w_value], [True, False], 256)
    replaced = jnp.zeros((own_cache.shape[2],), jnp.bool_).at[rec_positions].set(True)

    heads = local_heads
    chunks = 2
    piece = local_rows // chunks
    chunk_len = span_len // chunks
    order = dealt.reshape(groups, chunks, piece, -1).transpose(1, 0, 2, 3).reshape(span_len, -1)
    row_of = (
        jnp.arange(span_len, dtype=jnp.int32).reshape(groups, chunks, piece).transpose(1, 0, 2).reshape(-1)
    )
    rec_count = recomputed.shape[0]
    fresh = jnp.concatenate(
        [order[:, local_width:], recomputed], axis=0
    )
    fresh_rank = jnp.concatenate([row_of, jnp.full((rec_count,), -1, jnp.int32)])[None, :]
    fresh_count = span_len + rec_count
    never = jnp.int32(1 << 30)
    cap = own_cache.shape[2]
    block_len = 1024
    key_rows = jnp.arange(cap, dtype=jnp.int32)
    own_rank = jnp.where((key_rows < own_count) & ~replaced, -1, never)[None, :]
    own_flags = (jnp.arange(cap // block_len, dtype=jnp.int32) * block_len < own_count).astype(jnp.int32)
    gcap = fetched.shape[1]
    guest_rows = jnp.arange(gcap, dtype=jnp.int32)
    guest_rank = jnp.where(guest_rows < guest_count, -1, never)[None, :]
    guest_starts = jnp.arange(gcap // block_len, dtype=jnp.int32) * block_len
    guest_flags = (guest_starts < guest_count).astype(jnp.int32) + (
        guest_starts + block_len <= guest_count
    ).astype(jnp.int32)
    blocks = lax.axis_size("tp")
    out_by_block = w_out.reshape(local_width, blocks, -1)

    returned = []
    exchanged = []
    for chunk in range(chunks):
        query_rows = row_of[chunk * chunk_len : (chunk + 1) * chunk_len][:, None]
        state = (
            jnp.full((chunk_len, local_width), FLOOR, jnp.float32),
            jnp.zeros((chunk_len, local_width), jnp.float32),
            jnp.zeros((chunk_len, local_width), jnp.float32),
        )
        state = attend(
            state, jnp.ones((1,), jnp.int32), query_rows, fresh_rank, order, chunk,
            fresh, lambda kb: (kb, 0), fresh, lambda kb: (kb, 1),
            fresh_count, heads, fresh_count,
        )
        state = attend(
            state, own_flags, query_rows, own_rank, order, chunk,
            own_cache[0], lambda kb: (0, kb, 0), own_cache[0], lambda kb: (1, kb, 0),
            cap, heads, block_len,
        )
        state = attend(
            state, guest_flags, query_rows, guest_rank, order, chunk,
            fetched, lambda kb: (0, kb, 0), fetched, lambda kb: (1, kb, 0),
            gcap, heads, block_len,
        )
        attended = (state[2] / state[1]).astype(jnp.bfloat16)
        partial_value = jnp.einsum(
            "qc,ctd->tqd", attended, out_by_block, preferred_element_type=jnp.float32
        ).astype(jnp.bfloat16)
        exchanged.append(
            lax.all_to_all(partial_value, "tp", split_axis=0, concat_axis=0, tiled=True)
        )
    for chunk in range(chunks):
        mixed_rows = exchanged[chunk].astype(jnp.float32).sum(axis=0).astype(jnp.bfloat16)
        returned.append(exchange(mixed_rows.reshape(groups, piece, -1), "grp", 1 + chunk))
    returned_rows = jnp.stack(returned, axis=1).reshape(groups, local_rows, -1)
    return jnp.take(returned_rows, server, axis=0)


def solution(mesh):
    return jax.shard_map(
        shards,
        mesh=mesh,
        in_specs=(
            P(None, "grp", None),
            P(None, "tp"),
            P(None, "tp"),
            P(None, "tp"),
            P("tp", None),
            P("grp", None, None, "tp"),
            P("grp", None, None, "tp"),
            P("grp", None, None),
            P(),
            P(),
            P(),
            P("grp", None),
        ),
        out_specs=P(None, "grp", "tp"),
        check_vma=False,
    )
```

```python
import functools

import jax
import jax.numpy as jnp
from jax import lax
from jax.experimental import pallas as pl
from jax.experimental.pallas import tpu as pltpu
from jax.sharding import PartitionSpec as P

HEAD_DIM = 128


FLOOR = -1e30


def flash_step(flags_ref, qrow_ref, rank_ref, q_ref, k_ref, v_ref, m_in, l_in, acc_in, m_out, l_out, acc_out):
    kb = pl.program_id(1)

    @pl.when(kb == 0)
    def _():
        m_out[...] = m_in[...]
        l_out[...] = l_in[...]
        acc_out[...] = acc_in[...]

    @pl.when(flags_ref[kb] > 0)
    def _():
        scores = lax.dot_general(
            q_ref[...], k_ref[...], (((1,), (1,)), ((), ())), preferred_element_type=jnp.float32
        ) * (HEAD_DIM ** -0.5)
        scores = jnp.where(rank_ref[...] <= qrow_ref[...], scores, FLOOR)
        m_prev = m_out[...]
        m_new = jnp.maximum(m_prev, jnp.max(scores, axis=1, keepdims=True))
        factor = jnp.exp(m_prev - m_new)
        expanded = jnp.exp(scores - m_new[:, :1])
        l_out[...] = factor * l_out[...] + jnp.sum(expanded, axis=1, keepdims=True)
        acc_out[...] = factor * acc_out[...] + jnp.dot(
            expanded.astype(jnp.bfloat16), v_ref[...], preferred_element_type=jnp.float32
        )
        m_out[...] = m_new


def attend(state, flags, qrow, rank, q_src, q_block, k_src, k_map, v_src, v_map, key_count, heads, block_len):
    query_count = qrow.shape[0]
    state_spec = pl.BlockSpec((query_count, HEAD_DIM), lambda h, kb, f: (0, h))
    k_block = (block_len, HEAD_DIM) if k_src.ndim == 2 else (None, block_len, HEAD_DIM)
    v_block = (block_len, HEAD_DIM) if v_src.ndim == 2 else (None, block_len, HEAD_DIM)
    grid_spec = pltpu.PrefetchScalarGridSpec(
        num_scalar_prefetch=1,
        grid=(heads, key_count // block_len),
        in_specs=[
            pl.BlockSpec((query_count, 1), lambda h, kb, f: (0, 0)),
            pl.BlockSpec((1, block_len), lambda h, kb, f: (0, kb)),
            pl.BlockSpec((query_count, HEAD_DIM), lambda h, kb, f: (q_block, h)),
            pl.BlockSpec(k_block, lambda h, kb, f: k_map(h, kb)),
            pl.BlockSpec(v_block, lambda h, kb, f: v_map(h, kb)),
            state_spec,
            state_spec,
            state_spec,
        ],
        out_specs=[state_spec, state_spec, state_spec],
    )
    shape = jax.ShapeDtypeStruct(state[0].shape, jnp.float32)
    return pl.pallas_call(
        flash_step,
        grid_spec=grid_spec,
        out_shape=[shape, shape, shape],
        input_output_aliases={6: 0, 7: 1, 8: 2},
        compiler_params=pltpu.CompilerParams(dimension_semantics=("arbitrary", "arbitrary")),
    )(flags, qrow, rank, q_src, k_src, v_src, *state)


def exchange_step(axis, count, x_ref, y_ref, local_sem, send_sem, recv_sem):
    me = lax.axis_index(axis)
    barrier = pltpu.get_barrier_semaphore()
    for step in range(1, count):
        pl.semaphore_signal(
            barrier, inc=1, device_id={axis: lax.rem(me + step, count)},
            device_id_type=pl.DeviceIdType.MESH,
        )
    pl.semaphore_wait(barrier, count - 1)
    own = pltpu.make_async_copy(x_ref.at[me], y_ref.at[me], local_sem)
    own.start()
    sends = []
    for step in range(1, count):
        target = lax.rem(me + step, count)
        copy = pltpu.make_async_remote_copy(
            src_ref=x_ref.at[target],
            dst_ref=y_ref.at[me],
            send_sem=send_sem.at[step],
            recv_sem=recv_sem.at[me],
            device_id={axis: target},
            device_id_type=pl.DeviceIdType.MESH,
        )
        copy.start()
        sends.append(copy)
    for copy in sends:
        copy.wait_send()
    for step in range(1, count):
        source = lax.rem(me + count - step, count)
        pltpu.make_async_remote_copy(
            src_ref=x_ref.at[source],
            dst_ref=y_ref.at[source],
            send_sem=send_sem.at[step],
            recv_sem=recv_sem.at[source],
            device_id={axis: source},
            device_id_type=pl.DeviceIdType.MESH,
        ).wait_recv()
    own.wait()


def exchange(blocks, axis, collective):
    count = blocks.shape[0]
    return pl.pallas_call(
        functools.partial(exchange_step, axis, count),
        out_shape=jax.ShapeDtypeStruct(blocks.shape, blocks.dtype),
        in_specs=[pl.BlockSpec(memory_space=pl.ANY)],
        out_specs=pl.BlockSpec(memory_space=pl.ANY),
        scratch_shapes=[
            pltpu.SemaphoreType.DMA(()),
            pltpu.SemaphoreType.DMA((count,)),
            pltpu.SemaphoreType.DMA((count,)),
        ],
        compiler_params=pltpu.CompilerParams(collective_id=collective, has_side_effects=True),
    )(blocks)


def project_step(turned, x_ref, cos_ref, sin_ref, *refs):
    weights, out_ref = refs[:-1], refs[-1]
    widened = x_ref[...].astype(jnp.float32)
    centred = widened - jnp.mean(widened, axis=-1, keepdims=True)
    variance = jnp.mean(centred * centred, axis=-1, keepdims=True)
    normed = (centred * lax.rsqrt(variance + norm_eps)).astype(jnp.bfloat16)
    cosine = cos_ref[...]
    sine = sin_ref[...]
    for index, weight in enumerate(weights):
        width = weight.shape[1]
        product = jnp.dot(normed, weight[...], preferred_element_type=jnp.float32)
        if turned[index]:
            pieces = []
            for head in range(width // HEAD_DIM):
                part = product[:, head * HEAD_DIM : (head + 1) * HEAD_DIM]
                pieces.append(part * cosine + pltpu.roll(part, HEAD_DIM // 2, 1) * sine)
            product = jnp.concatenate(pieces, axis=1)
        out_ref[:, index * width : (index + 1) * width] = product.astype(out_ref.dtype)


def rope_tables(positions):
    half_dim = HEAD_DIM // 2
    frequency = jnp.exp(-jnp.log(rope_base) * jnp.arange(half_dim, dtype=jnp.float32) / half_dim)
    angles = positions.astype(jnp.float32)[:, None] * frequency[None, :]
    cosine = jnp.cos(angles)
    sine = jnp.sin(angles)
    return jnp.concatenate([cosine, cosine], axis=1), jnp.concatenate([-sine, sine], axis=1)


def project(rows, positions, weights, turned, block_rows):
    count, width = rows.shape
    cosine, sine = rope_tables(positions)
    out_width = sum(w.shape[1] for w in weights)
    return pl.pallas_call(
        functools.partial(project_step, tuple(turned)),
        grid=(count // block_rows,),
        in_specs=[
            pl.BlockSpec((block_rows, width), lambda i: (i, 0)),
            pl.BlockSpec((block_rows, HEAD_DIM), lambda i: (i, 0)),
            pl.BlockSpec((block_rows, HEAD_DIM), lambda i: (i, 0)),
        ]
        + [pl.BlockSpec(w.shape, lambda i: (0, 0)) for w in weights],
        out_specs=pl.BlockSpec((block_rows, out_width), lambda i: (i, 0)),
        out_shape=jax.ShapeDtypeStruct((count, out_width), jnp.bfloat16),
    )(rows, cosine, sine, *weights)


rope_base = 10000.0
norm_eps = 1e-05


def swapped(value, axis, apart):
    mask = 2**apart
    pairs = [(source, source ^ mask) for source in range(lax.axis_size(axis))]
    return lax.ppermute(value, axis, pairs)


def shards(
    tokens,
    w_query,
    w_key,
    w_value,
    w_out,
    own_cache,
    guest_cache,
    rec_hidden,
    deal_order,
    own_len,
    guest_len,
    rec_index,
):
    groups = lax.axis_size("grp")
    group_id = lax.axis_index("grp")
    partner_id = (group_id + groups // 2) % groups
    swap_bit = groups.bit_length() - 2
    local_width = w_query.shape[1]
    local_heads = local_width // HEAD_DIM
    requests, local_rows, model_width = tokens.shape

    fetched = swapped(guest_cache[0], "grp", swap_bit)

    server = jnp.zeros_like(deal_order).at[deal_order].set(jnp.arange(groups, dtype=jnp.int32))
    start_of = own_len[server] + guest_len[(server + groups // 2) % groups]
    local_positions = (
        start_of[:, None] + group_id * local_rows + jnp.arange(local_rows, dtype=jnp.int32)[None, :]
    ).reshape(-1)

    projected = project(
        tokens.reshape(-1, model_width), local_positions, [w_query, w_key, w_value],
        [True, True, False], 256,
    ).reshape(requests, local_rows, -1)
    arranged = jnp.take(projected, deal_order, axis=0)
    dealt = lax.all_to_all(arranged, "grp", split_axis=0, concat_axis=1, tiled=True)[0]
    span_len = dealt.shape[0]

    own_count = own_len[group_id]
    guest_count = guest_len[partner_id]
    rec_positions = rec_index[0]
    recomputed = project(rec_hidden[0], rec_positions, [w_key, w_value], [True, False], 256)
    replaced = jnp.zeros((own_cache.shape[2],), jnp.bool_).at[rec_positions].set(True)

    heads = local_heads
    chunks = 2
    piece = local_rows // chunks
    chunk_len = span_len // chunks
    order = dealt.reshape(groups, chunks, piece, -1).transpose(1, 0, 2, 3).reshape(span_len, -1)
    row_of = (
        jnp.arange(span_len, dtype=jnp.int32).reshape(groups, chunks, piece).transpose(1, 0, 2).reshape(-1)
    )
    rec_count = recomputed.shape[0]
    fresh = jnp.concatenate(
        [order[:, local_width:], recomputed], axis=0
    )
    fresh_rank = jnp.concatenate([row_of, jnp.full((rec_count,), -1, jnp.int32)])[None, :]
    fresh_count = span_len + rec_count
    never = jnp.int32(1 << 30)
    cap = own_cache.shape[2]
    block_len = 2048
    key_rows = jnp.arange(cap, dtype=jnp.int32)
    own_rank = jnp.where((key_rows < own_count) & ~replaced, -1, never)[None, :]
    own_flags = (jnp.arange(cap // block_len, dtype=jnp.int32) * block_len < own_count).astype(jnp.int32)
    gcap = fetched.shape[1]
    guest_rows = jnp.arange(gcap, dtype=jnp.int32)
    guest_rank = jnp.where(guest_rows < guest_count, -1, never)[None, :]
    guest_flags = (jnp.arange(gcap // block_len, dtype=jnp.int32) * block_len < guest_count).astype(jnp.int32)
    blocks = lax.axis_size("tp")
    out_by_block = w_out.reshape(local_width, blocks, -1)

    returned = []
    exchanged = []
    for chunk in range(chunks):
        query_rows = row_of[chunk * chunk_len : (chunk + 1) * chunk_len][:, None]
        state = (
            jnp.full((chunk_len, local_width), FLOOR, jnp.float32),
            jnp.zeros((chunk_len, local_width), jnp.float32),
            jnp.zeros((chunk_len, local_width), jnp.float32),
        )
        state = attend(
            state, jnp.ones((1,), jnp.int32), query_rows, fresh_rank, order, chunk,
            fresh, lambda h, kb: (kb, h), fresh, lambda h, kb: (kb, heads + h),
            fresh_count, heads, fresh_count,
        )
        state = attend(
            state, own_flags, query_rows, own_rank, order, chunk,
            own_cache[0], lambda h, kb: (0, kb, h), own_cache[0], lambda h, kb: (1, kb, h),
            cap, heads, block_len,
        )
        state = attend(
            state, guest_flags, query_rows, guest_rank, order, chunk,
            fetched, lambda h, kb: (0, kb, h), fetched, lambda h, kb: (1, kb, h),
            gcap, heads, block_len,
        )
        attended = (state[2] / state[1]).astype(jnp.bfloat16)
        partial_value = jnp.einsum(
            "qc,ctd->tqd", attended, out_by_block, preferred_element_type=jnp.float32
        ).astype(jnp.bfloat16)
        exchanged.append(
            lax.all_to_all(partial_value, "tp", split_axis=0, concat_axis=0, tiled=True)
        )
    for chunk in range(chunks):
        mixed_rows = exchanged[chunk].astype(jnp.float32).sum(axis=0).astype(jnp.bfloat16)
        returned.append(exchange(mixed_rows.reshape(groups, piece, -1), "grp", 1 + chunk))
    returned_rows = jnp.stack(returned, axis=1).reshape(groups, local_rows, -1)
    return jnp.take(returned_rows, server, axis=0)


def solution(mesh):
    return jax.shard_map(
        shards,
        mesh=mesh,
        in_specs=(
            P(None, "grp", None),
            P(None, "tp"),
            P(None, "tp"),
            P(None, "tp"),
            P("tp", None),
            P("grp", None, None, "tp"),
            P("grp", None, None, "tp"),
            P("grp", None, None),
            P(),
            P(),
            P(),
            P("grp", None),
        ),
        out_specs=P(None, "grp", "tp"),
        check_vma=False,
    )
```

```python
import functools

import jax
import jax.numpy as jnp
from jax import lax
from jax.experimental import pallas as pl
from jax.experimental.pallas import tpu as pltpu
from jax.sharding import PartitionSpec as P

HEAD_DIM = 128


FLOOR = -1e30


def flash_step(flags_ref, qrow_ref, rank_ref, q_ref, k_ref, v_ref, m_in, l_in, acc_in, m_out, l_out, acc_out):
    kb = pl.program_id(1)

    @pl.when(kb == 0)
    def _():
        m_out[...] = m_in[...]
        l_out[...] = l_in[...]
        acc_out[...] = acc_in[...]

    @pl.when(flags_ref[kb] > 0)
    def _():
        scores = lax.dot_general(
            q_ref[...], k_ref[...], (((1,), (1,)), ((), ())), preferred_element_type=jnp.float32
        ) * (HEAD_DIM ** -0.5)
        scores = jnp.where(rank_ref[...] <= qrow_ref[...], scores, FLOOR)
        m_prev = m_out[...]
        m_new = jnp.maximum(m_prev, jnp.max(scores, axis=1, keepdims=True))
        factor = jnp.exp(m_prev - m_new)
        expanded = jnp.exp(scores - m_new[:, :1])
        l_out[...] = factor * l_out[...] + jnp.sum(expanded, axis=1, keepdims=True)
        acc_out[...] = factor * acc_out[...] + jnp.dot(
            expanded.astype(jnp.bfloat16), v_ref[...], preferred_element_type=jnp.float32
        )
        m_out[...] = m_new


def attend(state, flags, qrow, rank, q_src, q_block, k_src, k_map, v_src, v_map, key_count, heads, block_len):
    query_count = qrow.shape[0]
    state_spec = pl.BlockSpec((query_count, HEAD_DIM), lambda h, kb, f: (0, h))
    k_block = (block_len, HEAD_DIM) if k_src.ndim == 2 else (None, block_len, HEAD_DIM)
    v_block = (block_len, HEAD_DIM) if v_src.ndim == 2 else (None, block_len, HEAD_DIM)
    grid_spec = pltpu.PrefetchScalarGridSpec(
        num_scalar_prefetch=1,
        grid=(heads, key_count // block_len),
        in_specs=[
            pl.BlockSpec((query_count, 1), lambda h, kb, f: (0, 0)),
            pl.BlockSpec((1, block_len), lambda h, kb, f: (0, kb)),
            pl.BlockSpec((query_count, HEAD_DIM), lambda h, kb, f: (q_block, h)),
            pl.BlockSpec(k_block, lambda h, kb, f: k_map(h, kb)),
            pl.BlockSpec(v_block, lambda h, kb, f: v_map(h, kb)),
            state_spec,
            state_spec,
            state_spec,
        ],
        out_specs=[state_spec, state_spec, state_spec],
    )
    shape = jax.ShapeDtypeStruct(state[0].shape, jnp.float32)
    return pl.pallas_call(
        flash_step,
        grid_spec=grid_spec,
        out_shape=[shape, shape, shape],
        input_output_aliases={6: 0, 7: 1, 8: 2},
        compiler_params=pltpu.CompilerParams(dimension_semantics=("arbitrary", "arbitrary")),
    )(flags, qrow, rank, q_src, k_src, v_src, *state)


def exchange_step(axis, count, x_ref, y_ref, local_sem, send_sem, recv_sem):
    me = lax.axis_index(axis)
    barrier = pltpu.get_barrier_semaphore()
    for step in range(1, count):
        pl.semaphore_signal(
            barrier, inc=1, device_id={axis: lax.rem(me + step, count)},
            device_id_type=pl.DeviceIdType.MESH,
        )
    pl.semaphore_wait(barrier, count - 1)
    own = pltpu.make_async_copy(x_ref.at[me], y_ref.at[me], local_sem)
    own.start()
    sends = []
    for step in range(1, count):
        target = lax.rem(me + step, count)
        copy = pltpu.make_async_remote_copy(
            src_ref=x_ref.at[target],
            dst_ref=y_ref.at[me],
            send_sem=send_sem.at[step],
            recv_sem=recv_sem.at[me],
            device_id={axis: target},
            device_id_type=pl.DeviceIdType.MESH,
        )
        copy.start()
        sends.append(copy)
    for copy in sends:
        copy.wait_send()
    for step in range(1, count):
        source = lax.rem(me + count - step, count)
        pltpu.make_async_remote_copy(
            src_ref=x_ref.at[source],
            dst_ref=y_ref.at[source],
            send_sem=send_sem.at[step],
            recv_sem=recv_sem.at[source],
            device_id={axis: source},
            device_id_type=pl.DeviceIdType.MESH,
        ).wait_recv()
    own.wait()


def exchange(blocks, axis, collective):
    count = blocks.shape[0]
    return pl.pallas_call(
        functools.partial(exchange_step, axis, count),
        out_shape=jax.ShapeDtypeStruct(blocks.shape, blocks.dtype),
        in_specs=[pl.BlockSpec(memory_space=pl.ANY)],
        out_specs=pl.BlockSpec(memory_space=pl.ANY),
        scratch_shapes=[
            pltpu.SemaphoreType.DMA(()),
            pltpu.SemaphoreType.DMA((count,)),
            pltpu.SemaphoreType.DMA((count,)),
        ],
        compiler_params=pltpu.CompilerParams(collective_id=collective, has_side_effects=True),
    )(blocks)


def project_step(turned, x_ref, cos_ref, sin_ref, *refs):
    weights, out_ref = refs[:-1], refs[-1]
    widened = x_ref[...].astype(jnp.float32)
    centred = widened - jnp.mean(widened, axis=-1, keepdims=True)
    variance = jnp.mean(centred * centred, axis=-1, keepdims=True)
    normed = (centred * lax.rsqrt(variance + norm_eps)).astype(jnp.bfloat16)
    cosine = cos_ref[...]
    sine = sin_ref[...]
    for index, weight in enumerate(weights):
        width = weight.shape[1]
        product = jnp.dot(normed, weight[...], preferred_element_type=jnp.float32)
        if turned[index]:
            pieces = []
            for head in range(width // HEAD_DIM):
                part = product[:, head * HEAD_DIM : (head + 1) * HEAD_DIM]
                pieces.append(part * cosine + pltpu.roll(part, HEAD_DIM // 2, 1) * sine)
            product = jnp.concatenate(pieces, axis=1)
        out_ref[:, index * width : (index + 1) * width] = product.astype(out_ref.dtype)


def rope_tables(positions):
    half_dim = HEAD_DIM // 2
    frequency = jnp.exp(-jnp.log(rope_base) * jnp.arange(half_dim, dtype=jnp.float32) / half_dim)
    doubled = jnp.concatenate([frequency, frequency])
    sign = jnp.concatenate([-jnp.ones((half_dim,), jnp.float32), jnp.ones((half_dim,), jnp.float32)])
    angles = positions.astype(jnp.float32)[:, None] * doubled[None, :]
    return jnp.cos(angles), jnp.sin(angles) * sign[None, :]


def project(rows, positions, weights, turned, block_rows):
    count, width = rows.shape
    cosine, sine = rope_tables(positions)
    out_width = sum(w.shape[1] for w in weights)
    return pl.pallas_call(
        functools.partial(project_step, tuple(turned)),
        grid=(count // block_rows,),
        in_specs=[
            pl.BlockSpec((block_rows, width), lambda i: (i, 0)),
            pl.BlockSpec((block_rows, HEAD_DIM), lambda i: (i, 0)),
            pl.BlockSpec((block_rows, HEAD_DIM), lambda i: (i, 0)),
        ]
        + [pl.BlockSpec(w.shape, lambda i: (0, 0)) for w in weights],
        out_specs=pl.BlockSpec((block_rows, out_width), lambda i: (i, 0)),
        out_shape=jax.ShapeDtypeStruct((count, out_width), jnp.bfloat16),
    )(rows, cosine, sine, *weights)


rope_base = 10000.0
norm_eps = 1e-05


def swapped(value, axis, apart):
    mask = 2**apart
    pairs = [(source, source ^ mask) for source in range(lax.axis_size(axis))]
    return lax.ppermute(value, axis, pairs)


def shards(
    tokens,
    w_query,
    w_key,
    w_value,
    w_out,
    own_cache,
    guest_cache,
    rec_hidden,
    deal_order,
    own_len,
    guest_len,
    rec_index,
):
    groups = lax.axis_size("grp")
    group_id = lax.axis_index("grp")
    partner_id = (group_id + groups // 2) % groups
    swap_bit = groups.bit_length() - 2
    local_width = w_query.shape[1]
    local_heads = local_width // HEAD_DIM
    requests, local_rows, model_width = tokens.shape

    fetched = swapped(guest_cache[0], "grp", swap_bit)

    server = jnp.zeros_like(deal_order).at[deal_order].set(jnp.arange(groups, dtype=jnp.int32))
    start_of = jnp.zeros_like(deal_order).at[deal_order].set(
        own_len + jnp.roll(guest_len, -(groups // 2))
    )
    local_positions = (
        start_of[:, None] + group_id * local_rows + jnp.arange(local_rows, dtype=jnp.int32)[None, :]
    ).reshape(-1)

    projected = project(
        tokens.reshape(-1, model_width), local_positions, [w_query, w_key, w_value],
        [True, True, False], 256,
    ).reshape(requests, local_rows, -1)
    arranged = jnp.take(projected, deal_order, axis=0)
    dealt = lax.all_to_all(arranged, "grp", split_axis=0, concat_axis=1, tiled=True)[0]
    span_len = dealt.shape[0]

    own_count = own_len[group_id]
    guest_count = guest_len[partner_id]
    rec_positions = rec_index[0]
    recomputed = project(rec_hidden[0], rec_positions, [w_key, w_value], [True, False], 256)
    replaced = jnp.zeros((own_cache.shape[2],), jnp.bool_).at[rec_positions].set(True)

    heads = local_heads
    chunks = 2
    piece = local_rows // chunks
    chunk_len = span_len // chunks
    order = dealt.reshape(groups, chunks, piece, -1).transpose(1, 0, 2, 3).reshape(span_len, -1)
    row_of = (
        jnp.arange(span_len, dtype=jnp.int32).reshape(groups, chunks, piece).transpose(1, 0, 2).reshape(-1)
    )
    rec_count = recomputed.shape[0]
    fresh = jnp.concatenate(
        [order[:, local_width:], recomputed], axis=0
    )
    fresh_rank = jnp.concatenate([row_of, jnp.full((rec_count,), -1, jnp.int32)])[None, :]
    fresh_count = span_len + rec_count
    never = jnp.int32(1 << 30)
    cap = own_cache.shape[2]
    block_len = 2048
    key_rows = jnp.arange(cap, dtype=jnp.int32)
    own_rank = jnp.where((key_rows < own_count) & ~replaced, -1, never)[None, :]
    own_flags = (jnp.arange(cap // block_len, dtype=jnp.int32) * block_len < own_count).astype(jnp.int32)
    gcap = fetched.shape[1]
    guest_rows = jnp.arange(gcap, dtype=jnp.int32)
    guest_rank = jnp.where(guest_rows < guest_count, -1, never)[None, :]
    guest_flags = (jnp.arange(gcap // block_len, dtype=jnp.int32) * block_len < guest_count).astype(jnp.int32)
    blocks = lax.axis_size("tp")
    out_by_block = w_out.reshape(local_width, blocks, -1)

    returned = []
    exchanged = []
    for chunk in range(chunks):
        query_rows = row_of[chunk * chunk_len : (chunk + 1) * chunk_len][:, None]
        state = (
            jnp.full((chunk_len, local_width), FLOOR, jnp.float32),
            jnp.zeros((chunk_len, local_width), jnp.float32),
            jnp.zeros((chunk_len, local_width), jnp.float32),
        )
        state = attend(
            state, jnp.ones((1,), jnp.int32), query_rows, fresh_rank, order, chunk,
            fresh, lambda h, kb: (kb, h), fresh, lambda h, kb: (kb, heads + h),
            fresh_count, heads, fresh_count,
        )
        state = attend(
            state, own_flags, query_rows, own_rank, order, chunk,
            own_cache[0], lambda h, kb: (0, kb, h), own_cache[0], lambda h, kb: (1, kb, h),
            cap, heads, block_len,
        )
        state = attend(
            state, guest_flags, query_rows, guest_rank, order, chunk,
            fetched, lambda h, kb: (0, kb, h), fetched, lambda h, kb: (1, kb, h),
            gcap, heads, block_len,
        )
        attended = (state[2] / state[1]).astype(jnp.bfloat16)
        partial_value = jnp.einsum(
            "qc,ctd->tqd", attended, out_by_block, preferred_element_type=jnp.float32
        ).astype(jnp.bfloat16)
        exchanged.append(
            lax.all_to_all(partial_value, "tp", split_axis=0, concat_axis=0, tiled=True)
        )
    for chunk in range(chunks):
        mixed_rows = exchanged[chunk].astype(jnp.float32).sum(axis=0).astype(jnp.bfloat16)
        returned.append(exchange(mixed_rows.reshape(groups, piece, -1), "grp", 1 + chunk))
    returned_rows = jnp.stack(returned, axis=1).reshape(groups, local_rows, -1)
    return jnp.take(returned_rows, server, axis=0)


def solution(mesh):
    return jax.shard_map(
        shards,
        mesh=mesh,
        in_specs=(
            P(None, "grp", None),
            P(None, "tp"),
            P(None, "tp"),
            P(None, "tp"),
            P("tp", None),
            P("grp", None, None, "tp"),
            P("grp", None, None, "tp"),
            P("grp", None, None),
            P(),
            P(),
            P(),
            P("grp", None),
        ),
        out_specs=P(None, "grp", "tp"),
        check_vma=False,
    )
```

```python
import functools

import jax
import jax.numpy as jnp
from jax import lax
from jax.experimental import pallas as pl
from jax.experimental.pallas import tpu as pltpu
from jax.sharding import PartitionSpec as P

HEAD_DIM = 128


FLOOR = -1e30


def flash_step(flags_ref, qrow_ref, rank_ref, q_ref, k_ref, v_ref, m_in, l_in, acc_in, m_out, l_out, acc_out):
    kb = pl.program_id(1)

    @pl.when(kb == 0)
    def _():
        m_out[...] = m_in[...]
        l_out[...] = l_in[...]
        acc_out[...] = acc_in[...]

    @pl.when(flags_ref[kb] > 0)
    def _():
        scores = lax.dot_general(
            q_ref[...], k_ref[...], (((1,), (1,)), ((), ())), preferred_element_type=jnp.float32
        ) * (HEAD_DIM ** -0.5)
        scores = jnp.where(rank_ref[...] <= qrow_ref[...], scores, FLOOR)
        m_prev = m_out[...]
        m_new = jnp.maximum(m_prev, jnp.max(scores, axis=1, keepdims=True))
        factor = jnp.exp(m_prev - m_new)
        expanded = jnp.exp(scores - m_new[:, :1])
        l_out[...] = factor * l_out[...] + jnp.sum(expanded, axis=1, keepdims=True)
        acc_out[...] = factor * acc_out[...] + jnp.dot(
            expanded.astype(jnp.bfloat16), v_ref[...], preferred_element_type=jnp.float32
        )
        m_out[...] = m_new


def attend(state, flags, qrow, rank, q_src, q_block, k_src, k_map, v_src, v_map, key_count, heads, block_len):
    query_count = qrow.shape[0]
    state_spec = pl.BlockSpec((query_count, HEAD_DIM), lambda h, kb, f: (0, h))
    k_block = (block_len, HEAD_DIM) if k_src.ndim == 2 else (None, block_len, HEAD_DIM)
    v_block = (block_len, HEAD_DIM) if v_src.ndim == 2 else (None, block_len, HEAD_DIM)
    grid_spec = pltpu.PrefetchScalarGridSpec(
        num_scalar_prefetch=1,
        grid=(heads, key_count // block_len),
        in_specs=[
            pl.BlockSpec((query_count, 1), lambda h, kb, f: (0, 0)),
            pl.BlockSpec((1, block_len), lambda h, kb, f: (0, kb)),
            pl.BlockSpec((query_count, HEAD_DIM), lambda h, kb, f: (q_block, h)),
            pl.BlockSpec(k_block, lambda h, kb, f: k_map(h, kb)),
            pl.BlockSpec(v_block, lambda h, kb, f: v_map(h, kb)),
            state_spec,
            state_spec,
            state_spec,
        ],
        out_specs=[state_spec, state_spec, state_spec],
    )
    shape = jax.ShapeDtypeStruct(state[0].shape, jnp.float32)
    return pl.pallas_call(
        flash_step,
        grid_spec=grid_spec,
        out_shape=[shape, shape, shape],
        input_output_aliases={6: 0, 7: 1, 8: 2},
        compiler_params=pltpu.CompilerParams(dimension_semantics=("arbitrary", "arbitrary")),
    )(flags, qrow, rank, q_src, k_src, v_src, *state)


def exchange_step(axis, count, x_ref, y_ref, local_sem, send_sem, recv_sem):
    me = lax.axis_index(axis)
    barrier = pltpu.get_barrier_semaphore()
    for step in range(1, count):
        pl.semaphore_signal(
            barrier, inc=1, device_id={axis: lax.rem(me + step, count)},
            device_id_type=pl.DeviceIdType.MESH,
        )
    pl.semaphore_wait(barrier, count - 1)
    own = pltpu.make_async_copy(x_ref.at[me], y_ref.at[me], local_sem)
    own.start()
    sends = []
    for step in range(1, count):
        target = lax.rem(me + step, count)
        copy = pltpu.make_async_remote_copy(
            src_ref=x_ref.at[target],
            dst_ref=y_ref.at[me],
            send_sem=send_sem.at[step],
            recv_sem=recv_sem.at[me],
            device_id={axis: target},
            device_id_type=pl.DeviceIdType.MESH,
        )
        copy.start()
        sends.append(copy)
    for copy in sends:
        copy.wait_send()
    for step in range(1, count):
        source = lax.rem(me + count - step, count)
        pltpu.make_async_remote_copy(
            src_ref=x_ref.at[source],
            dst_ref=y_ref.at[source],
            send_sem=send_sem.at[step],
            recv_sem=recv_sem.at[source],
            device_id={axis: source},
            device_id_type=pl.DeviceIdType.MESH,
        ).wait_recv()
    own.wait()


def exchange(blocks, axis, collective):
    count = blocks.shape[0]
    return pl.pallas_call(
        functools.partial(exchange_step, axis, count),
        out_shape=jax.ShapeDtypeStruct(blocks.shape, blocks.dtype),
        in_specs=[pl.BlockSpec(memory_space=pl.ANY)],
        out_specs=pl.BlockSpec(memory_space=pl.ANY),
        scratch_shapes=[
            pltpu.SemaphoreType.DMA(()),
            pltpu.SemaphoreType.DMA((count,)),
            pltpu.SemaphoreType.DMA((count,)),
        ],
        compiler_params=pltpu.CompilerParams(collective_id=collective, has_side_effects=True),
    )(blocks)


def project_step(turned, placed, *refs):
    if placed:
        slot_ref, refs = refs[0], refs[1:]
    x_ref, cos_ref, sin_ref = refs[:3]
    weights, out_ref = refs[3:-1], refs[-1]
    widened = x_ref[...].astype(jnp.float32)
    centred = widened - jnp.mean(widened, axis=-1, keepdims=True)
    variance = jnp.mean(centred * centred, axis=-1, keepdims=True)
    normed = (centred * lax.rsqrt(variance + norm_eps)).astype(jnp.bfloat16)
    cosine = cos_ref[...]
    sine = sin_ref[...]
    for index, weight in enumerate(weights):
        width = weight.shape[1]
        product = jnp.dot(normed, weight[...], preferred_element_type=jnp.float32)
        if turned[index]:
            pieces = []
            for head in range(width // HEAD_DIM):
                part = product[:, head * HEAD_DIM : (head + 1) * HEAD_DIM]
                pieces.append(part * cosine + pltpu.roll(part, HEAD_DIM // 2, 1) * sine)
            product = jnp.concatenate(pieces, axis=1)
        product = product.astype(out_ref.dtype)
        columns = slice(index * width, (index + 1) * width)
        if placed:
            rows = out_ref.shape[1]
            first = pl.program_id(0) * (product.shape[0] // rows)
            for j in range(product.shape[0] // rows):
                out_ref[slot_ref[first + j], :, columns] = product[j * rows : (j + 1) * rows]
        else:
            out_ref[:, columns] = product


def rope_tables(positions):
    half_dim = HEAD_DIM // 2
    frequency = jnp.exp(-jnp.log(rope_base) * jnp.arange(half_dim, dtype=jnp.float32) / half_dim)
    doubled = jnp.concatenate([frequency, frequency])
    sign = jnp.concatenate([-jnp.ones((half_dim,), jnp.float32), jnp.ones((half_dim,), jnp.float32)])
    angles = positions.astype(jnp.float32)[:, None] * doubled[None, :]
    return jnp.cos(angles), jnp.sin(angles) * sign[None, :]


def project(rows, positions, weights, turned, block_rows, slots=None, rows_per_slot=None):
    count, width = rows.shape
    cosine, sine = rope_tables(positions)
    out_width = sum(w.shape[1] for w in weights)
    placed = slots is not None
    extra = (lambda i, s: (i, 0)) if placed else (lambda i: (i, 0))
    fixed = (lambda i, s: (0, 0)) if placed else (lambda i: (0, 0))
    in_specs = [
        pl.BlockSpec((block_rows, width), extra),
        pl.BlockSpec((block_rows, HEAD_DIM), extra),
        pl.BlockSpec((block_rows, HEAD_DIM), extra),
    ] + [pl.BlockSpec(w.shape, fixed) for w in weights]
    if placed:
        out_shape = (count // rows_per_slot, rows_per_slot, out_width)
        grid_spec = pltpu.PrefetchScalarGridSpec(
            num_scalar_prefetch=1,
            grid=(count // block_rows,),
            in_specs=in_specs,
            out_specs=pl.BlockSpec(out_shape, lambda i, s: (0, 0, 0)),
        )
        operands = (slots, rows, cosine, sine, *weights)
    else:
        out_shape = (count, out_width)
        grid_spec = pl.GridSpec(
            grid=(count // block_rows,),
            in_specs=in_specs,
            out_specs=pl.BlockSpec((block_rows, out_width), extra),
        )
        operands = (rows, cosine, sine, *weights)
    return pl.pallas_call(
        functools.partial(project_step, tuple(turned), placed),
        grid_spec=grid_spec,
        out_shape=jax.ShapeDtypeStruct(out_shape, jnp.bfloat16),
    )(*operands)

rope_base = 10000.0
norm_eps = 1e-05


def swapped(value, axis, apart):
    mask = 2**apart
    pairs = [(source, source ^ mask) for source in range(lax.axis_size(axis))]
    return lax.ppermute(value, axis, pairs)


def shards(
    tokens,
    w_query,
    w_key,
    w_value,
    w_out,
    own_cache,
    guest_cache,
    rec_hidden,
    deal_order,
    own_len,
    guest_len,
    rec_index,
):
    groups = lax.axis_size("grp")
    group_id = lax.axis_index("grp")
    partner_id = (group_id + groups // 2) % groups
    swap_bit = groups.bit_length() - 2
    local_width = w_query.shape[1]
    local_heads = local_width // HEAD_DIM
    requests, local_rows, model_width = tokens.shape

    fetched = swapped(guest_cache[0], "grp", swap_bit)

    server = jnp.zeros_like(deal_order).at[deal_order].set(jnp.arange(groups, dtype=jnp.int32))
    start_of = jnp.zeros_like(deal_order).at[deal_order].set(
        own_len + jnp.roll(guest_len, -(groups // 2))
    )
    local_positions = (
        start_of[:, None] + group_id * local_rows + jnp.arange(local_rows, dtype=jnp.int32)[None, :]
    ).reshape(-1)

    arranged = project(
        tokens.reshape(-1, model_width), local_positions, [w_query, w_key, w_value],
        [True, True, False], 256, server, local_rows,
    )
    dealt = lax.all_to_all(arranged, "grp", split_axis=0, concat_axis=1, tiled=True)[0]
    span_len = dealt.shape[0]

    own_count = own_len[group_id]
    guest_count = guest_len[partner_id]
    rec_positions = rec_index[0]
    recomputed = project(rec_hidden[0], rec_positions, [w_key, w_value], [True, False], 256)
    replaced = jnp.zeros((own_cache.shape[2],), jnp.bool_).at[rec_positions].set(True)

    heads = local_heads
    chunks = 2
    piece = local_rows // chunks
    chunk_len = span_len // chunks
    order = dealt.reshape(groups, chunks, piece, -1).transpose(1, 0, 2, 3).reshape(span_len, -1)
    row_of = (
        jnp.arange(span_len, dtype=jnp.int32).reshape(groups, chunks, piece).transpose(1, 0, 2).reshape(-1)
    )
    rec_count = recomputed.shape[0]
    fresh = jnp.concatenate(
        [order[:, local_width:], recomputed], axis=0
    )
    fresh_rank = jnp.concatenate([row_of, jnp.full((rec_count,), -1, jnp.int32)])[None, :]
    fresh_count = span_len + rec_count
    never = jnp.int32(1 << 30)
    cap = own_cache.shape[2]
    block_len = 2048
    key_rows = jnp.arange(cap, dtype=jnp.int32)
    own_rank = jnp.where((key_rows < own_count) & ~replaced, -1, never)[None, :]
    own_flags = (jnp.arange(cap // block_len, dtype=jnp.int32) * block_len < own_count).astype(jnp.int32)
    gcap = fetched.shape[1]
    guest_rows = jnp.arange(gcap, dtype=jnp.int32)
    guest_rank = jnp.where(guest_rows < guest_count, -1, never)[None, :]
    guest_flags = (jnp.arange(gcap // block_len, dtype=jnp.int32) * block_len < guest_count).astype(jnp.int32)
    blocks = lax.axis_size("tp")
    out_by_block = w_out.reshape(local_width, blocks, -1)

    returned = []
    exchanged = []
    for chunk in range(chunks):
        query_rows = row_of[chunk * chunk_len : (chunk + 1) * chunk_len][:, None]
        state = (
            jnp.full((chunk_len, local_width), FLOOR, jnp.float32),
            jnp.zeros((chunk_len, local_width), jnp.float32),
            jnp.zeros((chunk_len, local_width), jnp.float32),
        )
        state = attend(
            state, jnp.ones((1,), jnp.int32), query_rows, fresh_rank, order, chunk,
            fresh, lambda h, kb: (kb, h), fresh, lambda h, kb: (kb, heads + h),
            fresh_count, heads, fresh_count,
        )
        state = attend(
            state, own_flags, query_rows, own_rank, order, chunk,
            own_cache[0], lambda h, kb: (0, kb, h), own_cache[0], lambda h, kb: (1, kb, h),
            cap, heads, block_len,
        )
        state = attend(
            state, guest_flags, query_rows, guest_rank, order, chunk,
            fetched, lambda h, kb: (0, kb, h), fetched, lambda h, kb: (1, kb, h),
            gcap, heads, block_len,
        )
        attended = (state[2] / state[1]).astype(jnp.bfloat16)
        partial_value = jnp.einsum(
            "qc,ctd->tqd", attended, out_by_block, preferred_element_type=jnp.float32
        ).astype(jnp.bfloat16)
        exchanged.append(
            lax.all_to_all(partial_value, "tp", split_axis=0, concat_axis=0, tiled=True)
        )
    for chunk in range(chunks):
        mixed_rows = exchanged[chunk].astype(jnp.float32).sum(axis=0).astype(jnp.bfloat16)
        returned.append(exchange(mixed_rows.reshape(groups, piece, -1), "grp", 1 + chunk))
    returned_rows = jnp.stack(returned, axis=1).reshape(groups, local_rows, -1)
    return jnp.take(returned_rows, server, axis=0)


def solution(mesh):
    return jax.shard_map(
        shards,
        mesh=mesh,
        in_specs=(
            P(None, "grp", None),
            P(None, "tp"),
            P(None, "tp"),
            P(None, "tp"),
            P("tp", None),
            P("grp", None, None, "tp"),
            P("grp", None, None, "tp"),
            P("grp", None, None),
            P(),
            P(),
            P(),
            P("grp", None),
        ),
        out_specs=P(None, "grp", "tp"),
        check_vma=False,
    )
```

```python
import functools

import jax
import jax.numpy as jnp
from jax import lax
from jax.experimental import pallas as pl
from jax.experimental.pallas import tpu as pltpu
from jax.sharding import PartitionSpec as P

HEAD_DIM = 128


FLOOR = -1e30


def flash_step(flags_ref, qrow_ref, rank_ref, q_ref, k_ref, v_ref, m_in, l_in, acc_in, m_out, l_out, acc_out):
    kb = pl.program_id(1)

    @pl.when(kb == 0)
    def _():
        m_out[...] = m_in[...]
        l_out[...] = l_in[...]
        acc_out[...] = acc_in[...]

    @pl.when(flags_ref[kb] > 0)
    def _():
        scores = lax.dot_general(
            q_ref[...], k_ref[...], (((1,), (1,)), ((), ())), preferred_element_type=jnp.float32
        ) * (HEAD_DIM ** -0.5)
        scores = jnp.where(rank_ref[...] <= qrow_ref[...], scores, FLOOR)
        m_prev = m_out[...]
        m_new = jnp.maximum(m_prev, jnp.max(scores, axis=1, keepdims=True))
        factor = jnp.exp(m_prev - m_new)
        expanded = jnp.exp(scores - m_new[:, :1])
        l_out[...] = factor * l_out[...] + jnp.sum(expanded, axis=1, keepdims=True)
        acc_out[...] = factor * acc_out[...] + jnp.dot(
            expanded.astype(jnp.bfloat16), v_ref[...], preferred_element_type=jnp.float32
        )
        m_out[...] = m_new


def attend(state, flags, qrow, rank, q_src, q_block, k_src, k_map, v_src, v_map, key_count, heads, block_len):
    query_count = qrow.shape[0]
    state_spec = pl.BlockSpec((query_count, HEAD_DIM), lambda h, kb, f: (0, h))
    k_block = (block_len, HEAD_DIM) if k_src.ndim == 2 else (None, block_len, HEAD_DIM)
    v_block = (block_len, HEAD_DIM) if v_src.ndim == 2 else (None, block_len, HEAD_DIM)
    grid_spec = pltpu.PrefetchScalarGridSpec(
        num_scalar_prefetch=1,
        grid=(heads, key_count // block_len),
        in_specs=[
            pl.BlockSpec((query_count, 1), lambda h, kb, f: (0, 0)),
            pl.BlockSpec((1, block_len), lambda h, kb, f: (0, kb)),
            pl.BlockSpec((query_count, HEAD_DIM), lambda h, kb, f: (q_block, h)),
            pl.BlockSpec(k_block, lambda h, kb, f: k_map(h, kb)),
            pl.BlockSpec(v_block, lambda h, kb, f: v_map(h, kb)),
            state_spec,
            state_spec,
            state_spec,
        ],
        out_specs=[state_spec, state_spec, state_spec],
    )
    shape = jax.ShapeDtypeStruct(state[0].shape, jnp.float32)
    return pl.pallas_call(
        flash_step,
        grid_spec=grid_spec,
        out_shape=[shape, shape, shape],
        input_output_aliases={6: 0, 7: 1, 8: 2},
        compiler_params=pltpu.CompilerParams(dimension_semantics=("arbitrary", "arbitrary")),
    )(flags, qrow, rank, q_src, k_src, v_src, *state)


def exchange_step(axis, count, x_ref, y_ref, local_sem, send_sem, recv_sem):
    me = lax.axis_index(axis)
    barrier = pltpu.get_barrier_semaphore()
    for step in range(1, count):
        pl.semaphore_signal(
            barrier, inc=1, device_id={axis: lax.rem(me + step, count)},
            device_id_type=pl.DeviceIdType.MESH,
        )
    pl.semaphore_wait(barrier, count - 1)
    own = pltpu.make_async_copy(x_ref.at[me], y_ref.at[me], local_sem)
    own.start()
    sends = []
    for step in range(1, count):
        target = lax.rem(me + step, count)
        copy = pltpu.make_async_remote_copy(
            src_ref=x_ref.at[target],
            dst_ref=y_ref.at[me],
            send_sem=send_sem.at[step],
            recv_sem=recv_sem.at[me],
            device_id={axis: target},
            device_id_type=pl.DeviceIdType.MESH,
        )
        copy.start()
        sends.append(copy)
    for copy in sends:
        copy.wait_send()
    for step in range(1, count):
        source = lax.rem(me + count - step, count)
        pltpu.make_async_remote_copy(
            src_ref=x_ref.at[source],
            dst_ref=y_ref.at[source],
            send_sem=send_sem.at[step],
            recv_sem=recv_sem.at[source],
            device_id={axis: source},
            device_id_type=pl.DeviceIdType.MESH,
        ).wait_recv()
    own.wait()


def exchange(blocks, axis, collective):
    count = blocks.shape[0]
    return pl.pallas_call(
        functools.partial(exchange_step, axis, count),
        out_shape=jax.ShapeDtypeStruct(blocks.shape, blocks.dtype),
        in_specs=[pl.BlockSpec(memory_space=pl.ANY)],
        out_specs=pl.BlockSpec(memory_space=pl.ANY),
        scratch_shapes=[
            pltpu.SemaphoreType.DMA(()),
            pltpu.SemaphoreType.DMA((count,)),
            pltpu.SemaphoreType.DMA((count,)),
        ],
        compiler_params=pltpu.CompilerParams(collective_id=collective, has_side_effects=True),
    )(blocks)


def project_step(turned, x_ref, cos_ref, sin_ref, *refs):
    weights, out_ref = refs[:-1], refs[-1]
    widened = x_ref[...].astype(jnp.float32)
    centred = widened - jnp.mean(widened, axis=-1, keepdims=True)
    variance = jnp.mean(centred * centred, axis=-1, keepdims=True)
    normed = (centred * lax.rsqrt(variance + norm_eps)).astype(jnp.bfloat16)
    cosine = cos_ref[...]
    sine = sin_ref[...]
    for index, weight in enumerate(weights):
        width = weight.shape[1]
        product = jnp.dot(normed, weight[...], preferred_element_type=jnp.float32)
        if turned[index]:
            pieces = []
            for head in range(width // HEAD_DIM):
                part = product[:, head * HEAD_DIM : (head + 1) * HEAD_DIM]
                pieces.append(part * cosine + pltpu.roll(part, HEAD_DIM // 2, 1) * sine)
            product = jnp.concatenate(pieces, axis=1)
        out_ref[:, index * width : (index + 1) * width] = product.astype(out_ref.dtype)


def rope_tables(positions):
    half_dim = HEAD_DIM // 2
    frequency = jnp.exp(-jnp.log(rope_base) * jnp.arange(half_dim, dtype=jnp.float32) / half_dim)
    doubled = jnp.concatenate([frequency, frequency])
    sign = jnp.concatenate([-jnp.ones((half_dim,), jnp.float32), jnp.ones((half_dim,), jnp.float32)])
    angles = positions.astype(jnp.float32)[:, None] * doubled[None, :]
    return jnp.cos(angles), jnp.sin(angles) * sign[None, :]


def project(rows, positions, weights, turned, block_rows):
    count, width = rows.shape
    cosine, sine = rope_tables(positions)
    out_width = sum(w.shape[1] for w in weights)
    return pl.pallas_call(
        functools.partial(project_step, tuple(turned)),
        grid=(count // block_rows,),
        in_specs=[
            pl.BlockSpec((block_rows, width), lambda i: (i, 0)),
            pl.BlockSpec((block_rows, HEAD_DIM), lambda i: (i, 0)),
            pl.BlockSpec((block_rows, HEAD_DIM), lambda i: (i, 0)),
        ]
        + [pl.BlockSpec(w.shape, lambda i: (0, 0)) for w in weights],
        out_specs=pl.BlockSpec((block_rows, out_width), lambda i: (i, 0)),
        out_shape=jax.ShapeDtypeStruct((count, out_width), jnp.bfloat16),
    )(rows, cosine, sine, *weights)


rope_base = 10000.0
norm_eps = 1e-05


def swapped(value, axis, apart):
    mask = 2**apart
    pairs = [(source, source ^ mask) for source in range(lax.axis_size(axis))]
    return lax.ppermute(value, axis, pairs)


def shards(
    tokens,
    w_query,
    w_key,
    w_value,
    w_out,
    own_cache,
    guest_cache,
    rec_hidden,
    deal_order,
    own_len,
    guest_len,
    rec_index,
):
    groups = lax.axis_size("grp")
    group_id = lax.axis_index("grp")
    partner_id = (group_id + groups // 2) % groups
    swap_bit = groups.bit_length() - 2
    local_width = w_query.shape[1]
    local_heads = local_width // HEAD_DIM
    requests, local_rows, model_width = tokens.shape

    fetched = swapped(guest_cache[0], "grp", swap_bit)

    server = jnp.zeros_like(deal_order).at[deal_order].set(jnp.arange(groups, dtype=jnp.int32))
    start_of = jnp.zeros_like(deal_order).at[deal_order].set(
        own_len + jnp.roll(guest_len, -(groups // 2))
    )
    local_positions = (
        start_of[:, None] + group_id * local_rows + jnp.arange(local_rows, dtype=jnp.int32)[None, :]
    ).reshape(-1)

    projected = project(
        tokens.reshape(-1, model_width), local_positions, [w_query, w_key, w_value],
        [True, True, False], 256,
    ).reshape(requests, local_rows, -1)
    arranged = jnp.take(projected, deal_order, axis=0)
    dealt = lax.all_to_all(arranged, "grp", split_axis=0, concat_axis=1, tiled=True)[0]
    span_len = dealt.shape[0]

    own_count = own_len[group_id]
    guest_count = guest_len[partner_id]
    rec_positions = rec_index[0]
    recomputed = project(rec_hidden[0], rec_positions, [w_key, w_value], [True, False], 256)
    replaced = jnp.zeros((own_cache.shape[2],), jnp.bool_).at[rec_positions].set(True)

    heads = local_heads
    chunks = 2
    piece = local_rows // chunks
    chunk_len = span_len // chunks
    order = dealt.reshape(groups, chunks, piece, -1).transpose(1, 0, 2, 3).reshape(span_len, -1)
    row_of = (
        jnp.arange(span_len, dtype=jnp.int32).reshape(groups, chunks, piece).transpose(1, 0, 2).reshape(-1)
    )
    rec_count = recomputed.shape[0]
    fresh = jnp.concatenate(
        [order[:, local_width:], recomputed], axis=0
    )
    fresh_rank = jnp.concatenate([row_of, jnp.full((rec_count,), -1, jnp.int32)])[None, :]
    fresh_count = span_len + rec_count
    never = jnp.int32(1 << 30)
    cap = own_cache.shape[2]
    block_len = 2048
    key_rows = jnp.arange(cap, dtype=jnp.int32)
    own_rank = jnp.where((key_rows < own_count) & ~replaced, -1, never)[None, :]
    own_flags = (jnp.arange(cap // block_len, dtype=jnp.int32) * block_len < own_count).astype(jnp.int32)
    gcap = fetched.shape[1]
    guest_rows = jnp.arange(gcap, dtype=jnp.int32)
    guest_rank = jnp.where(guest_rows < guest_count, -1, never)[None, :]
    guest_flags = (jnp.arange(gcap // block_len, dtype=jnp.int32) * block_len < guest_count).astype(jnp.int32)
    blocks = lax.axis_size("tp")
    out_by_block = w_out.reshape(local_width, blocks, -1)

    returned = []
    exchanged = []
    def fresh_call(chunk, state):
        return attend(
            state, jnp.ones((1,), jnp.int32), row_of[chunk * chunk_len : (chunk + 1) * chunk_len][:, None],
            fresh_rank, order, chunk,
            fresh, lambda h, kb: (kb, h), fresh, lambda h, kb: (kb, heads + h),
            fresh_count, heads, fresh_count,
        )

    def own_call(chunk, state):
        return attend(
            state, own_flags, row_of[chunk * chunk_len : (chunk + 1) * chunk_len][:, None],
            own_rank, order, chunk,
            own_cache[0], lambda h, kb: (0, kb, h), own_cache[0], lambda h, kb: (1, kb, h),
            cap, heads, block_len,
        )

    def guest_call(chunk, state):
        return attend(
            state, guest_flags, row_of[chunk * chunk_len : (chunk + 1) * chunk_len][:, None],
            guest_rank, order, chunk,
            fetched, lambda h, kb: (0, kb, h), fetched, lambda h, kb: (1, kb, h),
            gcap, heads, block_len,
        )

    def exchanged_partial(state):
        attended = (state[2] / state[1]).astype(jnp.bfloat16)
        partial_value = jnp.einsum(
            "qc,ctd->tqd", attended, out_by_block, preferred_element_type=jnp.float32
        ).astype(jnp.bfloat16)
        return lax.all_to_all(partial_value, "tp", split_axis=0, concat_axis=0, tiled=True)

    empty = (
        jnp.full((chunk_len, local_width), FLOOR, jnp.float32),
        jnp.zeros((chunk_len, local_width), jnp.float32),
        jnp.zeros((chunk_len, local_width), jnp.float32),
    )
    first = own_call(0, fresh_call(0, empty))
    second = fresh_call(1, empty)
    first, second = lax.optimization_barrier((first, second))
    first = guest_call(0, first)
    first, second = lax.optimization_barrier((first, second))
    exchanged.append(exchanged_partial(first))
    exchanged.append(exchanged_partial(guest_call(1, own_call(1, second))))
    for chunk in range(chunks):
        mixed_rows = exchanged[chunk].astype(jnp.float32).sum(axis=0).astype(jnp.bfloat16)
        returned.append(exchange(mixed_rows.reshape(groups, piece, -1), "grp", 1 + chunk))
    returned_rows = jnp.stack(returned, axis=1).reshape(groups, local_rows, -1)
    return jnp.take(returned_rows, server, axis=0)


def solution(mesh):
    return jax.shard_map(
        shards,
        mesh=mesh,
        in_specs=(
            P(None, "grp", None),
            P(None, "tp"),
            P(None, "tp"),
            P(None, "tp"),
            P("tp", None),
            P("grp", None, None, "tp"),
            P("grp", None, None, "tp"),
            P("grp", None, None),
            P(),
            P(),
            P(),
            P("grp", None),
        ),
        out_specs=P(None, "grp", "tp"),
        check_vma=False,
    )
```

```python
import functools

import jax
import jax.numpy as jnp
from jax import lax
from jax.experimental import pallas as pl
from jax.experimental.pallas import tpu as pltpu
from jax.sharding import PartitionSpec as P

HEAD_DIM = 128


FLOOR = -1e30


def flash_step(flags_ref, qrow_ref, rank_ref, q_ref, k_ref, v_ref, m_in, l_in, acc_in, m_out, l_out, acc_out):
    kb = pl.program_id(1)

    @pl.when(kb == 0)
    def _():
        m_out[...] = m_in[...]
        l_out[...] = l_in[...]
        acc_out[...] = acc_in[...]

    @pl.when(flags_ref[kb] > 0)
    def _():
        scores = lax.dot_general(
            q_ref[...], k_ref[...], (((1,), (1,)), ((), ())), preferred_element_type=jnp.float32
        ) * (HEAD_DIM ** -0.5)
        scores = jnp.where(rank_ref[...] <= qrow_ref[...], scores, FLOOR)
        m_prev = m_out[...]
        m_new = jnp.maximum(m_prev, jnp.max(scores, axis=1, keepdims=True))
        factor = jnp.exp(m_prev - m_new)
        expanded = jnp.exp(scores - m_new[:, :1])
        l_out[...] = factor * l_out[...] + jnp.sum(expanded, axis=1, keepdims=True)
        acc_out[...] = factor * acc_out[...] + jnp.dot(
            expanded.astype(jnp.bfloat16), v_ref[...], preferred_element_type=jnp.float32
        )
        m_out[...] = m_new


def attend(state, flags, qrow, rank, q_src, q_block, k_src, k_map, v_src, v_map, key_count, heads, block_len):
    query_count = qrow.shape[0]
    state_spec = pl.BlockSpec((query_count, HEAD_DIM), lambda h, kb, f: (0, h))
    k_block = (block_len, HEAD_DIM) if k_src.ndim == 2 else (None, block_len, HEAD_DIM)
    v_block = (block_len, HEAD_DIM) if v_src.ndim == 2 else (None, block_len, HEAD_DIM)
    grid_spec = pltpu.PrefetchScalarGridSpec(
        num_scalar_prefetch=1,
        grid=(heads, key_count // block_len),
        in_specs=[
            pl.BlockSpec((query_count, 1), lambda h, kb, f: (0, 0)),
            pl.BlockSpec((1, block_len), lambda h, kb, f: (0, kb)),
            pl.BlockSpec((query_count, HEAD_DIM), lambda h, kb, f: (q_block, h)),
            pl.BlockSpec(k_block, lambda h, kb, f: k_map(h, kb)),
            pl.BlockSpec(v_block, lambda h, kb, f: v_map(h, kb)),
            state_spec,
            state_spec,
            state_spec,
        ],
        out_specs=[state_spec, state_spec, state_spec],
    )
    shape = jax.ShapeDtypeStruct(state[0].shape, jnp.float32)
    return pl.pallas_call(
        flash_step,
        grid_spec=grid_spec,
        out_shape=[shape, shape, shape],
        input_output_aliases={6: 0, 7: 1, 8: 2},
        compiler_params=pltpu.CompilerParams(dimension_semantics=("arbitrary", "arbitrary")),
    )(flags, qrow, rank, q_src, k_src, v_src, *state)


def exchange_step(axis, count, x_ref, y_ref, local_sem, send_sem, recv_sem):
    me = lax.axis_index(axis)
    barrier = pltpu.get_barrier_semaphore()
    for step in range(1, count):
        pl.semaphore_signal(
            barrier, inc=1, device_id={axis: lax.rem(me + step, count)},
            device_id_type=pl.DeviceIdType.MESH,
        )
    pl.semaphore_wait(barrier, count - 1)
    own = pltpu.make_async_copy(x_ref.at[me], y_ref.at[me], local_sem)
    own.start()
    sends = []
    for step in range(1, count):
        target = lax.rem(me + step, count)
        copy = pltpu.make_async_remote_copy(
            src_ref=x_ref.at[target],
            dst_ref=y_ref.at[me],
            send_sem=send_sem.at[step],
            recv_sem=recv_sem.at[me],
            device_id={axis: target},
            device_id_type=pl.DeviceIdType.MESH,
        )
        copy.start()
        sends.append(copy)
    for copy in sends:
        copy.wait_send()
    for step in range(1, count):
        source = lax.rem(me + count - step, count)
        pltpu.make_async_remote_copy(
            src_ref=x_ref.at[source],
            dst_ref=y_ref.at[source],
            send_sem=send_sem.at[step],
            recv_sem=recv_sem.at[source],
            device_id={axis: source},
            device_id_type=pl.DeviceIdType.MESH,
        ).wait_recv()
    own.wait()


def exchange(blocks, axis, collective):
    count = blocks.shape[0]
    return pl.pallas_call(
        functools.partial(exchange_step, axis, count),
        out_shape=jax.ShapeDtypeStruct(blocks.shape, blocks.dtype),
        in_specs=[pl.BlockSpec(memory_space=pl.ANY)],
        out_specs=pl.BlockSpec(memory_space=pl.ANY),
        scratch_shapes=[
            pltpu.SemaphoreType.DMA(()),
            pltpu.SemaphoreType.DMA((count,)),
            pltpu.SemaphoreType.DMA((count,)),
        ],
        compiler_params=pltpu.CompilerParams(collective_id=collective, has_side_effects=True),
    )(blocks)


def project_step(turned, x_ref, cos_ref, sin_ref, *refs):
    weights, out_ref = refs[:-1], refs[-1]
    widened = x_ref[...].astype(jnp.float32)
    centred = widened - jnp.mean(widened, axis=-1, keepdims=True)
    variance = jnp.mean(centred * centred, axis=-1, keepdims=True)
    normed = (centred * lax.rsqrt(variance + norm_eps)).astype(jnp.bfloat16)
    cosine = cos_ref[...]
    sine = sin_ref[...]
    for index, weight in enumerate(weights):
        width = weight.shape[1]
        product = jnp.dot(normed, weight[...], preferred_element_type=jnp.float32)
        if turned[index]:
            pieces = []
            for head in range(width // HEAD_DIM):
                part = product[:, head * HEAD_DIM : (head + 1) * HEAD_DIM]
                pieces.append(part * cosine + pltpu.roll(part, HEAD_DIM // 2, 1) * sine)
            product = jnp.concatenate(pieces, axis=1)
        out_ref[:, index * width : (index + 1) * width] = product.astype(out_ref.dtype)


def rope_tables(positions):
    half_dim = HEAD_DIM // 2
    frequency = jnp.exp(-jnp.log(rope_base) * jnp.arange(half_dim, dtype=jnp.float32) / half_dim)
    doubled = jnp.concatenate([frequency, frequency])
    sign = jnp.concatenate([-jnp.ones((half_dim,), jnp.float32), jnp.ones((half_dim,), jnp.float32)])
    angles = positions.astype(jnp.float32)[:, None] * doubled[None, :]
    return jnp.cos(angles), jnp.sin(angles) * sign[None, :]


def project(rows, positions, weights, turned, block_rows):
    count, width = rows.shape
    cosine, sine = rope_tables(positions)
    out_width = sum(w.shape[1] for w in weights)
    return pl.pallas_call(
        functools.partial(project_step, tuple(turned)),
        grid=(count // block_rows,),
        in_specs=[
            pl.BlockSpec((block_rows, width), lambda i: (i, 0)),
            pl.BlockSpec((block_rows, HEAD_DIM), lambda i: (i, 0)),
            pl.BlockSpec((block_rows, HEAD_DIM), lambda i: (i, 0)),
        ]
        + [pl.BlockSpec(w.shape, lambda i: (0, 0)) for w in weights],
        out_specs=pl.BlockSpec((block_rows, out_width), lambda i: (i, 0)),
        out_shape=jax.ShapeDtypeStruct((count, out_width), jnp.bfloat16),
    )(rows, cosine, sine, *weights)


rope_base = 10000.0
norm_eps = 1e-05


def swapped(value, axis, apart):
    mask = 2**apart
    pairs = [(source, source ^ mask) for source in range(lax.axis_size(axis))]
    return lax.ppermute(value, axis, pairs)


def shards(
    tokens,
    w_query,
    w_key,
    w_value,
    w_out,
    own_cache,
    guest_cache,
    rec_hidden,
    deal_order,
    own_len,
    guest_len,
    rec_index,
):
    groups = lax.axis_size("grp")
    group_id = lax.axis_index("grp")
    partner_id = (group_id + groups // 2) % groups
    swap_bit = groups.bit_length() - 2
    local_width = w_query.shape[1]
    local_heads = local_width // HEAD_DIM
    requests, local_rows, model_width = tokens.shape

    fetched = swapped(guest_cache[0], "grp", swap_bit)

    server = jnp.zeros_like(deal_order).at[deal_order].set(jnp.arange(groups, dtype=jnp.int32))
    start_of = jnp.zeros_like(deal_order).at[deal_order].set(
        own_len + jnp.roll(guest_len, -(groups // 2))
    )
    local_positions = (
        start_of[:, None] + group_id * local_rows + jnp.arange(local_rows, dtype=jnp.int32)[None, :]
    ).reshape(-1)

    projected = project(
        tokens.reshape(-1, model_width), local_positions, [w_query, w_key, w_value],
        [True, True, False], 256,
    ).reshape(requests, local_rows, -1)
    arranged = jnp.take(projected, deal_order, axis=0)
    dealt = lax.all_to_all(arranged, "grp", split_axis=0, concat_axis=1, tiled=True)[0]
    span_len = dealt.shape[0]

    own_count = own_len[group_id]
    guest_count = guest_len[partner_id]
    rec_positions = rec_index[0]
    recomputed = project(rec_hidden[0], rec_positions, [w_key, w_value], [True, False], 256)
    replaced = jnp.zeros((own_cache.shape[2],), jnp.bool_).at[rec_positions].set(True)

    heads = local_heads
    chunks = 2
    piece = local_rows // chunks
    chunk_len = span_len // chunks
    def chunk_major(rows):
        return rows.reshape(groups, chunks, piece, -1).transpose(1, 0, 2, 3).reshape(span_len, -1)

    order = chunk_major(dealt[:, :local_width])
    row_of = (
        jnp.arange(span_len, dtype=jnp.int32).reshape(groups, chunks, piece).transpose(1, 0, 2).reshape(-1)
    )
    rec_count = recomputed.shape[0]
    fresh = jnp.concatenate(
        [chunk_major(dealt[:, local_width:]), recomputed], axis=0
    )
    fresh_rank = jnp.concatenate([row_of, jnp.full((rec_count,), -1, jnp.int32)])[None, :]
    fresh_count = span_len + rec_count
    never = jnp.int32(1 << 30)
    cap = own_cache.shape[2]
    block_len = 2048
    key_rows = jnp.arange(cap, dtype=jnp.int32)
    own_rank = jnp.where((key_rows < own_count) & ~replaced, -1, never)[None, :]
    own_flags = (jnp.arange(cap // block_len, dtype=jnp.int32) * block_len < own_count).astype(jnp.int32)
    gcap = fetched.shape[1]
    guest_rows = jnp.arange(gcap, dtype=jnp.int32)
    guest_rank = jnp.where(guest_rows < guest_count, -1, never)[None, :]
    guest_flags = (jnp.arange(gcap // block_len, dtype=jnp.int32) * block_len < guest_count).astype(jnp.int32)
    blocks = lax.axis_size("tp")
    out_by_block = w_out.reshape(local_width, blocks, -1)

    returned = []
    exchanged = []
    for chunk in range(chunks):
        query_rows = row_of[chunk * chunk_len : (chunk + 1) * chunk_len][:, None]
        state = (
            jnp.full((chunk_len, local_width), FLOOR, jnp.float32),
            jnp.zeros((chunk_len, local_width), jnp.float32),
            jnp.zeros((chunk_len, local_width), jnp.float32),
        )
        state = attend(
            state, jnp.ones((1,), jnp.int32), query_rows, fresh_rank, order, chunk,
            fresh, lambda h, kb: (kb, h), fresh, lambda h, kb: (kb, heads + h),
            fresh_count, heads, fresh_count,
        )
        state = attend(
            state, own_flags, query_rows, own_rank, order, chunk,
            own_cache[0], lambda h, kb: (0, kb, h), own_cache[0], lambda h, kb: (1, kb, h),
            cap, heads, block_len,
        )
        state = attend(
            state, guest_flags, query_rows, guest_rank, order, chunk,
            fetched, lambda h, kb: (0, kb, h), fetched, lambda h, kb: (1, kb, h),
            gcap, heads, block_len,
        )
        attended = (state[2] / state[1]).astype(jnp.bfloat16)
        partial_value = jnp.einsum(
            "qc,ctd->tqd", attended, out_by_block, preferred_element_type=jnp.float32
        ).astype(jnp.bfloat16)
        exchanged.append(
            lax.all_to_all(partial_value, "tp", split_axis=0, concat_axis=0, tiled=True)
        )
    for chunk in range(chunks):
        mixed_rows = exchanged[chunk].astype(jnp.float32).sum(axis=0).astype(jnp.bfloat16)
        returned.append(exchange(mixed_rows.reshape(groups, piece, -1), "grp", 1 + chunk))
    returned_rows = jnp.stack(returned, axis=1).reshape(groups, local_rows, -1)
    return jnp.take(returned_rows, server, axis=0)


def solution(mesh):
    return jax.shard_map(
        shards,
        mesh=mesh,
        in_specs=(
            P(None, "grp", None),
            P(None, "tp"),
            P(None, "tp"),
            P(None, "tp"),
            P("tp", None),
            P("grp", None, None, "tp"),
            P("grp", None, None, "tp"),
            P("grp", None, None),
            P(),
            P(),
            P(),
            P("grp", None),
        ),
        out_specs=P(None, "grp", "tp"),
        check_vma=False,
    )
```

```python
import functools

import jax
import jax.numpy as jnp
from jax import lax
from jax.experimental import pallas as pl
from jax.experimental.pallas import tpu as pltpu
from jax.sharding import PartitionSpec as P

HEAD_DIM = 128


FLOOR = -1e30


def flash_step(flags_ref, qrow_ref, rank_ref, q_ref, k_ref, v_ref, m_in, l_in, acc_in, m_out, l_out, acc_out):
    kb = pl.program_id(1)

    @pl.when(kb == 0)
    def _():
        m_out[...] = m_in[...]
        l_out[...] = l_in[...]
        acc_out[...] = acc_in[...]

    @pl.when(flags_ref[kb] > 0)
    def _():
        scores = lax.dot_general(
            q_ref[...], k_ref[...], (((1,), (1,)), ((), ())), preferred_element_type=jnp.float32
        ) * (HEAD_DIM ** -0.5)
        scores = jnp.where(rank_ref[...] <= qrow_ref[...], scores, FLOOR)
        m_prev = m_out[...]
        m_new = jnp.maximum(m_prev, jnp.max(scores, axis=1, keepdims=True))
        factor = jnp.exp(m_prev - m_new)
        expanded = jnp.exp(scores - m_new[:, :1])
        l_out[...] = factor * l_out[...] + jnp.sum(expanded, axis=1, keepdims=True)
        acc_out[...] = factor * acc_out[...] + jnp.dot(
            expanded.astype(jnp.bfloat16), v_ref[...], preferred_element_type=jnp.float32
        )
        m_out[...] = m_new


def attend(state, flags, qrow, rank, q_src, q_block, k_src, k_map, v_src, v_map, key_count, heads, block_len):
    query_count = qrow.shape[0]
    state_spec = pl.BlockSpec((query_count, HEAD_DIM), lambda h, kb, f: (0, h))
    k_block = (block_len, HEAD_DIM) if k_src.ndim == 2 else (None, block_len, HEAD_DIM)
    v_block = (block_len, HEAD_DIM) if v_src.ndim == 2 else (None, block_len, HEAD_DIM)
    grid_spec = pltpu.PrefetchScalarGridSpec(
        num_scalar_prefetch=1,
        grid=(heads, key_count // block_len),
        in_specs=[
            pl.BlockSpec((query_count, 1), lambda h, kb, f: (0, 0)),
            pl.BlockSpec((1, block_len), lambda h, kb, f: (0, kb)),
            pl.BlockSpec((query_count, HEAD_DIM), lambda h, kb, f: (q_block, h)),
            pl.BlockSpec(k_block, lambda h, kb, f: k_map(h, kb)),
            pl.BlockSpec(v_block, lambda h, kb, f: v_map(h, kb)),
            state_spec,
            state_spec,
            state_spec,
        ],
        out_specs=[state_spec, state_spec, state_spec],
    )
    shape = jax.ShapeDtypeStruct(state[0].shape, jnp.float32)
    return pl.pallas_call(
        flash_step,
        grid_spec=grid_spec,
        out_shape=[shape, shape, shape],
        input_output_aliases={6: 0, 7: 1, 8: 2},
        compiler_params=pltpu.CompilerParams(dimension_semantics=("arbitrary", "arbitrary")),
    )(flags, qrow, rank, q_src, k_src, v_src, *state)


def exchange_step(axis, count, x_ref, y_ref, local_sem, send_sem, recv_sem):
    me = lax.axis_index(axis)
    barrier = pltpu.get_barrier_semaphore()
    for step in range(1, count):
        pl.semaphore_signal(
            barrier, inc=1, device_id={axis: lax.rem(me + step, count)},
            device_id_type=pl.DeviceIdType.MESH,
        )
    pl.semaphore_wait(barrier, count - 1)
    own = pltpu.make_async_copy(x_ref.at[me], y_ref.at[me], local_sem)
    own.start()
    sends = []
    for step in range(1, count):
        target = lax.rem(me + step, count)
        copy = pltpu.make_async_remote_copy(
            src_ref=x_ref.at[target],
            dst_ref=y_ref.at[me],
            send_sem=send_sem.at[step],
            recv_sem=recv_sem.at[me],
            device_id={axis: target},
            device_id_type=pl.DeviceIdType.MESH,
        )
        copy.start()
        sends.append(copy)
    for copy in sends:
        copy.wait_send()
    for step in range(1, count):
        source = lax.rem(me + count - step, count)
        pltpu.make_async_remote_copy(
            src_ref=x_ref.at[source],
            dst_ref=y_ref.at[source],
            send_sem=send_sem.at[step],
            recv_sem=recv_sem.at[source],
            device_id={axis: source},
            device_id_type=pl.DeviceIdType.MESH,
        ).wait_recv()
    own.wait()


def exchange(blocks, axis, collective):
    count = blocks.shape[0]
    return pl.pallas_call(
        functools.partial(exchange_step, axis, count),
        out_shape=jax.ShapeDtypeStruct(blocks.shape, blocks.dtype),
        in_specs=[pl.BlockSpec(memory_space=pl.ANY)],
        out_specs=pl.BlockSpec(memory_space=pl.ANY),
        scratch_shapes=[
            pltpu.SemaphoreType.DMA(()),
            pltpu.SemaphoreType.DMA((count,)),
            pltpu.SemaphoreType.DMA((count,)),
        ],
        compiler_params=pltpu.CompilerParams(collective_id=collective, has_side_effects=True),
    )(blocks)


def project_step(turned, placed, *refs):
    if placed:
        slot_ref, refs = refs[0], refs[1:]
    x_ref, cos_ref, sin_ref = refs[:3]
    weights, out_ref = refs[3:-1], refs[-1]
    widened = x_ref[...].astype(jnp.float32)
    centred = widened - jnp.mean(widened, axis=-1, keepdims=True)
    variance = jnp.mean(centred * centred, axis=-1, keepdims=True)
    normed = (centred * lax.rsqrt(variance + norm_eps)).astype(jnp.bfloat16)
    cosine = cos_ref[...]
    sine = sin_ref[...]
    for index, weight in enumerate(weights):
        width = weight.shape[1]
        product = jnp.dot(normed, weight[...], preferred_element_type=jnp.float32)
        if turned[index]:
            pieces = []
            for head in range(width // HEAD_DIM):
                part = product[:, head * HEAD_DIM : (head + 1) * HEAD_DIM]
                pieces.append(part * cosine + pltpu.roll(part, HEAD_DIM // 2, 1) * sine)
            product = jnp.concatenate(pieces, axis=1)
        product = product.astype(out_ref.dtype)
        columns = slice(index * width, (index + 1) * width)
        if placed:
            rows = out_ref.shape[1]
            first = pl.program_id(0) * (product.shape[0] // rows)
            for j in range(product.shape[0] // rows):
                out_ref[slot_ref[first + j], :, columns] = product[j * rows : (j + 1) * rows]
        else:
            out_ref[:, columns] = product


def rope_tables(positions):
    half_dim = HEAD_DIM // 2
    frequency = jnp.exp(-jnp.log(rope_base) * jnp.arange(half_dim, dtype=jnp.float32) / half_dim)
    doubled = jnp.concatenate([frequency, frequency])
    sign = jnp.concatenate([-jnp.ones((half_dim,), jnp.float32), jnp.ones((half_dim,), jnp.float32)])
    angles = positions.astype(jnp.float32)[:, None] * doubled[None, :]
    return jnp.cos(angles), jnp.sin(angles) * sign[None, :]


def project(rows, positions, weights, turned, block_rows, slots=None, rows_per_slot=None):
    count, width = rows.shape
    cosine, sine = rope_tables(positions)
    out_width = sum(w.shape[1] for w in weights)
    placed = slots is not None
    extra = (lambda i, s: (i, 0)) if placed else (lambda i: (i, 0))
    fixed = (lambda i, s: (0, 0)) if placed else (lambda i: (0, 0))
    in_specs = [
        pl.BlockSpec((block_rows, width), extra),
        pl.BlockSpec((block_rows, HEAD_DIM), extra),
        pl.BlockSpec((block_rows, HEAD_DIM), extra),
    ] + [pl.BlockSpec(w.shape, fixed) for w in weights]
    if placed:
        out_shape = (count // rows_per_slot, rows_per_slot, out_width)
        grid_spec = pltpu.PrefetchScalarGridSpec(
            num_scalar_prefetch=1,
            grid=(count // block_rows,),
            in_specs=in_specs,
            out_specs=pl.BlockSpec(out_shape, lambda i, s: (0, 0, 0)),
        )
        operands = (slots, rows, cosine, sine, *weights)
    else:
        out_shape = (count, out_width)
        grid_spec = pl.GridSpec(
            grid=(count // block_rows,),
            in_specs=in_specs,
            out_specs=pl.BlockSpec((block_rows, out_width), extra),
        )
        operands = (rows, cosine, sine, *weights)
    return pl.pallas_call(
        functools.partial(project_step, tuple(turned), placed),
        grid_spec=grid_spec,
        out_shape=jax.ShapeDtypeStruct(out_shape, jnp.bfloat16),
    )(*operands)

rope_base = 10000.0
norm_eps = 1e-05


def swapped(value, axis, apart):
    mask = 2**apart
    pairs = [(source, source ^ mask) for source in range(lax.axis_size(axis))]
    return lax.ppermute(value, axis, pairs)


def shards(
    tokens,
    w_query,
    w_key,
    w_value,
    w_out,
    own_cache,
    guest_cache,
    rec_hidden,
    deal_order,
    own_len,
    guest_len,
    rec_index,
):
    groups = lax.axis_size("grp")
    group_id = lax.axis_index("grp")
    partner_id = (group_id + groups // 2) % groups
    swap_bit = groups.bit_length() - 2
    local_width = w_query.shape[1]
    local_heads = local_width // HEAD_DIM
    requests, local_rows, model_width = tokens.shape

    fetched = swapped(guest_cache[0], "grp", swap_bit)

    server = jnp.zeros_like(deal_order).at[deal_order].set(jnp.arange(groups, dtype=jnp.int32))
    start_of = jnp.zeros_like(deal_order).at[deal_order].set(
        own_len + jnp.roll(guest_len, -(groups // 2))
    )
    local_positions = (
        start_of[:, None] + group_id * local_rows + jnp.arange(local_rows, dtype=jnp.int32)[None, :]
    ).reshape(-1)

    arranged = project(
        tokens.reshape(-1, model_width), local_positions, [w_query, w_key, w_value],
        [True, True, False], 256, server, local_rows,
    )
    dealt = lax.all_to_all(arranged, "grp", split_axis=0, concat_axis=1, tiled=True)[0]
    span_len = dealt.shape[0]

    own_count = own_len[group_id]
    guest_count = guest_len[partner_id]
    rec_positions = rec_index[0]
    recomputed = project(rec_hidden[0], rec_positions, [w_key, w_value], [True, False], 256)
    replaced = jnp.zeros((own_cache.shape[2],), jnp.bool_).at[rec_positions].set(True)

    heads = local_heads
    chunks = 2
    piece = local_rows // chunks
    chunk_len = span_len // chunks
    def chunk_major(rows):
        return rows.reshape(groups, chunks, piece, -1).transpose(1, 0, 2, 3).reshape(span_len, -1)

    order = chunk_major(dealt[:, :local_width])
    row_of = (
        jnp.arange(span_len, dtype=jnp.int32).reshape(groups, chunks, piece).transpose(1, 0, 2).reshape(-1)
    )
    rec_count = recomputed.shape[0]
    fresh = jnp.concatenate(
        [chunk_major(dealt[:, local_width:]), recomputed], axis=0
    )
    fresh_rank = jnp.concatenate([row_of, jnp.full((rec_count,), -1, jnp.int32)])[None, :]
    fresh_count = span_len + rec_count
    never = jnp.int32(1 << 30)
    cap = own_cache.shape[2]
    block_len = 2048
    key_rows = jnp.arange(cap, dtype=jnp.int32)
    own_rank = jnp.where((key_rows < own_count) & ~replaced, -1, never)[None, :]
    own_flags = (jnp.arange(cap // block_len, dtype=jnp.int32) * block_len < own_count).astype(jnp.int32)
    gcap = fetched.shape[1]
    guest_rows = jnp.arange(gcap, dtype=jnp.int32)
    guest_rank = jnp.where(guest_rows < guest_count, -1, never)[None, :]
    guest_flags = (jnp.arange(gcap // block_len, dtype=jnp.int32) * block_len < guest_count).astype(jnp.int32)
    blocks = lax.axis_size("tp")
    out_by_block = w_out.reshape(local_width, blocks, -1)

    returned = []
    exchanged = []
    for chunk in range(chunks):
        query_rows = row_of[chunk * chunk_len : (chunk + 1) * chunk_len][:, None]
        state = (
            jnp.full((chunk_len, local_width), FLOOR, jnp.float32),
            jnp.zeros((chunk_len, local_width), jnp.float32),
            jnp.zeros((chunk_len, local_width), jnp.float32),
        )
        state = attend(
            state, jnp.ones((1,), jnp.int32), query_rows, fresh_rank, order, chunk,
            fresh, lambda h, kb: (kb, h), fresh, lambda h, kb: (kb, heads + h),
            fresh_count, heads, fresh_count,
        )
        state = attend(
            state, own_flags, query_rows, own_rank, order, chunk,
            own_cache[0], lambda h, kb: (0, kb, h), own_cache[0], lambda h, kb: (1, kb, h),
            cap, heads, block_len,
        )
        state = attend(
            state, guest_flags, query_rows, guest_rank, order, chunk,
            fetched, lambda h, kb: (0, kb, h), fetched, lambda h, kb: (1, kb, h),
            gcap, heads, block_len,
        )
        attended = (state[2] / state[1]).astype(jnp.bfloat16)
        partial_value = jnp.einsum(
            "qc,ctd->tqd", attended, out_by_block, preferred_element_type=jnp.float32
        ).astype(jnp.bfloat16)
        exchanged.append(
            lax.all_to_all(partial_value, "tp", split_axis=0, concat_axis=0, tiled=True)
        )
    for chunk in range(chunks):
        mixed_rows = exchanged[chunk].astype(jnp.float32).sum(axis=0).astype(jnp.bfloat16)
        returned.append(exchange(mixed_rows.reshape(groups, piece, -1), "grp", 1 + chunk))
    returned_rows = jnp.stack(returned, axis=1).reshape(groups, local_rows, -1)
    return jnp.take(returned_rows, server, axis=0)


def solution(mesh):
    return jax.shard_map(
        shards,
        mesh=mesh,
        in_specs=(
            P(None, "grp", None),
            P(None, "tp"),
            P(None, "tp"),
            P(None, "tp"),
            P("tp", None),
            P("grp", None, None, "tp"),
            P("grp", None, None, "tp"),
            P("grp", None, None),
            P(),
            P(),
            P(),
            P("grp", None),
        ),
        out_specs=P(None, "grp", "tp"),
        check_vma=False,
    )
```

```python
import functools

import jax
import jax.numpy as jnp
from jax import lax
from jax.experimental import pallas as pl
from jax.experimental.pallas import tpu as pltpu
from jax.sharding import PartitionSpec as P

HEAD_DIM = 128


FLOOR = -1e30


def flash_step(flags_ref, qrow_ref, rank_ref, q_ref, k_ref, v_ref, m_in, l_in, acc_in, m_out, l_out, acc_out):
    kb = pl.program_id(1)

    @pl.when(kb == 0)
    def _():
        m_out[...] = m_in[...]
        l_out[...] = l_in[...]
        acc_out[...] = acc_in[...]

    @pl.when(flags_ref[kb] > 0)
    def _():
        scores = lax.dot_general(
            q_ref[...], k_ref[...], (((1,), (1,)), ((), ())), preferred_element_type=jnp.float32
        ) * (HEAD_DIM ** -0.5)
        scores = jnp.where(rank_ref[...] <= qrow_ref[...], scores, FLOOR)
        m_prev = m_out[...]
        m_new = jnp.maximum(m_prev, jnp.max(scores, axis=1, keepdims=True))
        factor = jnp.exp(m_prev - m_new)
        expanded = jnp.exp(scores - m_new[:, :1])
        l_out[...] = factor * l_out[...] + jnp.sum(expanded, axis=1, keepdims=True)
        acc_out[...] = factor * acc_out[...] + jnp.dot(
            expanded.astype(jnp.bfloat16), v_ref[...], preferred_element_type=jnp.float32
        )
        m_out[...] = m_new


def attend(state, flags, qrow, rank, q_src, q_block, k_src, k_map, v_src, v_map, key_count, heads, block_len):
    query_count = qrow.shape[0]
    state_spec = pl.BlockSpec((query_count, HEAD_DIM), lambda h, kb, f: (0, h))
    k_block = (block_len, HEAD_DIM) if k_src.ndim == 2 else (None, block_len, HEAD_DIM)
    v_block = (block_len, HEAD_DIM) if v_src.ndim == 2 else (None, block_len, HEAD_DIM)
    grid_spec = pltpu.PrefetchScalarGridSpec(
        num_scalar_prefetch=1,
        grid=(heads, key_count // block_len),
        in_specs=[
            pl.BlockSpec((query_count, 1), lambda h, kb, f: (0, 0)),
            pl.BlockSpec((1, block_len), lambda h, kb, f: (0, kb)),
            pl.BlockSpec((query_count, HEAD_DIM), lambda h, kb, f: (q_block, h)),
            pl.BlockSpec(k_block, lambda h, kb, f: k_map(h, kb)),
            pl.BlockSpec(v_block, lambda h, kb, f: v_map(h, kb)),
            state_spec,
            state_spec,
            state_spec,
        ],
        out_specs=[state_spec, state_spec, state_spec],
    )
    shape = jax.ShapeDtypeStruct(state[0].shape, jnp.float32)
    return pl.pallas_call(
        flash_step,
        grid_spec=grid_spec,
        out_shape=[shape, shape, shape],
        input_output_aliases={6: 0, 7: 1, 8: 2},
        compiler_params=pltpu.CompilerParams(dimension_semantics=("arbitrary", "arbitrary")),
    )(flags, qrow, rank, q_src, k_src, v_src, *state)


def exchange_step(axis, count, x_ref, y_ref, local_sem, send_sem, recv_sem):
    me = lax.axis_index(axis)
    barrier = pltpu.get_barrier_semaphore()
    for step in range(1, count):
        pl.semaphore_signal(
            barrier, inc=1, device_id={axis: lax.rem(me + step, count)},
            device_id_type=pl.DeviceIdType.MESH,
        )
    pl.semaphore_wait(barrier, count - 1)
    own = pltpu.make_async_copy(x_ref.at[me], y_ref.at[me], local_sem)
    own.start()
    sends = []
    for step in range(1, count):
        target = lax.rem(me + step, count)
        copy = pltpu.make_async_remote_copy(
            src_ref=x_ref.at[target],
            dst_ref=y_ref.at[me],
            send_sem=send_sem.at[step],
            recv_sem=recv_sem.at[me],
            device_id={axis: target},
            device_id_type=pl.DeviceIdType.MESH,
        )
        copy.start()
        sends.append(copy)
    for copy in sends:
        copy.wait_send()
    for step in range(1, count):
        source = lax.rem(me + count - step, count)
        pltpu.make_async_remote_copy(
            src_ref=x_ref.at[source],
            dst_ref=y_ref.at[source],
            send_sem=send_sem.at[step],
            recv_sem=recv_sem.at[source],
            device_id={axis: source},
            device_id_type=pl.DeviceIdType.MESH,
        ).wait_recv()
    own.wait()


def exchange(blocks, axis, collective):
    count = blocks.shape[0]
    return pl.pallas_call(
        functools.partial(exchange_step, axis, count),
        out_shape=jax.ShapeDtypeStruct(blocks.shape, blocks.dtype),
        in_specs=[pl.BlockSpec(memory_space=pl.ANY)],
        out_specs=pl.BlockSpec(memory_space=pl.ANY),
        scratch_shapes=[
            pltpu.SemaphoreType.DMA(()),
            pltpu.SemaphoreType.DMA((count,)),
            pltpu.SemaphoreType.DMA((count,)),
        ],
        compiler_params=pltpu.CompilerParams(collective_id=collective, has_side_effects=True),
    )(blocks)


def project_step(turned, x_ref, cos_ref, sin_ref, *refs):
    weights, out_ref = refs[:-1], refs[-1]
    widened = x_ref[...].astype(jnp.float32)
    centred = widened - jnp.mean(widened, axis=-1, keepdims=True)
    variance = jnp.mean(centred * centred, axis=-1, keepdims=True)
    normed = (centred * lax.rsqrt(variance + norm_eps)).astype(jnp.bfloat16)
    cosine = cos_ref[...]
    sine = sin_ref[...]
    for index, weight in enumerate(weights):
        width = weight.shape[1]
        product = jnp.dot(normed, weight[...], preferred_element_type=jnp.float32)
        if turned[index]:
            pieces = []
            for head in range(width // HEAD_DIM):
                part = product[:, head * HEAD_DIM : (head + 1) * HEAD_DIM]
                pieces.append(part * cosine + pltpu.roll(part, HEAD_DIM // 2, 1) * sine)
            product = jnp.concatenate(pieces, axis=1)
        out_ref[:, index * width : (index + 1) * width] = product.astype(out_ref.dtype)


def rope_tables(positions):
    half_dim = HEAD_DIM // 2
    frequency = jnp.exp(-jnp.log(rope_base) * jnp.arange(half_dim, dtype=jnp.float32) / half_dim)
    doubled = jnp.concatenate([frequency, frequency])
    sign = jnp.concatenate([-jnp.ones((half_dim,), jnp.float32), jnp.ones((half_dim,), jnp.float32)])
    angles = positions.astype(jnp.float32)[:, None] * doubled[None, :]
    return jnp.cos(angles), jnp.sin(angles) * sign[None, :]


def project(rows, positions, weights, turned, block_rows):
    count, width = rows.shape
    cosine, sine = rope_tables(positions)
    out_width = sum(w.shape[1] for w in weights)
    return pl.pallas_call(
        functools.partial(project_step, tuple(turned)),
        grid=(count // block_rows,),
        in_specs=[
            pl.BlockSpec((block_rows, width), lambda i: (i, 0)),
            pl.BlockSpec((block_rows, HEAD_DIM), lambda i: (i, 0)),
            pl.BlockSpec((block_rows, HEAD_DIM), lambda i: (i, 0)),
        ]
        + [pl.BlockSpec(w.shape, lambda i: (0, 0)) for w in weights],
        out_specs=pl.BlockSpec((block_rows, out_width), lambda i: (i, 0)),
        out_shape=jax.ShapeDtypeStruct((count, out_width), jnp.bfloat16),
    )(rows, cosine, sine, *weights)


rope_base = 10000.0
norm_eps = 1e-05


def swapped(value, axis, apart):
    mask = 2**apart
    pairs = [(source, source ^ mask) for source in range(lax.axis_size(axis))]
    return lax.ppermute(value, axis, pairs)


def shards(
    tokens,
    w_query,
    w_key,
    w_value,
    w_out,
    own_cache,
    guest_cache,
    rec_hidden,
    deal_order,
    own_len,
    guest_len,
    rec_index,
):
    groups = lax.axis_size("grp")
    group_id = lax.axis_index("grp")
    partner_id = (group_id + groups // 2) % groups
    swap_bit = groups.bit_length() - 2
    local_width = w_query.shape[1]
    local_heads = local_width // HEAD_DIM
    requests, local_rows, model_width = tokens.shape

    fetched = swapped(guest_cache[0], "grp", swap_bit)

    server = jnp.zeros_like(deal_order).at[deal_order].set(jnp.arange(groups, dtype=jnp.int32))
    start_of = jnp.zeros_like(deal_order).at[deal_order].set(
        own_len + jnp.roll(guest_len, -(groups // 2))
    )
    local_positions = (
        start_of[:, None] + group_id * local_rows + jnp.arange(local_rows, dtype=jnp.int32)[None, :]
    ).reshape(-1)

    projected = project(
        tokens.reshape(-1, model_width), local_positions, [w_query, w_key, w_value],
        [True, True, False], 512,
    ).reshape(requests, local_rows, -1)
    arranged = jnp.take(projected, deal_order, axis=0)
    dealt = lax.all_to_all(arranged, "grp", split_axis=0, concat_axis=1, tiled=True)[0]
    span_len = dealt.shape[0]

    own_count = own_len[group_id]
    guest_count = guest_len[partner_id]
    rec_positions = rec_index[0]
    recomputed = project(rec_hidden[0], rec_positions, [w_key, w_value], [True, False], 256)
    replaced = jnp.zeros((own_cache.shape[2],), jnp.bool_).at[rec_positions].set(True)

    heads = local_heads
    chunks = 2
    piece = local_rows // chunks
    chunk_len = span_len // chunks
    order = dealt.reshape(groups, chunks, piece, -1).transpose(1, 0, 2, 3).reshape(span_len, -1)
    row_of = (
        jnp.arange(span_len, dtype=jnp.int32).reshape(groups, chunks, piece).transpose(1, 0, 2).reshape(-1)
    )
    rec_count = recomputed.shape[0]
    fresh = jnp.concatenate(
        [order[:, local_width:], recomputed], axis=0
    )
    fresh_rank = jnp.concatenate([row_of, jnp.full((rec_count,), -1, jnp.int32)])[None, :]
    fresh_count = span_len + rec_count
    never = jnp.int32(1 << 30)
    cap = own_cache.shape[2]
    block_len = 2048
    key_rows = jnp.arange(cap, dtype=jnp.int32)
    own_rank = jnp.where((key_rows < own_count) & ~replaced, -1, never)[None, :]
    own_flags = (jnp.arange(cap // block_len, dtype=jnp.int32) * block_len < own_count).astype(jnp.int32)
    gcap = fetched.shape[1]
    guest_rows = jnp.arange(gcap, dtype=jnp.int32)
    guest_rank = jnp.where(guest_rows < guest_count, -1, never)[None, :]
    guest_flags = (jnp.arange(gcap // block_len, dtype=jnp.int32) * block_len < guest_count).astype(jnp.int32)
    blocks = lax.axis_size("tp")
    out_by_block = w_out.reshape(local_width, blocks, -1)

    returned = []
    exchanged = []
    for chunk in range(chunks):
        query_rows = row_of[chunk * chunk_len : (chunk + 1) * chunk_len][:, None]
        state = (
            jnp.full((chunk_len, local_width), FLOOR, jnp.float32),
            jnp.zeros((chunk_len, local_width), jnp.float32),
            jnp.zeros((chunk_len, local_width), jnp.float32),
        )
        state = attend(
            state, jnp.ones((1,), jnp.int32), query_rows, fresh_rank, order, chunk,
            fresh, lambda h, kb: (kb, h), fresh, lambda h, kb: (kb, heads + h),
            fresh_count, heads, fresh_count,
        )
        state = attend(
            state, own_flags, query_rows, own_rank, order, chunk,
            own_cache[0], lambda h, kb: (0, kb, h), own_cache[0], lambda h, kb: (1, kb, h),
            cap, heads, block_len,
        )
        state = attend(
            state, guest_flags, query_rows, guest_rank, order, chunk,
            fetched, lambda h, kb: (0, kb, h), fetched, lambda h, kb: (1, kb, h),
            gcap, heads, block_len,
        )
        attended = (state[2] / state[1]).astype(jnp.bfloat16)
        partial_value = jnp.einsum(
            "qc,ctd->tqd", attended, out_by_block, preferred_element_type=jnp.float32
        ).astype(jnp.bfloat16)
        exchanged.append(
            lax.all_to_all(partial_value, "tp", split_axis=0, concat_axis=0, tiled=True)
        )
    for chunk in range(chunks):
        mixed_rows = exchanged[chunk].astype(jnp.float32).sum(axis=0).astype(jnp.bfloat16)
        returned.append(exchange(mixed_rows.reshape(groups, piece, -1), "grp", 1 + chunk))
    returned_rows = jnp.stack(returned, axis=1).reshape(groups, local_rows, -1)
    return jnp.take(returned_rows, server, axis=0)


def solution(mesh):
    return jax.shard_map(
        shards,
        mesh=mesh,
        in_specs=(
            P(None, "grp", None),
            P(None, "tp"),
            P(None, "tp"),
            P(None, "tp"),
            P("tp", None),
            P("grp", None, None, "tp"),
            P("grp", None, None, "tp"),
            P("grp", None, None),
            P(),
            P(),
            P(),
            P("grp", None),
        ),
        out_specs=P(None, "grp", "tp"),
        check_vma=False,
    )
```
